32 devices in a mesh: seq: 8 (over z, core), fsdp: 4 (over y, x).
Axes of the slice: x: 2, y: 2, z: 4, core: 2. Of those that a mesh axis runs over, the one named last changes fastest.
Arguments:
- tokens: bfloat16 [4096, 2048], P(('seq', 'fsdp')), may hold values from -36 to 36
- gain_attn: bfloat16 [2048], P(('seq', 'fsdp')), may hold values from 0.25 to 1.75
- w_query: bfloat16 [2048, 2048], P(('seq', 'fsdp')), may hold values from -0.125 to 0.125
- w_key: bfloat16 [2048, 256], P(('seq', 'fsdp')), may hold values from -0.125 to 0.125
- w_value: bfloat16 [2048, 256], P(('seq', 'fsdp')), may hold values from -0.125 to 0.125
- w_out: bfloat16 [2048, 2048], P(('seq', 'fsdp')), may hold values from -0.75 to 0.75
- gain_ffn: bfloat16 [2048], P(('seq', 'fsdp')), may hold values from 0.25 to 1.75
- w_gate: bfloat16 [2048, 5632], P(('seq', 'fsdp')), may hold values from -0.125 to 0.125
- w_up: bfloat16 [2048, 5632], P(('seq', 'fsdp')), may hold values from -0.125 to 0.125
- w_down: bfloat16 [2048, 5632], P(('seq', 'fsdp')), may hold values from -0.078125 to 0.078125
- out_grad: bfloat16 [4096, 2048], P(('seq', 'fsdp')), may hold values from -6 to 6
Outputs:
- block_out: bfloat16 [4096, 2048], P(('seq', 'fsdp'))
- grad_tokens: float32 [4096, 2048], P(('seq', 'fsdp'))
- grad_gain_attn: float32 [2048], P(('seq', 'fsdp'))
- grad_query: float32 [2048, 2048], P(('seq', 'fsdp'))
- grad_key: float32 [2048, 256], P(('seq', 'fsdp'))
- grad_value: float32 [2048, 256], P(('seq', 'fsdp'))
- grad_out_proj: float32 [2048, 2048], P(('seq', 'fsdp'))
- grad_gain_ffn: float32 [2048], P(('seq', 'fsdp'))
- grad_gate: float32 [2048, 5632], P(('seq', 'fsdp'))
- grad_up: float32 [2048, 5632], P(('seq', 'fsdp'))
- grad_down: float32 [2048, 5632], P(('seq', 'fsdp'))
The draws below stay inside these ranges and needn't reach their ends.
All inputs are finite; a program needn't handle non-finite values.
Results may differ from the reference program's by a relative error of at most 0.02.
Values may be sent and summed in bfloat16 or wider, within the bound.
No kernel may reach another device: no remote copies, remote signals or barrier semaphores. Data moves between devices by JAX's collectives and lax.ppermute only.
A program may use at most 576 MiB of HBM per device.

```python
import math
import jax
import jax.numpy as jnp
from jax import lax

D = 2048
H = 32
KV = 4
HD = 64
FF = 5632
TOKENS = 4096
N_SEQ = 8


def draw_tokens(key, part):
    key_base, key_rows, key_cols = jax.random.split(key, 3)
    row_scale = jnp.exp(jax.random.uniform(key_rows, (TOKENS, 1), jnp.float32, math.log(0.3), math.log(3.0)))
    col_scale = jnp.exp(jax.random.uniform(key_cols, (1, D), jnp.float32, math.log(0.3), math.log(3.0)))
    base = jnp.clip(jax.random.normal(key_base, (TOKENS, D), jnp.float32), -4.0, 4.0)
    return (base * row_scale * col_scale).astype(jnp.bfloat16)


def with_spikes(drawn, own_key, source, target, parts, factor):
    owner, partner = [(jnp.arange(drawn.shape[dim]) // (drawn.shape[dim] // parts)).reshape([-1 if axis == dim else 1 for axis in range(drawn.ndim)]) for dim in (source, target)]
    chosen = jax.random.permutation(own_key, parts)[partner]
    strong = (owner == chosen) | (owner == (partner + parts // 2) % parts)
    return jnp.where(strong, factor * drawn, drawn)


def block_scale(stream_key, dims, cuts, low, largest):
    loudness = 1.0
    for position, shards_of in cuts:
        draws = jax.random.uniform(jax.random.fold_in(jax.random.fold_in(stream_key, 6), position), (shards_of,), jnp.float32, low / len(cuts), largest / len(cuts))
        loudness = loudness * jnp.repeat(jnp.exp(draws), dims[position] // shards_of).reshape((-1,) + (1,) * (len(dims) - 1 - position))
    return loudness


def bell_draw(key, shape, scale, reach, cuts=(), held_as=jnp.bfloat16):
    array = scale * jax.random.normal(key, shape, jnp.float32)
    if cuts:
        array = array * block_scale(key, shape, cuts, -0.22, 0.18)
    return jnp.clip(array, -reach, reach).astype(held_as)


def bell_draw_with(rng, dims, spread, most, cuts, heavy, held_as=jnp.bfloat16):
    values = spread * jax.random.normal(rng, dims, jnp.float32)
    if cuts:
        values = values * block_scale(rng, dims, cuts, -0.22, 0.18)
    return jnp.clip(with_spikes(values, jax.random.fold_in(rng, 3), *heavy), -most, most).astype(held_as)


def setup_inputs(seed: int = 0) -> dict:
    seeds = jax.random.split(jax.random.key(seed), 12)
    tokens = draw_tokens(jax.random.fold_in(seeds[11], 71), 0)
    gain_attn = jnp.clip(1.0 + 0.15 * jax.random.normal(seeds[1], (D,), jnp.float32), 0.25, 1.75).astype(jnp.bfloat16)
    w_query = bell_draw(seeds[2], (D, H * HD), D ** -0.5, 0.125, ((0, 32),))
    w_key = bell_draw(seeds[3], (D, KV * HD), D ** -0.5, 0.125, ((0, 32),))
    w_value = bell_draw(seeds[4], (D, KV * HD), D ** -0.5, 0.125, ((0, 32),))
    w_out = bell_draw(seeds[5], (H * HD, D), (max(1, 128 * D // TOKENS)) ** -0.5, 0.75, ((0, 32),))
    gain_ffn = jnp.clip(1.0 + 0.15 * jax.random.normal(seeds[6], (D,), jnp.float32), 0.25, 1.75).astype(jnp.bfloat16)
    w_gate = bell_draw(seeds[7], (D, FF), D ** -0.5, 0.125, ((0, 32),))
    w_up = bell_draw(seeds[8], (D, FF), D ** -0.5, 0.125, ((0, 32),))
    w_down = bell_draw(seeds[9], (D, FF), FF ** -0.5, 0.078125, ((0, 32),))
    out_grad = bell_draw_with(seeds[10], (TOKENS, D), 1.0, 6.0, ((0, 32),), (0, 1, 32, 2.75))
    return {"tokens": tokens, "gain_attn": gain_attn, "w_query": w_query, "w_key": w_key, "w_value": w_value, "w_out": w_out, "gain_ffn": gain_ffn, "w_gate": w_gate, "w_up": w_up, "w_down": w_down, "out_grad": out_grad}


@jax.custom_vjp
def low(v):
    return lax.optimization_barrier(v.astype(jnp.bfloat16)).astype(jnp.float32)

@jax.custom_vjp
def low_back(v):
    return v

def low_keep(v):
    return (low(v), None)

def low_pass(kept, grad):
    return (grad,)

def back_keep(v):
    return (v, None)

def back_low(kept, grad):
    return (low(grad),)
low.defvjp(low_keep, low_pass)
low_back.defvjp(back_keep, back_low)
norm_eps = 1e-05
rope_base = 10000.0
masked_value = -1e+30

def matmul_high(left_side, right_side):
    return jnp.dot(left_side, right_side, precision=lax.Precision.HIGHEST, preferred_element_type=jnp.float32)

def rms_norm(values, gain):
    inverse = lax.rsqrt(lax.optimization_barrier(jnp.mean(values * values, axis=-1, keepdims=True)) + norm_eps)
    return values * inverse * gain

def rope_tables(positions, head_dim):
    half_dim = head_dim // 2
    frequency = rope_base ** (-(jnp.arange(half_dim, dtype=jnp.float32) * 2.0) / head_dim)
    angles = positions.astype(jnp.float32)[:, None] * frequency[None, :]
    return (jnp.cos(angles), jnp.sin(angles))

def rotate_heads(values, cosine_table, sine_table):
    half_dim = values.shape[-1] // 2
    lead_half = values[..., :half_dim]
    tail_half = values[..., half_dim:]
    cosine_part = cosine_table[:, None, :]
    sine_part = sine_table[:, None, :]
    return jnp.concatenate([lead_half * cosine_part - tail_half * sine_part, tail_half * cosine_part + lead_half * sine_part], axis=-1)

def attend_block(q_block, block_start, key_rows, value_rows):
    score_scale = HD ** (-0.5)
    scores = low_back(jnp.einsum('gqd,kd->gqk', q_block, key_rows, precision=lax.Precision.HIGHEST) * score_scale)
    rows_pos = block_start + jnp.arange(q_block.shape[1], dtype=jnp.int32)
    cols_pos = jnp.arange(key_rows.shape[0], dtype=jnp.int32)
    allowed = cols_pos[None, :] <= rows_pos[:, None]
    scores = jnp.where(allowed[None], scores, masked_value)
    log_total = jax.scipy.special.logsumexp(scores, axis=-1, keepdims=True)
    soft_probs = jnp.exp(scores - log_total)
    return jnp.einsum('gqk,kd->gqd', low(soft_probs), value_rows, precision=lax.Precision.HIGHEST)

def attend_slot(q_heads, key_rows, value_rows):
    seq_len = key_rows.shape[0]
    rows_block = min(1024, seq_len)
    blocks = seq_len // rows_block
    group_heads = q_heads.shape[0]
    q_blocks = q_heads.reshape(group_heads, blocks, rows_block, HD).transpose(1, 0, 2, 3)
    starts = jnp.arange(blocks, dtype=jnp.int32) * rows_block
    block_step = jax.checkpoint(attend_block)
    outputs = lax.map(lambda pieces: block_step(pieces[0], pieces[1], key_rows, value_rows), (q_blocks, starts))
    return outputs.transpose(1, 0, 2, 3).reshape(group_heads, seq_len, HD)

def forward(tokens_wide, gain_a, query_w, key_w, value_w, out_w, gain_f, gate_w, up_w, down_w):
    seq_len = tokens_wide.shape[0]
    group_heads = H // N_SEQ
    repeat = N_SEQ // KV
    h_attn = low(rms_norm(tokens_wide, gain_a))
    query_proj = low_back(low(matmul_high(h_attn, query_w)))
    key_proj = low_back(low(matmul_high(h_attn, key_w)))
    value_proj = low_back(low(matmul_high(h_attn, value_w)))
    key_slot = low_back(jnp.repeat(key_proj.reshape(seq_len, KV, HD), repeat, axis=1))
    value_slot = low_back(jnp.repeat(value_proj.reshape(seq_len, KV, HD), repeat, axis=1))
    cosine_table, sine_table = rope_tables(jnp.arange(seq_len, dtype=jnp.int32), HD)
    q_rot = low(rotate_heads(query_proj.reshape(seq_len, H, HD), cosine_table, sine_table))
    k_rot = low(rotate_heads(key_slot, cosine_table, sine_table))
    q_groups = q_rot.reshape(seq_len, N_SEQ, group_heads, HD).transpose(1, 2, 0, 3)
    k_groups = k_rot.transpose(1, 0, 2)
    v_groups = value_slot.transpose(1, 0, 2)
    outputs = lax.map(lambda pieces: attend_slot(pieces[0], pieces[1], pieces[2]), (q_groups, k_groups, v_groups))
    attn_out = low_back(low(outputs.transpose(2, 0, 1, 3).reshape(seq_len, H * HD)))
    middle = tokens_wide + low_back(matmul_high(attn_out, out_w))
    h_ffn = low(rms_norm(middle, gain_f))
    gate_proj = low_back(matmul_high(h_ffn, gate_w))
    up_proj = low_back(matmul_high(h_ffn, up_w))
    hidden = low(jax.nn.silu(gate_proj) * up_proj)
    return middle + matmul_high(hidden, down_w.T)

def reference(tokens, gain_attn, w_query, w_key, w_value, w_out, gain_ffn, w_gate, w_up, w_down, out_grad):
    block_out, pullback = jax.vjp(forward, tokens.astype(jnp.float32), gain_attn.astype(jnp.float32), w_query.astype(jnp.float32), w_key.astype(jnp.float32), w_value.astype(jnp.float32), w_out.astype(jnp.float32), gain_ffn.astype(jnp.float32), w_gate.astype(jnp.float32), w_up.astype(jnp.float32), w_down.astype(jnp.float32))
    grads = pullback(out_grad.astype(jnp.float32))
    return (block_out.astype(jnp.bfloat16), grads[0], grads[1], grads[2], grads[3], grads[4], grads[5], grads[6], grads[7], grads[8], grads[9])
```

```python
import functools
import math

import jax
import jax.numpy as jnp
from jax import lax
from jax.experimental import pallas as pl
from jax.experimental.pallas import tpu as pltpu
from jax.sharding import PartitionSpec as P

H = 32
KV = 4
HD = 64
AXES = ("seq", "fsdp")
norm_eps = 1e-05
rope_base = 10000.0
masked_value = -1e30
score_scale = HD ** (-0.5)
to_log2 = score_scale * math.log2(math.e)
bf16 = jnp.bfloat16
f32 = jnp.float32
KEY_TILE = 512
Q_ROWS = 512


def dot(a, b):
    return lax.dot_general(a, b, (((1,), (0,)), ((), ())), preferred_element_type=f32)


def dot_last(a, b):
    return lax.dot_general(a, b, (((1,), (1,)), ((), ())), preferred_element_type=f32)


def dot_first(a, b):
    return lax.dot_general(a, b, (((0,), (0,)), ((), ())), preferred_element_type=f32)


def inverse_rms(values):
    return lax.rsqrt(jnp.mean(values * values, axis=-1, keepdims=True) + norm_eps)


def rope_tables(positions):
    half = HD // 2
    frequency = rope_base ** (-(jnp.arange(half, dtype=f32) * 2.0) / HD)
    angles = positions.astype(f32)[..., None] * frequency
    return (jnp.cos(angles), jnp.sin(angles))


def rotate(values, cosine, sine):
    a, b = jnp.split(values, 2, axis=-1)
    return jnp.concatenate([a * cosine - b * sine, b * cosine + a * sine], axis=-1)


def unrotate(values, cosine, sine):
    a, b = jnp.split(values, 2, axis=-1)
    return jnp.concatenate([a * cosine + b * sine, b * cosine - a * sine], axis=-1)


def block_position(me, i, x_mask, z_mask):
    return me ^ (((i // 2) % 2) * x_mask + (i // 4) * z_mask)


def forward_kernel(x_mask, z_mask, rows, me_ref, q_ref, kv_ref, o_ref, ones_ref):
    me = me_ref[0]
    per_tile = KEY_TILE // rows
    lanes = lax.broadcasted_iota(jnp.int32, (KEY_TILE, 2 * HD), 1)

    def fill(j, carry):
        where = pl.ds(pl.multiple_of(j * KEY_TILE, KEY_TILE), KEY_TILE)
        ones_ref[where, :] = jnp.where(lanes < HD, jnp.ones((), bf16), kv_ref[where, :])
        return carry

    lax.fori_loop(0, kv_ref.shape[0] // KEY_TILE, fill, 0)

    def block(i, carry):
        position = block_position(me, i, x_mask, z_mask)
        last = position // per_tile
        q = q_ref[i]

        def scores(kt):
            physical = kt ^ (me // per_tile)
            where = pl.ds(pl.multiple_of(physical * KEY_TILE, KEY_TILE), KEY_TILE)
            return dot_last(q, kv_ref[where, :]), ones_ref[where, :]

        s, ones_v = scores(last)
        row = lax.broadcasted_iota(jnp.int32, s.shape, 0) % rows + (position % per_tile) * rows
        col = lax.broadcasted_iota(jnp.int32, s.shape, 1)
        key = ((col // rows) ^ (me % per_tile)) * rows + col % rows
        s = jnp.where(key <= row, s, masked_value)
        top = jnp.max(s, axis=-1, keepdims=True)
        p = jnp.exp2((s - top) * to_log2).astype(bf16)
        total = dot(p, ones_v)

        def turn(kt, state):
            top, total = state
            s, ones_v = scores(kt)
            new_top = jnp.maximum(top, jnp.max(s, axis=-1, keepdims=True))
            p = jnp.exp2((s - new_top) * to_log2).astype(bf16)
            total = total * jnp.exp2((top - new_top) * to_log2) + dot(p, ones_v)
            return new_top, total

        top, total = lax.fori_loop(0, last, turn, (top, total))
        weight = total[:, :1]
        lane = lax.broadcasted_iota(jnp.int32, total.shape, 1)
        o_ref[i] = jnp.where(lane < HD, top * to_log2 + jnp.log2(weight), total / weight)
        return carry

    lax.fori_loop(0, q_ref.shape[0], block, 0)


def backward_kernel(
    x_mask, z_mask, rows, me_ref, q_ref, g_ref, kv_ref, log_ref, delta_ref, dq_ref, dkv_ref
):
    me = me_ref[0]
    per_tile = KEY_TILE // rows

    def clear(j, carry):
        where = pl.ds(pl.multiple_of(j * KEY_TILE, KEY_TILE), KEY_TILE)
        dkv_ref[where, :] = jnp.zeros((KEY_TILE, 2 * HD), f32)
        return carry

    lax.fori_loop(0, kv_ref.shape[0] // KEY_TILE, clear, 0)

    def block(i, carry):
        position = block_position(me, i, x_mask, z_mask)
        last = position // per_tile
        q = q_ref[i]
        g = g_ref[i]
        log_total = log_ref[i]
        delta = delta_ref[i]

        def tile(kt, keep):
            physical = kt ^ (me // per_tile)
            where = pl.ds(pl.multiple_of(physical * KEY_TILE, KEY_TILE), KEY_TILE)
            kv = kv_ref[where, :]
            p = jnp.exp2(dot_last(kv, q) * to_log2 - log_total)
            if keep is not None:
                p = jnp.where(keep, p, 0.0)
            ds = (p * (dot_last(kv, g) - delta)).astype(bf16)
            dkv_ref[where, :] += dot(p.astype(bf16), g) + dot(ds, q)
            return dot_first(ds, kv)

        shape = (KEY_TILE, q.shape[0])
        col = lax.broadcasted_iota(jnp.int32, shape, 0)
        row = lax.broadcasted_iota(jnp.int32, shape, 1) % rows + (position % per_tile) * rows
        key = ((col // rows) ^ (me % per_tile)) * rows + col % rows
        dq = tile(last, key <= row)
        dq = lax.fori_loop(0, last, lambda kt, dq: dq + tile(kt, None), dq)
        dq_ref[i] = dq
        return carry

    lax.fori_loop(0, q_ref.shape[0], block, 0)


SMEM_SPEC = pl.BlockSpec(memory_space=pltpu.SMEM)
VMEM_SPEC = pl.BlockSpec(memory_space=pltpu.VMEM)


def attention_forward(me, q, kv, x_mask, z_mask, rows):
    tiles = q.shape[0] * kv.shape[0] // KEY_TILE // 2
    cost = pl.CostEstimate(
        flops=tiles * 4 * Q_ROWS * KEY_TILE * 2 * HD * 2,
        bytes_accessed=2 * (q.size * 3 + kv.size),
        transcendentals=tiles * Q_ROWS * KEY_TILE,
    )
    return pl.pallas_call(
        functools.partial(forward_kernel, x_mask, z_mask, rows),
        out_shape=jax.ShapeDtypeStruct(q.shape, f32),
        in_specs=[SMEM_SPEC, VMEM_SPEC, VMEM_SPEC],
        out_specs=VMEM_SPEC,
        scratch_shapes=[pltpu.VMEM(kv.shape, bf16)],
        compiler_params=pltpu.CompilerParams(vmem_limit_bytes=40 << 20),
        cost_estimate=cost,
        name="attention_forward",
    )(me, q, kv)


def attention_backward(me, q, g, kv, log_total, delta, x_mask, z_mask, rows):
    tiles = q.shape[0] * kv.shape[0] // KEY_TILE // 2
    cost = pl.CostEstimate(
        flops=tiles * 10 * Q_ROWS * KEY_TILE * 2 * HD * 2,
        bytes_accessed=2 * (q.size * 4 + kv.size * 3),
        transcendentals=tiles * Q_ROWS * KEY_TILE,
    )
    return pl.pallas_call(
        functools.partial(backward_kernel, x_mask, z_mask, rows),
        out_shape=(
            jax.ShapeDtypeStruct(q.shape, f32),
            jax.ShapeDtypeStruct(kv.shape, f32),
        ),
        in_specs=[SMEM_SPEC] + [VMEM_SPEC] * 5,
        out_specs=(VMEM_SPEC, VMEM_SPEC),
        compiler_params=pltpu.CompilerParams(vmem_limit_bytes=48 << 20),
        cost_estimate=cost,
        name="attention_backward",
    )(me, q, g, kv, log_total, delta)


def on_device(
    tokens, gain_attn, w_query, w_key, w_value, w_out, gain_ffn, w_gate, w_up, w_down, out_grad
):
    n_seq = lax.axis_size("seq")
    n_fsdp = lax.axis_size("fsdp")
    n = n_seq * n_fsdp
    me = lax.axis_index(AXES)
    rows = tokens.shape[0]
    width = tokens.shape[1]
    slab = w_gate.shape[0]
    hidden_width = w_gate.shape[1]
    group_heads = H // KV
    x_mask, z_mask, core = 1, 2 * n_fsdp, n_fsdp
    t_masks = [0, x_mask, z_mask, x_mask | z_mask]
    far = [n_fsdp << k for k in range(2, n_seq.bit_length() - 1)]
    near = [1 << k for k in range(1, n_fsdp.bit_length() - 1)]
    d_bits = far + near + [core]
    d_masks = [0]
    for bit in d_bits:
        d_masks = d_masks + [m | bit for m in d_masks]
    d_all = sum(d_bits)
    x_bit = me % 2
    z_bit = (me // z_mask) % 2
    t = 2 * z_bit + x_bit
    tok = 4 * rows

    def swap(value, mask):
        return lax.ppermute(value, AXES, [(i, i ^ mask) for i in range(n)])

    def order_t(p):
        q = [
            jnp.where(x_bit == 1, p[1], p[0]),
            jnp.where(x_bit == 1, p[0], p[1]),
            jnp.where(x_bit == 1, p[3], p[2]),
            jnp.where(x_bit == 1, p[2], p[3]),
        ]
        return [
            jnp.where(z_bit == 1, q[2], q[0]),
            jnp.where(z_bit == 1, q[3], q[1]),
            jnp.where(z_bit == 1, q[0], q[2]),
            jnp.where(z_bit == 1, q[1], q[3]),
        ]

    def exchange_t(piece):
        return order_t([piece(t)] + [swap(piece(t ^ r), t_masks[r]) for r in (1, 2, 3)])

    def gather_t(value):
        return jnp.concatenate([value] + [swap(value, m) for m in t_masks[1:]], axis=0)

    def scatter_t(partial):
        mine = partial[:rows]
        for r in (1, 2, 3):
            sent = swap(partial[r * rows : (r + 1) * rows].astype(bf16), t_masks[r])
            mine = mine + sent.astype(f32)
        return mine

    def gather_d(value):
        pieces = [value]
        for bit in far + near:
            pieces = pieces + [swap(p, bit) for p in pieces]
        half = jnp.concatenate(pieces, axis=0)
        return jnp.concatenate([half, swap(half, core)], axis=0)

    def scatter_d(own, other):
        total = own + swap(other.astype(bf16), core).astype(f32)
        for bit in reversed(far + near):
            half = total.shape[0] // 2
            total = total[:half] + swap(total[half:].astype(bf16), bit).astype(f32)
        return total

    unit = 2 * slab

    def place(mask):
        return sum(((mask // bit) % 2) << k for k, bit in enumerate(d_bits))

    def to_relative(value):
        parts = []
        for m in d_masks:
            for z in (0, z_mask):
                start = (((me & d_all) ^ m) + z) // 2 * unit
                parts.append(lax.dynamic_slice_in_dim(value, start, unit, value.ndim - 1))
        return jnp.concatenate(parts, axis=-1)

    def to_natural(value):
        parts = []
        for b in range(0, n, 2):
            start = ((place(b) ^ place(me)) * 2 + (1 if b & z_mask else 0)) * unit
            parts.append(lax.dynamic_slice_in_dim(value, start, unit, value.ndim - 1))
        return jnp.concatenate(parts, axis=-1)

    gains = jnp.stack([gain_attn, gain_ffn])
    natural_gains = gains
    for bit in [x_mask, z_mask] + d_bits:
        gains = jnp.stack([gains, swap(gains, bit)])
    lead = len(d_bits)
    gains = jnp.where(z_bit == 1, jnp.flip(gains, lead), gains)
    gains = jnp.where(x_bit == 1, jnp.flip(gains, lead + 1), gains)
    gains = jnp.moveaxis(gains, -2, 0).reshape(2, width).astype(f32)
    gain_a, gain_f = gains[0:1], gains[1:2]

    q_cols = group_heads * HD
    group_tokens = gather_t(to_relative(tokens))

    def qkv_piece(j):
        return jnp.concatenate(
            [
                lax.dynamic_slice_in_dim(w_query, j * q_cols, q_cols, 1),
                lax.dynamic_slice_in_dim(w_key, j * HD, HD, 1),
                lax.dynamic_slice_in_dim(w_value, j * HD, HD, 1),
            ],
            axis=1,
        )

    qkv_w = gather_d(jnp.concatenate(exchange_t(qkv_piece), axis=0))

    cols = hidden_width // 4

    def ffn_weight(w):
        return gather_d(
            jnp.concatenate(
                exchange_t(lambda j: lax.dynamic_slice_in_dim(w, j * cols, cols, 1)), axis=0
            )
        )

    gate_w, up_w, down_w = ffn_weight(w_gate), ffn_weight(w_up), ffn_weight(w_down)

    bits = n.bit_length() - 1
    z_place, x_place = z_mask.bit_length() - 1, 0
    source = {z_place: bits - 1, x_place: bits - 2}
    free = [b for b in range(bits - 2)]
    open_places = [b for b in range(bits) if b not in source]
    for b in list(open_places):
        if b in free:
            source[b] = b
            free.remove(b)
            open_places.remove(b)
    for b, s in zip(open_places, free):
        source[b] = s

    def goes_to(i):
        return sum(((i >> s) & 1) << b for b, s in source.items())

    def came_from(i):
        return sum(((i >> b) & 1) << s for b, s in source.items())

    per_group = n // 4
    out_pieces = [lax.ppermute(w_out, AXES, [(i, goes_to(i)) for i in range(n)])]
    for bit in far + near:
        out_pieces = out_pieces + [swap(p, bit) for p in out_pieces]
    out_half = jnp.concatenate(out_pieces, axis=0)
    out_both = jnp.concatenate([out_half, swap(out_half, core)], axis=0)
    my_row = came_from(me) % per_group
    out_places = [(my_row ^ (came_from(m) % per_group)) * slab for m in d_masks]
    out_w = jnp.zeros((per_group * slab, width), bf16)
    for k in range(per_group):
        out_w = lax.dynamic_update_slice_in_dim(
            out_w, out_both[k * slab : (k + 1) * slab], out_places[k], 0
        )

    wide = group_tokens.astype(f32)
    h_attn = (wide * inverse_rms(wide) * gain_a).astype(bf16)
    qkv = dot(h_attn, qkv_w).astype(bf16).astype(f32)
    blocks = jnp.stack([me ^ m for m in t_masks])
    positions = blocks[:, None] * rows + jnp.arange(rows, dtype=jnp.int32)
    cosine, sine = rope_tables(positions)
    cos_h, sin_h = cosine[:, None], sine[:, None]
    q = qkv[:, :q_cols].reshape(4, rows, group_heads, HD).transpose(0, 2, 1, 3)
    q = rotate(q, cos_h, sin_h).astype(bf16)
    q = jnp.concatenate([q, jnp.zeros_like(q)], axis=-1)
    per_block = Q_ROWS // rows
    n_blocks = 4 * group_heads // per_block
    q = q.reshape(n_blocks, Q_ROWS, 2 * HD)
    k = rotate(qkv[:, q_cols : q_cols + HD].reshape(4, rows, HD), cosine, sine).astype(bf16)
    v = qkv[:, q_cols + HD :].reshape(4, rows, HD).astype(bf16)
    kv = jnp.concatenate([k, v], axis=-1)
    chips = [m for m in d_masks if not m & core]
    kv = jnp.stack([kv] + [swap(kv, m) for m in chips[1:]])
    kv = jnp.concatenate([kv, swap(kv, core)], axis=0)
    order = list(reversed(d_bits)) + [z_mask, x_mask]
    axes = sorted(range(len(order)), key=lambda a: -order[a])
    kv = kv.reshape((2,) * len(order) + (rows, 2 * HD))
    kv = kv.transpose(axes + [len(order), len(order) + 1]).reshape(n * rows, 2 * HD)

    me_ref = me.reshape(1).astype(jnp.int32)
    attn = attention_forward(me_ref, q, kv, x_mask, z_mask, rows)
    log_total = attn[:, :, 0].reshape(n_blocks, 1, Q_ROWS)
    attn_wide = attn[:, :, HD:].reshape(4, group_heads, rows, HD).transpose(0, 2, 1, 3)
    attn_wide = attn_wide.reshape(tok, q_cols)
    attn_out = attn_wide.astype(bf16)
    middle = tokens.astype(f32) + scatter_t(dot(attn_out, out_w))

    inverse_ffn = inverse_rms(middle)
    normed_ffn = middle * inverse_ffn
    h_ffn = gather_t((to_relative(normed_ffn) * gain_f).astype(bf16))
    g = gather_t(to_relative(out_grad))
    gate = dot(h_ffn, gate_w)
    up = dot(h_ffn, up_w)
    sig = jax.nn.sigmoid(gate)
    act = gate * sig
    hidden = (act * up).astype(bf16)
    d_hidden = dot(g, down_w)
    d_gate = (d_hidden * up * sig * (1.0 + gate * (1.0 - sig))).astype(bf16)
    d_up = (d_hidden * act).astype(bf16)
    d_hffn = to_natural(scatter_t(dot_last(d_gate, gate_w) + dot_last(d_up, up_w)))
    block_out = (middle + to_natural(scatter_t(dot_last(hidden, down_w)))).astype(bf16)

    def weight_grad(left, right):
        half = left.shape[1] // 2
        other = dot_first(left[:, half:], right)
        own = dot_first(left[:, :half], right)
        return scatter_d(own, other)

    def give_back(shard):
        def piece(j):
            return lax.dynamic_slice_in_dim(shard, j * slab, slab, 0)

        got = [piece(t)] + [
            swap(piece(t ^ r).astype(bf16), t_masks[r]).astype(f32) for r in (1, 2, 3)
        ]
        return order_t(got)

    grad_gate = jnp.concatenate(give_back(weight_grad(h_ffn, d_gate)), axis=1)
    grad_up = jnp.concatenate(give_back(weight_grad(h_ffn, d_up)), axis=1)
    grad_down = jnp.concatenate(give_back(weight_grad(g, hidden)), axis=1)

    def natural_gain(own):
        return own

    gain_f_nat = to_natural(gain_f)
    gain_a_nat = to_natural(gain_a)
    scaled = d_hffn * gain_f_nat
    gain_ffn_term = jnp.sum(d_hffn * normed_ffn, axis=0)
    d_middle = out_grad.astype(f32) + inverse_ffn * (
        scaled - normed_ffn * jnp.mean(scaled * normed_ffn, axis=-1, keepdims=True)
    )
    d_branch = gather_t(d_middle.astype(bf16))
    d_attn = dot_last(d_branch, out_w).astype(bf16)

    out_term = dot_first(attn_out, d_branch)
    out_parts = [lax.dynamic_slice_in_dim(out_term, s, slab, 0) for s in out_places]
    half = per_group // 2
    out_shard = scatter_d(
        jnp.concatenate(out_parts[:half], axis=0), jnp.concatenate(out_parts[half:], axis=0)
    )
    grad_out_proj = lax.ppermute(
        out_shard.astype(bf16), AXES, [(goes_to(i), i) for i in range(n)]
    ).astype(f32)

    d_wide = d_attn.astype(f32)
    delta = jnp.sum((d_wide * attn_wide).reshape(4, rows, group_heads, HD), axis=-1)
    delta = delta.transpose(0, 2, 1).reshape(n_blocks, 1, Q_ROWS)
    d_heads = d_attn.reshape(4, rows, group_heads, HD).transpose(0, 2, 1, 3)
    d_heads = jnp.concatenate([jnp.zeros_like(d_heads), d_heads], axis=-1)
    d_heads = d_heads.reshape(n_blocks, Q_ROWS, 2 * HD)
    dq, dkv = attention_backward(
        me_ref, q, d_heads, kv, log_total, delta, x_mask, z_mask, rows
    )
    dq = dq[:, :, :HD].reshape(4, group_heads, rows, HD) * score_scale
    d_query = unrotate(dq, cos_h, sin_h).astype(bf16).transpose(0, 2, 1, 3).reshape(tok, q_cols)

    back = [axes.index(a) for a in range(len(order))]
    dkv = dkv.reshape((2,) * len(order) + (rows, 2 * HD))
    dkv = dkv.transpose(back + [len(order), len(order) + 1]).reshape(-1, tok, 2 * HD)
    half = dkv.shape[0] // 2
    dkv = dkv[:half] + swap(dkv[half:].astype(bf16), core).astype(f32)
    kv_sum = dkv[0]
    for k_mask, m in enumerate(chips[1:], 1):
        kv_sum = kv_sum + swap(dkv[k_mask].astype(bf16), m).astype(f32)
    dk = unrotate(kv_sum[:, :HD].reshape(4, rows, HD) * score_scale, cosine, sine)
    d_kv = jnp.concatenate([dk.reshape(tok, HD), kv_sum[:, HD:]], axis=1).astype(bf16)
    d_qkv = jnp.concatenate([d_query, d_kv], axis=1)

    d_hattn = to_natural(scatter_t(dot_last(d_qkv, qkv_w)))
    qkv_grads = give_back(weight_grad(h_attn, d_qkv))
    grad_query = jnp.concatenate([p[:, :q_cols] for p in qkv_grads], axis=1)
    grad_key = jnp.concatenate([p[:, q_cols : q_cols + HD] for p in qkv_grads], axis=1)
    grad_value = jnp.concatenate([p[:, q_cols + HD :] for p in qkv_grads], axis=1)

    own = tokens.astype(f32)
    inverse_attn = inverse_rms(own)
    normed_attn = own * inverse_attn
    scaled = d_hattn * gain_a_nat
    gain_attn_term = jnp.sum(d_hattn * normed_attn, axis=0)
    grad_tokens = d_middle + inverse_attn * (
        scaled - normed_attn * jnp.mean(scaled * normed_attn, axis=-1, keepdims=True)
    )
    gain_terms = jnp.stack([gain_attn_term, gain_ffn_term])
    for bit in t_masks[1:3] + d_bits:
        gain_terms = gain_terms + swap(gain_terms, bit)
    gain_terms = lax.dynamic_slice_in_dim(gain_terms, me * slab, slab, 1)
    return (
        block_out,
        grad_tokens,
        gain_terms[0],
        grad_query,
        grad_key,
        grad_value,
        grad_out_proj,
        gain_terms[1],
        grad_gate,
        grad_up,
        grad_down,
    )


def solution(mesh):
    spec2 = P(AXES, None)
    spec1 = P(AXES)
    return jax.shard_map(
        on_device,
        mesh=mesh,
        in_specs=(
            spec2,
            spec1,
            spec2,
            spec2,
            spec2,
            spec2,
            spec1,
            spec2,
            spec2,
            spec2,
            spec2,
        ),
        out_specs=(
            spec2,
            spec2,
            spec1,
            spec2,
            spec2,
            spec2,
            spec2,
            spec1,
            spec2,
            spec2,
            spec2,
        ),
        check_vma=False,
    )
```

```python
import functools
import math

import jax
import jax.numpy as jnp
from jax import lax
from jax.experimental import pallas as pl
from jax.experimental.pallas import tpu as pltpu
from jax.sharding import PartitionSpec as P

H = 32
KV = 4
HD = 64
AXES = ("seq", "fsdp")
norm_eps = 1e-05
rope_base = 10000.0
masked_value = -1e30
score_scale = HD ** (-0.5)
to_log2 = score_scale * math.log2(math.e)
bf16 = jnp.bfloat16
f32 = jnp.float32
KEY_TILE = 512
ONES = 16
LANES = 128
GAIN_ROWS = 16
CHUNKS = 2
HEADS = H // KV
PER_CHUNK = HEADS // CHUNKS
Q_COLS = HEADS * HD
QKV_COLS = Q_COLS + 2 * HD

SMEM_SPEC = pl.BlockSpec(memory_space=pltpu.SMEM)
VMEM_SPEC = pl.BlockSpec(memory_space=pltpu.VMEM)
ANY_SPEC = pl.BlockSpec(memory_space=pl.ANY)


def dot(a, b):
    return lax.dot_general(a, b, (((1,), (0,)), ((), ())), preferred_element_type=f32)


def dot_last(a, b):
    return lax.dot_general(a, b, (((1,), (1,)), ((), ())), preferred_element_type=f32)


def dot_first(a, b):
    return lax.dot_general(a, b, (((0,), (0,)), ((), ())), preferred_element_type=f32)


def inverse_rms(values):
    return lax.rsqrt(jnp.mean(values * values, axis=-1, keepdims=True) + norm_eps)


def rope_tables(positions):
    half = HD // 2
    frequency = rope_base ** (-(jnp.arange(half, dtype=f32) * 2.0) / HD)
    angles = positions.astype(f32)[None, :] * frequency[:, None]
    return (jnp.cos(angles), jnp.sin(angles))


def rotate(values, cosine, sine):
    a, b = values[: HD // 2], values[HD // 2 :]
    return jnp.concatenate([a * cosine - b * sine, b * cosine + a * sine], axis=0)


def unrotate(values, cosine, sine):
    a, b = values[: HD // 2], values[HD // 2 :]
    return jnp.concatenate([a * cosine + b * sine, b * cosine - a * sine], axis=0)


def hold(value, *others):
    return lax.optimization_barrier((value, others))[0]


def call(kernel, name, out, args, specs, flops, scratch=(), exps=0):
    out_shape = tuple(jax.ShapeDtypeStruct(s, d) for s, d in out)
    size = sum(a.size * a.dtype.itemsize for a in args)
    size += sum(math.prod(s.shape) * s.dtype.itemsize for s in out_shape)
    return pl.pallas_call(
        kernel,
        out_shape=out_shape,
        in_specs=specs,
        out_specs=(VMEM_SPEC,) * len(out_shape),
        scratch_shapes=list(scratch),
        compiler_params=pltpu.CompilerParams(vmem_limit_bytes=58 << 20),
        cost_estimate=pl.CostEstimate(flops=flops, bytes_accessed=size, transcendentals=exps),
        name=name,
    )(*args)


def columns_of(ref, starts, k):
    runs = [
        ref[:, pl.ds(pl.multiple_of(starts[2 * k + z], LANES), LANES)] for z in (0, 1)
    ]
    return jnp.concatenate(runs, axis=1)


def pack_kernel(member, q_ref, k_ref, v_ref, ga_ref, gf_ref, out_ref):
    slab = q_ref.shape[0]
    side = member[0]
    row = lax.broadcasted_iota(jnp.int32, (GAIN_ROWS, LANES), 0)
    lane = lax.broadcasted_iota(jnp.int32, (GAIN_ROWS, LANES), 1)
    gains = []
    for ref in (ga_ref, gf_ref):
        gains.append(jnp.concatenate([ref[...].astype(f32)] * (LANES // slab), axis=1))
    block = jnp.where(row == 0, gains[0], jnp.where(row == 1, gains[1], 0.0))
    block = jnp.where(lane // slab == side, block, 0.0).astype(bf16)
    block = jnp.concatenate([block, jnp.zeros((GAIN_ROWS, QKV_COLS - LANES), bf16)], axis=1)
    for i in range(4):
        at = i * (slab + GAIN_ROWS)
        out_ref[at : at + slab, :Q_COLS] = q_ref[:, i * Q_COLS : (i + 1) * Q_COLS]
        kv = [ref[:, i * HD : (i + 1) * HD] for ref in (k_ref, v_ref)]
        out_ref[at : at + slab, Q_COLS:] = jnp.concatenate(kv, axis=1)
        out_ref[at + slab : at + slab + GAIN_ROWS] = block


def pack_attention(side, w_query, w_key, w_value, gain_attn, gain_ffn):
    slab = w_query.shape[0]
    return call(
        pack_kernel,
        "pack_attention",
        [((4 * (slab + GAIN_ROWS), QKV_COLS), bf16)],
        [side, w_query, w_key, w_value, gain_attn.reshape(1, slab), gain_ffn.reshape(1, slab)],
        [SMEM_SPEC] + [VMEM_SPEC] * 5,
        0,
    )[0]


def pack_columns_kernel(cols, *refs):
    ins, out_ref = refs[:-1], refs[-1]
    slab = ins[0].shape[0]
    for i in range(4):
        for w, ref in enumerate(ins):
            out_ref[i * slab : (i + 1) * slab, w * cols : (w + 1) * cols] = ref[
                :, i * cols : (i + 1) * cols
            ]


def pack_columns(weights, name):
    slab, cols = weights[0].shape[0], weights[0].shape[1] // 4
    return call(
        functools.partial(pack_columns_kernel, cols),
        name,
        [((4 * slab, cols * len(weights)), bf16)],
        list(weights),
        [VMEM_SPEC] * len(weights),
        0,
    )[0]


def unpack_columns_kernel(cols, in_ref, *outs):
    slab = outs[0].shape[0]
    for i in range(4):
        for w, ref in enumerate(outs):
            ref[:, i * cols : (i + 1) * cols] = in_ref[
                i * slab : (i + 1) * slab, w * cols : (w + 1) * cols
            ].astype(f32)


def unpack_columns(value, count, name):
    slab, cols = value.shape[0] // 4, value.shape[1] // count
    return call(
        functools.partial(unpack_columns_kernel, cols),
        name,
        [((slab, 4 * cols), f32)] * count,
        [value],
        [VMEM_SPEC],
        0,
    )


def unpack_keys_kernel(member, in_ref, k_ref, v_ref, gain_ref):
    slab = k_ref.shape[0]
    gains = jnp.zeros((2, LANES), f32)
    keys, values = [], []
    for i in range(4):
        at = i * (slab + GAIN_ROWS)
        kv = in_ref[at : at + slab].astype(f32)
        keys.append(kv[:, :HD])
        values.append(kv[:, HD:])
        gains = gains + in_ref[at + slab : at + slab + GAIN_ROWS].astype(f32)[:2]
    k_ref[...] = jnp.concatenate(keys, axis=1)
    v_ref[...] = jnp.concatenate(values, axis=1)
    halves = [gains[:, j * slab : (j + 1) * slab] for j in range(2)]
    gain_ref[...] = jnp.where(member[0] == 0, halves[0], halves[1])


def unpack_keys(side, value):
    slab = value.shape[0] // 4 - GAIN_ROWS
    return call(
        unpack_keys_kernel,
        "unpack_keys",
        [((slab, 4 * HD), f32), ((slab, 4 * HD), f32), ((2, slab), f32)],
        [side, value],
        [SMEM_SPEC, VMEM_SPEC],
        0,
    )


def run_at(starts, j):
    start = starts[j]
    return pl.ds(start if isinstance(start, int) else pl.multiple_of(start, LANES), LANES)


def run_of(j):
    return slice(j * LANES, (j + 1) * LANES)


def sum_of(refs, columns=slice(None)):
    total = refs[0][:, columns].astype(f32)
    for ref in refs[1:]:
        total = total + ref[:, columns].astype(f32)
    return total


def middle_kernel(starts, tok_ref, gain_ref, *rest):
    parts, (mid_ref, h_ref) = rest[:4], rest[4:]
    middle = tok_ref[...].astype(f32) + sum_of(parts)
    mid_ref[...] = middle
    inverse = inverse_rms(middle)
    for j in range(tok_ref.shape[1] // LANES):
        run = run_at(starts, j)
        h_ref[:, run_of(j)] = (mid_ref[:, run] * inverse * gain_ref[:, run]).astype(bf16)


def middle_norm(starts, tokens, gain, parts):
    return call(
        middle_kernel,
        "middle_norm",
        [(tokens.shape, f32), (tokens.shape, bf16)],
        [starts, tokens, gain] + parts,
        [SMEM_SPEC] + [VMEM_SPEC] * 6,
        0,
    )


def arrange_kernel(starts, in_ref, out_ref):
    for j in range(in_ref.shape[1] // LANES):
        out_ref[:, run_of(j)] = in_ref[:, run_at(starts, j)]


def arrange(starts, value):
    return call(
        arrange_kernel,
        "arrange",
        [(value.shape, bf16)],
        [starts, value],
        [SMEM_SPEC, VMEM_SPEC],
        0,
    )[0]


def block_kernel(starts, mid_ref, part_ref, out_ref):
    rows = mid_ref.shape[0]
    parts = [part_ref.at[pl.ds(r * rows, rows)] for r in range(4)]
    for j in range(mid_ref.shape[1] // LANES):
        where = run_at(starts, j)
        out_ref[:, where] = (mid_ref[:, where] + sum_of(parts, run_of(j))).astype(bf16)


def block_output(starts, middle, parts):
    return call(
        block_kernel,
        "block_output",
        [(middle.shape, bf16)],
        [starts, middle, parts],
        [SMEM_SPEC, VMEM_SPEC, VMEM_SPEC],
        0,
    )[0]


def norm_back_kernel(starts, mid_ref, grad_ref, gain_ref, *rest):
    parts, (d_ref, low_ref, term_ref) = rest[:4], rest[4:]
    middle = mid_ref[...]
    inverse = inverse_rms(middle)
    for j in range(mid_ref.shape[1] // LANES):
        d_ref[:, run_at(starts, j)] = sum_of(parts, run_of(j))
    grad = d_ref[...]
    normed = middle * inverse
    term_ref[...] = jnp.sum(grad * normed, axis=0, keepdims=True)
    scaled = grad * gain_ref[...]
    mean = jnp.mean(scaled * normed, axis=-1, keepdims=True)
    d_middle = grad_ref[...].astype(f32) + inverse * (scaled - normed * mean)
    d_ref[...] = d_middle
    low_ref[...] = d_middle.astype(bf16)


def norm_back(starts, middle, out_grad, gain, parts):
    return call(
        norm_back_kernel,
        "norm_back",
        [(middle.shape, f32), (middle.shape, bf16), ((1, middle.shape[1]), f32)],
        [starts, middle, out_grad, gain] + parts,
        [SMEM_SPEC] + [VMEM_SPEC] * 7,
        0,
    )


def query_grad_kernel(count, starts, h_ref, d_ref, own_ref, other_ref):
    for ref, first in ((other_ref, count // 2), (own_ref, 0)):
        for k in range(count // 2):
            ref[k] = dot_first(columns_of(h_ref, starts, first + k), d_ref[...]).astype(bf16)


def query_grads(starts, h, d, count):
    half = (count // 2, 2 * LANES, d.shape[1])
    return call(
        functools.partial(query_grad_kernel, count),
        "query_grads",
        [(half, bf16), (half, bf16)],
        [starts, h, d],
        [SMEM_SPEC] + [VMEM_SPEC] * 2,
        2 * h.shape[0] * h.shape[1] * d.shape[1],
    )


def key_grad_kernel(count, starts, h_ref, d_ref, ga_ref, gf_ref, own_ref, other_ref):
    row = lax.broadcasted_iota(jnp.int32, (GAIN_ROWS, LANES), 0)
    slab = own_ref.shape[1] // 4 - GAIN_ROWS
    for ref, first in ((other_ref, count // 2), (own_ref, 0)):
        for k in range(count // 2):
            grad = dot_first(columns_of(h_ref, starts, first + k), d_ref[...]).astype(bf16)
            for i in range(4):
                where = run_at(starts, 2 * (first + k) + i // 2)
                gains = jnp.where(row == 0, ga_ref[:, where], gf_ref[:, where])
                at = i * (slab + GAIN_ROWS)
                ref[k, at : at + slab] = grad[i * slab : (i + 1) * slab]
                ref[k, at + slab : at + slab + GAIN_ROWS] = jnp.where(row < 2, gains, 0.0).astype(
                    bf16
                )


def key_grads(starts, h, d, gain_a, gain_f, count, slab):
    half = (count // 2, 4 * (slab + GAIN_ROWS), 2 * HD)
    return call(
        functools.partial(key_grad_kernel, count),
        "key_grads",
        [(half, bf16), (half, bf16)],
        [starts, h, d, gain_a, gain_f],
        [SMEM_SPEC] + [VMEM_SPEC] * 4,
        4 * h.shape[0] * h.shape[1] * HD,
    )


def weight_rows(piece):
    slab = piece.shape[0] // 4 - GAIN_ROWS
    at = [i * (slab + GAIN_ROWS) for i in range(4)]
    return jnp.concatenate([piece[a : a + slab] for a in at], axis=0)


def project_kernel(count, rows, starts, cos_ref, sin_ref, *rest):
    toks, pieces = rest[:4], rest[4 : 4 + count]
    h_ref, q_ref, kv_ref, gain_ref = rest[4 + count :]
    stride = pieces[0].shape[0] // 4
    for k in range(count):
        for z in (0, 1):
            gains = None
            for x in (0, 1):
                at = (2 * z + x + 1) * stride - GAIN_ROWS
                part = pieces[k][at : at + GAIN_ROWS, :LANES].astype(f32)
                gains = part if gains is None else gains + part
            gain_ref[:, run_at(starts, 2 * k + z)] = gains[:8]

    for r, tok_ref in enumerate(toks):
        wide = tok_ref[...].astype(f32)
        h_ref[r * rows : (r + 1) * rows] = (wide * inverse_rms(wide) * gain_ref[:1]).astype(bf16)
    total = None
    for k in range(count):
        product = dot(columns_of(h_ref, starts, k), weight_rows(pieces[k]))
        total = product if total is None else total + product
    turned = total.astype(bf16).astype(f32).T
    cosine, sine = cos_ref[...], sin_ref[...]
    for head in range(HEADS):
        q = rotate(turned[head * HD : (head + 1) * HD], cosine, sine).astype(bf16)
        at = head % PER_CHUNK * rows
        for r in range(4):
            q_ref[r, head // PER_CHUNK, :HD, at : at + rows] = q[:, r * rows : (r + 1) * rows]
    q_ref[:, :, HD:, :] = jnp.zeros((4, CHUNKS, HD, PER_CHUNK * rows), bf16)
    kv_ref[:HD] = rotate(turned[Q_COLS : Q_COLS + HD], cosine, sine).astype(bf16)
    kv_ref[HD:] = turned[Q_COLS + HD :].astype(bf16)


def project(starts, toks, cosine, sine, pieces):
    rows, width = toks[0].shape
    tok = 4 * rows
    count = len(pieces)
    return call(
        functools.partial(project_kernel, count, rows),
        "project",
        [
            ((tok, width), bf16),
            ((4, CHUNKS, 2 * HD, PER_CHUNK * rows), bf16),
            ((2 * HD, tok), bf16),
            ((8, width), f32),
        ],
        [starts, cosine, sine] + toks + pieces,
        [SMEM_SPEC] + [VMEM_SPEC] * (6 + count),
        2 * tok * width * QKV_COLS,
    )


def out_kernel(rows, places, attn_a_ref, attn_b_ref, *rest):
    pieces, parts, (attn_t_ref, w_ref) = rest[:-6], rest[-6:-2], rest[-2:]
    count = places.shape[0] // 2
    slab = pieces[0].shape[0] // count
    for k in range(2 * count):
        piece = pieces[k // count][k % count * slab : (k % count + 1) * slab, :]
        w_ref[pl.ds(pl.multiple_of(places[k], slab), slab), :] = piece
    for head in range(HEADS):
        at = head % PER_CHUNK * rows
        for r in range(4):
            block = (attn_a_ref, attn_b_ref)[r % 2][r // 2, head // PER_CHUNK, :, at : at + rows]
            attn_t_ref[head * HD : (head + 1) * HD, r * rows : (r + 1) * rows] = block.astype(bf16)
    step = 512
    for c in range(0, w_ref.shape[1], step):
        part = dot_first(attn_t_ref[...], w_ref[:, c : c + step]).astype(bf16)
        for r in range(4):
            parts[r][:, c : c + step] = part[r * rows : (r + 1) * rows]


def out_products(places, attn, pieces, rows):
    width = pieces[0].shape[1]
    tok = 4 * rows
    return call(
        functools.partial(out_kernel, rows),
        "out_products",
        [((rows, width), bf16)] * 4 + [((Q_COLS, tok), bf16), ((Q_COLS, width), bf16)],
        [places] + attn + pieces,
        [SMEM_SPEC] + [VMEM_SPEC] * (2 + len(pieces)),
        2 * tok * width * Q_COLS,
    )


def out_back_kernel(rows, w_ref, attn_a_ref, attn_b_ref, *rest):
    parts, (g_ref, delta_ref, d_ref) = rest[:4], rest[4:]
    for r in range(4):
        d_ref[r * rows : (r + 1) * rows] = parts[r][...]
    turned = dot_last(w_ref[...], d_ref[...]).astype(bf16)
    g_ref[:, :, :HD, :] = jnp.zeros((4, CHUNKS, HD, PER_CHUNK * rows), bf16)
    for head in range(HEADS):
        at = head % PER_CHUNK * rows
        chunk = head // PER_CHUNK
        for r in range(4):
            g = turned[head * HD : (head + 1) * HD, r * rows : (r + 1) * rows]
            g_ref[r, chunk, HD:, at : at + rows] = g
            attn = (attn_a_ref, attn_b_ref)[r % 2][r // 2, chunk, :, at : at + rows]
            delta = jnp.sum(g.astype(f32) * attn, axis=0, keepdims=True)
            delta_ref[r, chunk, :, at : at + rows] = delta


def out_back(w, attn, parts):
    rows, width = parts[0].shape
    return call(
        functools.partial(out_back_kernel, rows),
        "out_back",
        [
            ((4, CHUNKS, 2 * HD, PER_CHUNK * rows), bf16),
            ((4, CHUNKS, 1, PER_CHUNK * rows), f32),
        ],
        [w] + attn + parts,
        [VMEM_SPEC] * 7,
        8 * rows * width * Q_COLS,
        [pltpu.VMEM((4 * rows, width), bf16)],
    )


def out_grad_kernel(places, attn_t_ref, *rest):
    parts, (own_ref, other_ref, whole_ref, d_ref) = rest[:4], rest[4:]
    rows = parts[0].shape[0]
    for r in range(4):
        d_ref[r * rows : (r + 1) * rows] = parts[r][...]
    whole_ref[...] = dot(attn_t_ref[...], d_ref[...])
    half, slab = own_ref.shape[0], own_ref.shape[1]
    for k in range(half):
        for ref, place in ((own_ref, places[k]), (other_ref, places[half + k])):
            ref[k] = whole_ref[pl.ds(pl.multiple_of(place, slab), slab), :].astype(bf16)


def out_grads(places, attn_t, parts, slab):
    rows, width = parts[0].shape
    half = (places.shape[0] // 2, slab, width)
    return call(
        out_grad_kernel,
        "out_grads",
        [(half, bf16), (half, bf16)],
        [places, attn_t] + parts,
        [SMEM_SPEC] + [VMEM_SPEC] * 5,
        8 * rows * width * Q_COLS,
        [pltpu.VMEM((Q_COLS, width), f32), pltpu.VMEM((4 * rows, width), bf16)],
    )


def back_query_kernel(rows, dq0_ref, dq1_ref, cos_ref, sin_ref, d_ref, turned_ref):
    cosine, sine = cos_ref[...], sin_ref[...]
    for head in range(HEADS):
        at = head % PER_CHUNK * rows
        blocks = [
            (dq0_ref, dq1_ref)[r % 2][r // 2, head // PER_CHUNK, :, at : at + rows]
            for r in range(4)
        ]
        dq = jnp.concatenate(blocks, axis=1) * score_scale
        turned_ref[head * HD : (head + 1) * HD] = unrotate(dq, cosine, sine)
    d_ref[...] = turned_ref[...].T.astype(bf16)


def back_query(dq0, dq1, cosine, sine, rows):
    return call(
        functools.partial(back_query_kernel, rows),
        "back_query",
        [((4 * rows, Q_COLS), bf16)],
        [dq0, dq1, cosine, sine],
        [VMEM_SPEC] * 4,
        0,
        [pltpu.VMEM((Q_COLS, 4 * rows), f32)],
    )[0]


def back_project_kernel(count, rows, starts, dq_ref, kv_ref, cos_ref, sin_ref, *rest):
    toks, pieces, parts = rest[:4], rest[4 : 4 + count], rest[4 + count : 8 + count]
    d_ref, gain_ref, both_ref, inv_ref = rest[8 + count :]
    kv = kv_ref[...].T
    dk = unrotate(kv[:HD] * score_scale, cos_ref[...], sin_ref[...])
    d_ref[...] = jnp.concatenate([dk, kv[HD:]], axis=0).T.astype(bf16)
    both_ref[:, :Q_COLS] = dq_ref[...]
    both_ref[:, Q_COLS:] = d_ref[...]
    for r, tok_ref in enumerate(toks):
        inverse = inverse_rms(tok_ref[...].astype(f32))
        inv_ref[r * rows : (r + 1) * rows] = jnp.broadcast_to(inverse, (rows, LANES))
    for k in range(count):
        product = dot_last(both_ref[...], weight_rows(pieces[k]))
        for z in (0, 1):
            where = run_at(starts, 2 * k + z)
            term = None
            for r in range(4):
                at = slice(r * rows, (r + 1) * rows)
                value = product[at, run_of(z)]
                parts[r][:, where] = value.astype(bf16)
                normed = toks[r][:, where].astype(f32) * inv_ref[at]
                here = jnp.sum(value * normed, axis=0, keepdims=True)
                term = here if term is None else term + here
            gain_ref[:, where] = term


def back_project(starts, dq, kv_sum, cosine, sine, toks, pieces):
    rows, width = toks[0].shape
    tok = 4 * rows
    count = len(pieces)
    return call(
        functools.partial(back_project_kernel, count, rows),
        "back_project",
        [((rows, width), bf16)] * 4 + [((tok, 2 * HD), bf16), ((1, width), f32)],
        [starts, dq, kv_sum, cosine, sine] + toks + pieces,
        [SMEM_SPEC] + [VMEM_SPEC] * (8 + count),
        2 * tok * width * QKV_COLS,
        [pltpu.VMEM((tok, QKV_COLS), bf16), pltpu.VMEM((tok, LANES), f32)],
    )


def rows_of(tile):
    return pl.ds(pl.multiple_of(tile * KEY_TILE, KEY_TILE), KEY_TILE)


def causal(position, rows, columns):
    shape = (KEY_TILE, columns)
    key = lax.broadcasted_iota(jnp.int32, shape, 0)
    row = lax.broadcasted_iota(jnp.int32, shape, 1) % rows
    return key <= row + position % (KEY_TILE // rows) * rows


def fill_keys(place, rows, core, chip, own, all_ref, kvt_ref, kv_ref):
    per_tile = KEY_TILE // rows
    for p, (at, core_bit, member) in enumerate(place):
        where = pl.ds(pl.multiple_of((member ^ own) * rows, rows), rows)
        block = all_ref[core_bit ^ core, at ^ chip, :, where]
        kvt_ref[p // per_tile, :, p % per_tile * rows : (p % per_tile + 1) * rows] = block
        kv_ref[p * rows : (p + 1) * rows, :] = block.T


def forward_kernel(
    offsets, picks, place, rows, me_ref, q_ref, all_ref, o_ref, log_ref, kv_ref, kvt_ref, vt_ref
):
    me, core, chip, own = me_ref[0], me_ref[1], me_ref[2], me_ref[3]
    chunks = q_ref.shape[1]
    fill_keys(place, rows, core, chip, own, all_ref, kvt_ref, kv_ref)
    vt_ref[:, :ONES] = jnp.ones((vt_ref.shape[0], ONES, KEY_TILE), bf16)
    vt_ref[:, ONES:] = kvt_ref[:, HD:]
    for i, (pick, offset) in enumerate(zip(picks, offsets)):
        position = me ^ offset
        last = position // (KEY_TILE // rows)

        def scores(tile):
            kv = kv_ref[rows_of(tile), :]
            return [dot(kv, q_ref[pick, c]) for c in range(chunks)], vt_ref[tile]

        keep = causal(position, rows, q_ref.shape[3])
        found, vt = scores(last)
        state = []
        for s in found:
            s = jnp.where(keep, s, masked_value)
            top = jnp.max(s, axis=0, keepdims=True)
            state.append((top, dot(vt, jnp.exp2((s - top) * to_log2).astype(bf16))))

        def turn(kt, state):
            found, vt = scores(kt)
            out = []
            for s, (top, total) in zip(found, state):
                new_top = jnp.maximum(top, jnp.max(s, axis=0, keepdims=True))
                p = jnp.exp2((s - new_top) * to_log2).astype(bf16)
                out.append((new_top, total * jnp.exp2((top - new_top) * to_log2) + dot(vt, p)))
            return tuple(out)

        state = lax.fori_loop(0, last, turn, tuple(state))
        for c, (top, total) in enumerate(state):
            weight = total[:1]
            o_ref[i, c] = total[ONES:] / weight
            log_ref[i, c] = top * to_log2 + jnp.log2(weight)


def backward_kernel(offsets, picks, place, rows, core_mask, first, *refs):
    me_ref, q_ref, g_ref, all_ref, log_ref, delta_ref = refs[:6]
    kv_ref, kvt_ref = refs[-2:]
    if first:
        dq_ref, dkv_ref = refs[6:8]
        dkv_ref[...] = jnp.zeros_like(dkv_ref)
    else:
        begun_ref, dq_ref, own_ref, other_ref, dkv_ref = refs[6:11]
        dkv_ref[...] = begun_ref[...]
    me, core, chip, own = me_ref[0], me_ref[1], me_ref[2], me_ref[3]
    chunks = q_ref.shape[1]
    fill_keys(place, rows, core, chip, own, all_ref, kvt_ref, kv_ref)
    for i, (pick, offset) in enumerate(zip(picks, offsets)):
        position = me ^ offset
        last = position // (KEY_TILE // rows)

        def turn(tile, keep):
            kv = kv_ref[rows_of(tile), :]
            kvt = kvt_ref[tile]
            pairs = [(dot(kv, q_ref[pick, c]), dot(kv, g_ref[pick, c])) for c in range(chunks)]
            summed, out = None, []
            for c, (s, dp) in enumerate(pairs):
                p = jnp.exp2(s * to_log2 - log_ref[i, c])
                if keep is not None:
                    p = jnp.where(keep, p, 0.0)
                ds = (p * (dp - delta_ref[pick, c])).astype(bf16)
                part = dot_last(p.astype(bf16), g_ref[pick, c]) + dot_last(ds, q_ref[pick, c])
                summed = part if summed is None else summed + part
                out.append(dot(kvt, ds)[:HD])
            dkv_ref[rows_of(tile), :] += summed
            return tuple(out)

        dq = turn(last, causal(position, rows, q_ref.shape[3]))
        dq = lax.fori_loop(
            0, last, lambda tile, dq: tuple(a + b for a, b in zip(dq, turn(tile, None))), dq
        )
        for c in range(chunks):
            dq_ref[i, c] = dq[c]
    if not first:
        for p, (at, core_bit, member) in enumerate(place):
            if core_bit == 0:
                near = (p + core * core_mask) * rows
                far = (p + (1 - core) * core_mask) * rows
                where = pl.ds(pl.multiple_of((member ^ own) * rows, rows), rows)
                own_ref[at ^ chip, where] = dkv_ref[pl.ds(pl.multiple_of(near, rows), rows), :]
                other = dkv_ref[pl.ds(pl.multiple_of(far, rows), rows), :]
                other_ref[at ^ chip, where] = other.astype(bf16)


def attention_forward(me, q, kv_all, offsets, picks, place, rows):
    blocks, chunks, columns = len(picks), q.shape[1], q.shape[3]
    keys = len(place) * rows
    scores = blocks * chunks * columns * keys // 2
    return call(
        functools.partial(forward_kernel, offsets, picks, place, rows),
        "attention_forward",
        [((blocks, chunks, HD, columns), f32), ((blocks, chunks, 1, columns), f32)],
        [me, q, kv_all],
        [SMEM_SPEC, VMEM_SPEC, VMEM_SPEC],
        scores * 8 * HD,
        [
            pltpu.VMEM((keys, 2 * HD), bf16),
            pltpu.VMEM((keys // KEY_TILE, 2 * HD, KEY_TILE), bf16),
            pltpu.VMEM((keys // KEY_TILE, ONES + HD, KEY_TILE), bf16),
        ],
        scores,
    )


def attention_backward(
    me, q, g, kv_all, log_total, delta, dkv, offsets, picks, place, rows, core_mask
):
    chunks, columns = q.shape[1], q.shape[3]
    keys = len(place) * rows
    scores = len(picks) * chunks * columns * keys // 2
    shares = (kv_all.shape[1], kv_all.shape[3], 2 * HD)
    out = [((len(picks), chunks, HD, columns), f32)]
    scratch = [
        pltpu.VMEM((keys, 2 * HD), bf16),
        pltpu.VMEM((keys // KEY_TILE, 2 * HD, KEY_TILE), bf16),
    ]
    args = [me, q, g, kv_all, log_total, delta]
    if dkv is None:
        out = out + [((keys, 2 * HD), f32)]
    else:
        out = out + [(shares, f32), (shares, bf16)]
        scratch = [pltpu.VMEM((keys, 2 * HD), f32)] + scratch
        args = args + [dkv]
    return call(
        functools.partial(backward_kernel, offsets, picks, place, rows, core_mask, dkv is None),
        "attention_backward",
        out,
        args,
        [SMEM_SPEC] + [VMEM_SPEC] * (len(args) - 1),
        scores * 20 * HD,
        scratch,
        scores,
    )


def on_device(
    tokens, gain_attn, w_query, w_key, w_value, w_out, gain_ffn, w_gate, w_up, w_down, out_grad
):
    n_seq = lax.axis_size("seq")
    n_fsdp = lax.axis_size("fsdp")
    n = n_seq * n_fsdp
    me = lax.axis_index(AXES)
    rows, width = tokens.shape
    slab, hidden_width = w_gate.shape
    x_mask, z_mask, core = 1, 2 * n_fsdp, n_fsdp
    t_masks = [0, x_mask, z_mask, x_mask | z_mask]
    far = [n_fsdp << k for k in range(2, n_seq.bit_length() - 1)]
    near = [1 << k for k in range(1, n_fsdp.bit_length() - 1)]
    d_bits = far + near + [core]
    d_masks = [0]
    for bit in d_bits:
        d_masks = d_masks + [m | bit for m in d_masks]
    chips = d_masks[: len(d_masks) // 2]
    d_all = sum(d_bits)
    t_groups = [[b | m for m in t_masks] for b in sorted(d_masks)]

    def swap(value, mask):
        return lax.ppermute(value, AXES, [(i, i ^ mask) for i in range(n)])

    def trade(value, groups):
        return lax.all_to_all(
            value, AXES, split_axis=0, concat_axis=0, tiled=True, axis_index_groups=groups
        )

    def sum_blocks(value, count):
        value = value.reshape((count, -1) + value.shape[1:])
        total = value[0].astype(f32)
        for i in range(1, count):
            total = total + value[i].astype(f32)
        return total

    def spread(pieces, bits):
        pieces = dict(pieces)
        for bit in bits:
            pieces.update({m | bit: swap(v, bit) for m, v in list(pieces.items())})
        return pieces

    def beyond(pieces):
        return {m: v for m, v in pieces.items() if m}

    def joined(own, relayed):
        pieces = {**own, **relayed}
        half = [pieces[m] for m in chips]
        return half + [swap(p, core) for p in half]

    def sum_over(total, bits, after=None):
        for bit in reversed(bits):
            half = total.shape[0] // 2
            got = swap(total[half:].astype(bf16), bit)
            if after is not None:
                got = hold(got, after)
            total = total[:half].astype(f32) + got.astype(f32)
        return total

    def core_sum(pair):
        own, other = pair
        return own.astype(f32) + swap(other, core).astype(f32)

    unit = 2 * slab
    aligned = unit == LANES
    zs = jnp.array([0, z_mask], jnp.int32)
    relative = ((me & d_all) ^ jnp.array(d_masks, jnp.int32))[:, None] + zs[None, :]
    relative = (relative.reshape(-1) // 2 * unit).astype(jnp.int32)
    t = me % 2 + 2 * ((me // z_mask) % 2)
    fixed = [(m | z) // 2 * unit for m in sorted(d_masks) for z in (0, z_mask)]
    fixed = jnp.array(fixed, jnp.int32)
    d_groups = [[b | m for m in sorted(d_masks)] for b in t_masks]
    side = (me % 2).reshape(1).astype(jnp.int32)

    def arranged(value, where):
        return value.reshape(value.shape[0], -1, unit)[:, where // unit].reshape(value.shape)

    def restored(value, where):
        runs = value.reshape(value.shape[0], -1, unit)
        return jnp.zeros_like(runs).at[:, where // unit].set(runs).reshape(value.shape)

    if aligned:
        starts, n_pieces = relative, len(d_masks)
    else:
        starts, n_pieces = jnp.arange(0, width, LANES, dtype=jnp.int32), width // (2 * LANES)

    def copies(value, count):
        shape = (count,) + value.shape
        return jnp.broadcast_to(value[None], shape).reshape((-1,) + value.shape[1:])

    def gather_t(value):
        return [value] + [swap(value, m) for m in t_masks[1:]]

    def relay_t(value):
        along = swap(value, z_mask)
        return [value, swap(value, x_mask), along, swap(along, x_mask)]

    def scatter_t(parts):
        return [parts[0]] + [swap(p, m) for p, m in zip(parts[1:], t_masks[1:])]

    def blocks_of(value):
        return [value[r * rows : (r + 1) * rows] for r in range(4)]

    def send(total, bits):
        total = sum_over(total, bits[1:])
        half = total.shape[0] // 2
        return total[:half].astype(f32), swap(total[half:].astype(bf16), bits[0])

    def give_back(total):
        return trade(total.reshape(4 * slab, -1).astype(bf16), t_groups)

    def by_member(value):
        size = value.shape[0] // 4
        parts = [lax.dynamic_slice_in_dim(value, (t ^ r) * size, size, 0) for r in range(4)]
        return jnp.concatenate(parts, axis=0)

    qkv_shard = trade(pack_attention(side, w_query, w_key, w_value, gain_attn, gain_ffn), t_groups)
    cols = hidden_width // 4
    qkv_far = spread({0: qkv_shard}, far)
    qkv_own = spread({0: qkv_shard}, near)
    near_tokens = hold(tokens, qkv_shard)
    toks = [tokens] + [swap(near_tokens, m) for m in t_masks[1:3]]
    toks = toks + [swap(hold(tokens, qkv_far, qkv_own), t_masks[3])]
    qkv_w = joined(qkv_own, spread(beyond(qkv_far), near))
    if aligned:
        qkv_k = qkv_w
    else:
        parts = jnp.stack(qkv_w).reshape(-1, 2, 2, slab + GAIN_ROWS, QKV_COLS)
        runs = parts[:, :, :, :slab].reshape(-1, unit, QKV_COLS)
        whole = jnp.zeros_like(runs).at[relative // unit].set(runs).reshape(-1, 4, 64, QKV_COLS)
        gains = jnp.stack(
            [parts[:, :, x, slab:, x * slab : (x + 1) * slab] for x in (0, 1)], axis=3
        ).reshape(-1, GAIN_ROWS, unit)
        gains = jnp.zeros_like(gains).at[relative // unit].set(gains)
        gains = jnp.moveaxis(gains, 1, 0).reshape(GAIN_ROWS, -1, 2, 64)
        gains = jnp.moveaxis(gains, 0, 2)
        lane = jnp.arange(QKV_COLS) // 64
        extra = jnp.where(
            lane[None, None, None] == jnp.arange(2)[None, :, None, None],
            jnp.tile(gains, (1, 1, 1, QKV_COLS // 64)),
            jnp.zeros((), bf16),
        ).reshape(-1, 4, GAIN_ROWS, QKV_COLS)
        whole = jnp.concatenate([whole, extra], axis=2).reshape(n_pieces, -1, QKV_COLS)
        qkv_k = [whole[i] for i in range(n_pieces)]

    bits = n.bit_length() - 1
    source = {z_mask.bit_length() - 1: bits - 1, 0: bits - 2}
    free = list(range(bits - 2))
    open_places = [b for b in range(bits) if b not in source]
    for b in list(open_places):
        if b in free:
            source[b] = b
            free.remove(b)
            open_places.remove(b)
    source.update(zip(open_places, free))

    def goes_to(i):
        return sum(((i >> s) & 1) << b for b, s in source.items())

    def came_from(i):
        return sum(((i >> b) & 1) << s for b, s in source.items())

    per_group = n // 4
    out_shard = lax.ppermute(hold(w_out, qkv_shard), AXES, [(i, goes_to(i)) for i in range(n)])
    my_row = came_from(me) % per_group
    out_places = jnp.array([came_from(m) % per_group for m in d_masks], jnp.int32)
    out_places = ((my_row ^ out_places) * slab).astype(jnp.int32)

    out_shard = hold(out_shard, qkv_far)
    out_far = spread({0: out_shard}, far)
    out_own = spread({0: out_shard}, near)
    qkv_k, toks, out_far, out_own = lax.optimization_barrier((qkv_k, toks, out_far, out_own))
    out_all = {**out_own, **spread(beyond(out_far), near)}
    blocks = me ^ jnp.array(t_masks, jnp.int32)
    positions = (blocks[:, None] * rows + jnp.arange(rows, dtype=jnp.int32)).reshape(-1)
    cosine, sine = rope_tables(positions)
    h_attn, q, kv, gains = project(starts, toks, cosine, sine, qkv_k)
    gain_a, gain_f = gains[0:1], gains[1:2]
    pair_shard = trade(hold(pack_columns([w_gate, w_up], "pack_gate_up"), kv), t_groups)
    kv_parts = [kv] + [swap(kv, m) for m in chips[1:]]
    kv_parts, pair_shard, out_all = lax.optimization_barrier((kv_parts, pair_shard, out_all))
    kv = jnp.stack(kv_parts)
    kv_all = jnp.stack([kv, swap(kv, core)])
    place = [
        (
            chips.index(p & sum(far + near)),
            1 if p & core else 0,
            t_masks.index(p & (x_mask | z_mask)),
        )
        for p in range(n)
    ]
    my_chip = sum(((me // bit) % 2) << i for i, bit in enumerate(far + near))
    me_ref = jnp.stack([me, (me // core) % 2, my_chip, t]).astype(jnp.int32)

    pair_w = lax.all_gather(pair_shard, AXES, axis=0, tiled=True, axis_index_groups=d_groups)
    out_half = jnp.concatenate([out_all[m] for m in chips], axis=0)
    out_pieces = [out_half, swap(hold(out_half, kv_all), core)]
    down_shard = trade(pack_columns([hold(w_down, kv_all)], "pack_down"), t_groups)
    g4 = arrange(relative, out_grad) if aligned else arranged(out_grad, relative)

    def forward(x, q):
        return attention_forward(
            me_ref, q, kv_all, [x * x_mask, z_mask + x * x_mask], [x, 2 + x], place, rows
        )

    def backward(x, dkv):
        return attention_backward(
            me_ref,
            q,
            d_heads,
            kv_all,
            log_totals[x],
            delta,
            dkv,
            [x * x_mask, z_mask + x * x_mask],
            [x, 2 + x],
            place,
            rows,
            core,
        )

    attn_a, log_a = forward(0, q)
    attn_a, q_b, out_pieces, down_shard = lax.optimization_barrier(
        (attn_a, q, out_pieces, down_shard)
    )
    down_own = spread({0: hold(down_shard, attn_a)}, near)
    g = trade(copies(hold(g4, attn_a), 4), t_groups)
    attn_b, log_b = forward(1, q_b)
    attn, log_totals = [attn_a, attn_b], [log_a, log_b]
    *middle_parts, attn_t, out_w = out_products(out_places, attn, out_pieces, rows)
    middle_parts = scatter_t(middle_parts)

    def halves(pieces):
        half = jnp.concatenate([pieces[m] for m in chips], axis=0)
        return [half, swap(half, core)]

    middle_parts, down_own, g = lax.optimization_barrier((middle_parts, down_own, g))
    down_far = spread({0: hold(down_shard, middle_parts)}, far)
    g = by_member(hold(g, middle_parts))

    if aligned:
        middle, h = middle_norm(fixed, tokens, gain_f, middle_parts)
    else:
        middle = tokens.astype(f32) + sum([p.astype(f32) for p in middle_parts])
        h = arranged((middle * inverse_rms(middle) * gain_f).astype(bf16), fixed)
    h_parts = gather_t(h)
    h_parts, g = lax.optimization_barrier((h_parts, g))
    down_all = {**down_own, **spread(hold(beyond(down_far), h_parts), near)}
    h_ffn = jnp.concatenate(h_parts, axis=0)
    half_width = width // 2

    def by_halves(left, w):
        return dot(left[:, :half_width], w[0]) + dot(left[:, half_width:], w[1])

    down_w = halves(down_all)
    pair = dot(h_ffn, pair_w)
    gate, up = pair[:, :cols], pair[:, cols:]
    sig = jax.nn.sigmoid(gate)
    act = gate * sig
    hidden = (act * up).astype(bf16)
    d_hidden = by_halves(g, down_w)
    d_gate = (d_hidden * up * sig * (1.0 + gate * (1.0 - sig))).astype(bf16)
    d_up = (d_hidden * act).astype(bf16)
    d_pair = jnp.concatenate([d_gate, d_up], axis=1)
    d_hffn_part = dot_last(d_pair, pair_w).astype(bf16)
    d_hffn_blocks = blocks_of(d_hffn_part)
    d_hffn_parts = scatter_t(d_hffn_blocks)

    def weight_grad(left, right):
        other = dot_first(left[:, half_width:], right).astype(bf16)
        return dot_first(left[:, :half_width], right) + swap(other, core).astype(f32)

    pair_grad = dot_first(hold(h_ffn, d_hffn_blocks), d_pair).astype(bf16)
    pair_total = lax.psum_scatter(
        pair_grad, AXES, scatter_dimension=0, tiled=True, axis_index_groups=d_groups
    )
    block_part = jnp.concatenate(
        [dot_last(hold(hidden, pair_grad), w).astype(bf16) for w in down_w], axis=1
    )
    d_hffn_parts, pair_grad, block_part = lax.optimization_barrier(
        (d_hffn_parts, pair_grad, block_part)
    )
    down_sum = weight_grad(hold(g, d_hffn_parts), hidden)
    block_blocks = by_member(hold(block_part, d_hffn_parts))

    if aligned:
        d_middle, d_low, gain_ffn_term = norm_back(fixed, middle, out_grad, gain_f, d_hffn_parts)
    else:
        d_hffn = restored(sum([p.astype(f32) for p in d_hffn_parts]), fixed)
        inverse = inverse_rms(middle)
        normed = middle * inverse
        scaled = d_hffn * gain_f
        gain_ffn_term = jnp.sum(d_hffn * normed, axis=0, keepdims=True)
        d_middle = out_grad.astype(f32) + inverse * (
            scaled - normed * jnp.mean(scaled * normed, axis=-1, keepdims=True)
        )
        d_low = d_middle.astype(bf16)
    d_branch = relay_t(d_low)
    d_branch, down_sum, block_blocks = lax.optimization_barrier((d_branch, down_sum, block_blocks))
    d_heads, delta = out_back(out_w, attn, d_branch)

    block_parts = trade(hold(block_blocks, d_heads), t_groups)
    down_near = hold(down_sum, d_heads)
    for bit in reversed(near):
        half = down_near.shape[0] // 2
        down_got = swap(down_near[half:].astype(bf16), bit)
        down_near = down_near[:half].astype(f32)
        if bit != near[0]:
            down_near = down_near + down_got.astype(f32)
    out_pair = out_grads(out_places, attn_t, hold(d_branch, d_heads), slab)
    out_sum = core_sum(out_pair)
    dq0, dkv = backward(0, None)
    dkv, out_sum = lax.optimization_barrier((dkv, out_sum))
    out_keep, out_got = send(out_sum, near)
    dq1, own, other = backward(1, dkv)
    other, down_got, block_parts, out_got = lax.optimization_barrier(
        (other, down_got, block_parts, out_got)
    )
    kv_sums = own + swap(other, core).astype(f32)
    kv_sends = [kv_sums[i].astype(bf16) for i in range(len(chips))]
    kv_parts = [swap(kv_sends[i], m) for i, m in enumerate(chips) if m]
    dq0, dq1, block_parts, down_got, out_got, pair_total = hold(
        (dq0, dq1, block_parts, down_got, out_got, pair_total), kv_sends
    )
    d_query = back_query(dq0, dq1, cosine, sine, rows)
    if aligned:
        query_pair = query_grads(starts, h_attn, d_query, n_pieces)
    else:
        grads = dot_first(h_attn, d_query).astype(bf16).reshape(-1, unit, Q_COLS)
        grads = grads[relative // unit].reshape(len(d_masks), -1, Q_COLS)
        query_pair = grads[: len(chips)], grads[len(chips) :]
    query_sum = core_sum(query_pair)
    down_keep, down_got = send(down_near + down_got.astype(f32), far)
    pair_parts = trade(pair_total, t_groups)
    if aligned:
        block_out = block_output(relative, middle, block_parts)
    else:
        block_out = (middle + restored(sum_blocks(block_parts, 4), relative)).astype(bf16)
    kv_parts, query_sum, block_out = lax.optimization_barrier((kv_parts, query_sum, block_out))
    kv_sum = kv_sums[0]
    for part in kv_parts:
        kv_sum = kv_sum + part.astype(f32)
    query_keep, query_got = send(query_sum, near)
    out_keep, out_got = send(out_keep + out_got.astype(f32), far)
    *d_hattn_blocks, d_kv, gain_attn_part = back_project(
        starts, d_query, kv_sum, cosine, sine, toks, qkv_k
    )
    d_hattn_blocks, query_got = lax.optimization_barrier((d_hattn_blocks, query_got))
    query_keep, query_got = send(query_keep + query_got.astype(f32), far)
    d_hattn_parts = scatter_t(d_hattn_blocks)
    d_kv, gain_attn_part = hold((d_kv, gain_attn_part), d_hattn_blocks)
    if aligned:
        own, other = key_grads(starts, h_attn, d_kv, gain_attn_part, gain_ffn_term, n_pieces, slab)
    else:
        grads = dot_first(h_attn, d_kv).astype(bf16).reshape(-1, unit, 2 * HD)
        grads = grads[relative // unit].reshape(-1, 4, slab, 2 * HD)
        terms = jnp.concatenate([gain_attn_part, gain_ffn_term]).astype(bf16)
        terms = terms.reshape(2, -1, unit)[:, relative // unit].reshape(2, -1, 2, 1, unit)
        terms = jnp.moveaxis(jnp.broadcast_to(terms, terms.shape[:3] + (2, unit)), 0, 3)
        terms = terms.reshape(-1, 4, 2, unit)
        terms = jnp.pad(terms, ((0, 0), (0, 0), (0, GAIN_ROWS - 2), (0, 2 * HD - unit)))
        grads = jnp.concatenate([grads, terms], axis=2).reshape(len(d_masks), -1, 2 * HD)
        own, other = grads[: len(chips)], grads[len(chips) :]
    key_sum = core_sum((own, other))
    grad_gate, grad_up = unpack_columns(pair_parts, 2, "unpack_gate_up")
    d_hattn_parts, key_sum, query_got, out_got, down_got, grad_gate, grad_up = (
        lax.optimization_barrier(
            (d_hattn_parts, key_sum, query_got, out_got, down_got, grad_gate, grad_up)
        )
    )
    query_total = query_keep + query_got.astype(f32)
    out_total = (out_keep + out_got.astype(f32)).astype(bf16).reshape(slab, width)
    down_total = down_keep + down_got.astype(f32)
    key_total = sum_over(sum_over(key_sum, near), far)
    grad_query = unpack_columns(give_back(query_total), 1, "unpack_query")[0]
    grad_out_proj = lax.ppermute(out_total, AXES, [(goes_to(i), i) for i in range(n)]).astype(f32)
    grad_down = unpack_columns(give_back(down_total), 1, "unpack_down")[0]
    key_parts = trade(key_total.reshape(-1, 2 * HD).astype(bf16), t_groups)
    grad_key, grad_value, gain_terms = unpack_keys(side, key_parts)

    own = tokens.astype(f32)
    inverse_attn = inverse_rms(own)
    normed_attn = own * inverse_attn
    d_hattn = d_hattn_parts[0].astype(f32)
    for part in d_hattn_parts[1:]:
        d_hattn = d_hattn + part.astype(f32)
    scaled = d_hattn * gain_a
    grad_tokens = d_middle + inverse_attn * (
        scaled - normed_attn * jnp.mean(scaled * normed_attn, axis=-1, keepdims=True)
    )
    return (
        block_out,
        grad_tokens,
        gain_terms[0],
        grad_query,
        grad_key,
        grad_value,
        grad_out_proj,
        gain_terms[1],
        grad_gate,
        grad_up,
        grad_down,
    )


def solution(mesh):
    spec2 = P(AXES, None)
    spec1 = P(AXES)
    return jax.shard_map(
        on_device,
        mesh=mesh,
        in_specs=(
            spec2,
            spec1,
            spec2,
            spec2,
            spec2,
            spec2,
            spec1,
            spec2,
            spec2,
            spec2,
            spec2,
        ),
        out_specs=(
            spec2,
            spec2,
            spec1,
            spec2,
            spec2,
            spec2,
            spec2,
            spec1,
            spec2,
            spec2,
            spec2,
        ),
        check_vma=False,
    )
```

```python
import functools
import math

import jax
import jax.numpy as jnp
from jax import lax
from jax.experimental import pallas as pl
from jax.experimental.pallas import tpu as pltpu
from jax.sharding import PartitionSpec as P

H = 32
KV = 4
HD = 64
AXES = ("seq", "fsdp")
norm_eps = 1e-05
rope_base = 10000.0
masked_value = -1e30
score_scale = HD ** (-0.5)
to_log2 = score_scale * math.log2(math.e)
bf16 = jnp.bfloat16
f32 = jnp.float32
KEY_TILE = 512
ONES = 16
LANES = 128
GAIN_ROWS = 16
CHUNKS = 2
HEADS = H // KV
PER_CHUNK = HEADS // CHUNKS
Q_COLS = HEADS * HD
QKV_COLS = Q_COLS + 2 * HD

SMEM_SPEC = pl.BlockSpec(memory_space=pltpu.SMEM)
VMEM_SPEC = pl.BlockSpec(memory_space=pltpu.VMEM)
ANY_SPEC = pl.BlockSpec(memory_space=pl.ANY)


def dot(a, b):
    return lax.dot_general(a, b, (((1,), (0,)), ((), ())), preferred_element_type=f32)


def dot_last(a, b):
    return lax.dot_general(a, b, (((1,), (1,)), ((), ())), preferred_element_type=f32)


def dot_first(a, b):
    return lax.dot_general(a, b, (((0,), (0,)), ((), ())), preferred_element_type=f32)


def inverse_rms(values):
    return lax.rsqrt(jnp.mean(values * values, axis=-1, keepdims=True) + norm_eps)


def rope_tables(positions):
    half = HD // 2
    frequency = rope_base ** (-(jnp.arange(half, dtype=f32) * 2.0) / HD)
    angles = positions.astype(f32)[None, :] * frequency[:, None]
    return (jnp.cos(angles), jnp.sin(angles))


def rotate(values, cosine, sine):
    a, b = values[: HD // 2], values[HD // 2 :]
    return jnp.concatenate([a * cosine - b * sine, b * cosine + a * sine], axis=0)


def unrotate(values, cosine, sine):
    a, b = values[: HD // 2], values[HD // 2 :]
    return jnp.concatenate([a * cosine + b * sine, b * cosine - a * sine], axis=0)


def hold(value, *others):
    return lax.optimization_barrier((value, others))[0]


def call(kernel, name, out, args, specs, flops, scratch=(), exps=0):
    out_shape = tuple(jax.ShapeDtypeStruct(s, d) for s, d in out)
    size = sum(a.size * a.dtype.itemsize for a in args)
    size += sum(math.prod(s.shape) * s.dtype.itemsize for s in out_shape)
    return pl.pallas_call(
        kernel,
        out_shape=out_shape,
        in_specs=specs,
        out_specs=(VMEM_SPEC,) * len(out_shape),
        scratch_shapes=list(scratch),
        compiler_params=pltpu.CompilerParams(vmem_limit_bytes=58 << 20),
        cost_estimate=pl.CostEstimate(flops=flops, bytes_accessed=size, transcendentals=exps),
        name=name,
    )(*args)


def columns_of(ref, starts, k):
    runs = [
        ref[:, pl.ds(pl.multiple_of(starts[2 * k + z], LANES), LANES)] for z in (0, 1)
    ]
    return jnp.concatenate(runs, axis=1)


def pack_kernel(member, q_ref, k_ref, v_ref, ga_ref, gf_ref, out_ref):
    slab = q_ref.shape[0]
    side = member[0]
    row = lax.broadcasted_iota(jnp.int32, (GAIN_ROWS, LANES), 0)
    lane = lax.broadcasted_iota(jnp.int32, (GAIN_ROWS, LANES), 1)
    gains = []
    for ref in (ga_ref, gf_ref):
        gains.append(jnp.concatenate([ref[...].astype(f32)] * (LANES // slab), axis=1))
    block = jnp.where(row == 0, gains[0], jnp.where(row == 1, gains[1], 0.0))
    block = jnp.where(lane // slab == side, block, 0.0).astype(bf16)
    block = jnp.concatenate([block, jnp.zeros((GAIN_ROWS, QKV_COLS - LANES), bf16)], axis=1)
    for i in range(4):
        at = i * (slab + GAIN_ROWS)
        out_ref[at : at + slab, :Q_COLS] = q_ref[:, i * Q_COLS : (i + 1) * Q_COLS]
        kv = [ref[:, i * HD : (i + 1) * HD] for ref in (k_ref, v_ref)]
        out_ref[at : at + slab, Q_COLS:] = jnp.concatenate(kv, axis=1)
        out_ref[at + slab : at + slab + GAIN_ROWS] = block


def pack_attention(side, w_query, w_key, w_value, gain_attn, gain_ffn):
    slab = w_query.shape[0]
    return call(
        pack_kernel,
        "pack_attention",
        [((4 * (slab + GAIN_ROWS), QKV_COLS), bf16)],
        [side, w_query, w_key, w_value, gain_attn.reshape(1, slab), gain_ffn.reshape(1, slab)],
        [SMEM_SPEC] + [VMEM_SPEC] * 5,
        0,
    )[0]


def pack_columns_kernel(cols, *refs):
    ins, out_ref = refs[:-1], refs[-1]
    slab = ins[0].shape[0]
    for i in range(4):
        for w, ref in enumerate(ins):
            out_ref[i * slab : (i + 1) * slab, w * cols : (w + 1) * cols] = ref[
                :, i * cols : (i + 1) * cols
            ]


def pack_columns(weights, name):
    slab, cols = weights[0].shape[0], weights[0].shape[1] // 4
    return call(
        functools.partial(pack_columns_kernel, cols),
        name,
        [((4 * slab, cols * len(weights)), bf16)],
        list(weights),
        [VMEM_SPEC] * len(weights),
        0,
    )[0]


def unpack_columns_kernel(cols, in_ref, *outs):
    slab = outs[0].shape[0]
    for i in range(4):
        for w, ref in enumerate(outs):
            ref[:, i * cols : (i + 1) * cols] = in_ref[
                i * slab : (i + 1) * slab, w * cols : (w + 1) * cols
            ].astype(f32)


def unpack_columns(value, count, name):
    slab, cols = value.shape[0] // 4, value.shape[1] // count
    return call(
        functools.partial(unpack_columns_kernel, cols),
        name,
        [((slab, 4 * cols), f32)] * count,
        [value],
        [VMEM_SPEC],
        0,
    )


def unpack_two_kernel(in_ref, first_ref, second_ref):
    slab = first_ref.shape[0]
    wide, cols = first_ref.shape[1] // 4, second_ref.shape[1] // 4
    for i in range(4):
        rows = slice(i * slab, (i + 1) * slab)
        first_ref[:, i * wide : (i + 1) * wide] = in_ref[rows, :wide].astype(f32)
        second_ref[:, i * cols : (i + 1) * cols] = in_ref[rows, wide:].astype(f32)


def unpack_two(value, wide, name):
    slab, cols = value.shape[0] // 4, value.shape[1] - wide
    return call(
        unpack_two_kernel,
        name,
        [((slab, 4 * wide), f32), ((slab, 4 * cols), f32)],
        [value],
        [VMEM_SPEC],
        0,
    )


def unpack_keys_kernel(member, in_ref, k_ref, v_ref, gain_ref):
    slab = k_ref.shape[0]
    gains = jnp.zeros((2, LANES), f32)
    keys, values = [], []
    for i in range(4):
        at = i * (slab + GAIN_ROWS)
        kv = in_ref[at : at + slab].astype(f32)
        keys.append(kv[:, :HD])
        values.append(kv[:, HD:])
        gains = gains + in_ref[at + slab : at + slab + GAIN_ROWS].astype(f32)[:2]
    k_ref[...] = jnp.concatenate(keys, axis=1)
    v_ref[...] = jnp.concatenate(values, axis=1)
    halves = [gains[:, j * slab : (j + 1) * slab] for j in range(2)]
    gain_ref[...] = jnp.where(member[0] == 0, halves[0], halves[1])


def unpack_keys(side, value):
    slab = value.shape[0] // 4 - GAIN_ROWS
    return call(
        unpack_keys_kernel,
        "unpack_keys",
        [((slab, 4 * HD), f32), ((slab, 4 * HD), f32), ((2, slab), f32)],
        [side, value],
        [SMEM_SPEC, VMEM_SPEC],
        0,
    )


def run_at(starts, j):
    start = starts[j]
    return pl.ds(start if isinstance(start, int) else pl.multiple_of(start, LANES), LANES)


def run_of(j):
    return slice(j * LANES, (j + 1) * LANES)


def sum_of(refs, columns=slice(None)):
    total = refs[0][:, columns].astype(f32)
    for ref in refs[1:]:
        total = total + ref[:, columns].astype(f32)
    return total


def middle_kernel(starts, tok_ref, gain_ref, *rest):
    parts, (mid_ref, h_ref) = rest[:4], rest[4:]
    middle = tok_ref[...].astype(f32) + sum_of(parts)
    mid_ref[...] = middle
    inverse = inverse_rms(middle)
    for j in range(tok_ref.shape[1] // LANES):
        run = run_at(starts, j)
        h_ref[:, run_of(j)] = (mid_ref[:, run] * inverse * gain_ref[:, run]).astype(bf16)


def middle_norm(starts, tokens, gain, parts):
    return call(
        middle_kernel,
        "middle_norm",
        [(tokens.shape, f32), (tokens.shape, bf16)],
        [starts, tokens, gain] + parts,
        [SMEM_SPEC] + [VMEM_SPEC] * 6,
        0,
    )


def arrange_kernel(starts, in_ref, out_ref):
    for j in range(in_ref.shape[1] // LANES):
        out_ref[:, run_of(j)] = in_ref[:, run_at(starts, j)]


def arrange(starts, value):
    return call(
        arrange_kernel,
        "arrange",
        [(value.shape, bf16)],
        [starts, value],
        [SMEM_SPEC, VMEM_SPEC],
        0,
    )[0]


def block_kernel(starts, mid_ref, part_ref, out_ref):
    rows = mid_ref.shape[0]
    parts = [part_ref.at[pl.ds(r * rows, rows)] for r in range(4)]
    for j in range(mid_ref.shape[1] // LANES):
        where = run_at(starts, j)
        out_ref[:, where] = (mid_ref[:, where] + sum_of(parts, run_of(j))).astype(bf16)


def block_output(starts, middle, parts):
    return call(
        block_kernel,
        "block_output",
        [(middle.shape, bf16)],
        [starts, middle, parts],
        [SMEM_SPEC, VMEM_SPEC, VMEM_SPEC],
        0,
    )[0]


def norm_back_kernel(starts, mid_ref, grad_ref, gain_ref, *rest):
    parts, (d_ref, low_ref, term_ref) = rest[:4], rest[4:]
    middle = mid_ref[...]
    inverse = inverse_rms(middle)
    for j in range(mid_ref.shape[1] // LANES):
        d_ref[:, run_at(starts, j)] = sum_of(parts, run_of(j))
    grad = d_ref[...]
    normed = middle * inverse
    term_ref[...] = jnp.sum(grad * normed, axis=0, keepdims=True)
    scaled = grad * gain_ref[...]
    mean = jnp.mean(scaled * normed, axis=-1, keepdims=True)
    d_middle = grad_ref[...].astype(f32) + inverse * (scaled - normed * mean)
    d_ref[...] = d_middle
    low_ref[...] = d_middle.astype(bf16)


def norm_back(starts, middle, out_grad, gain, parts):
    return call(
        norm_back_kernel,
        "norm_back",
        [(middle.shape, f32), (middle.shape, bf16), ((1, middle.shape[1]), f32)],
        [starts, middle, out_grad, gain] + parts,
        [SMEM_SPEC] + [VMEM_SPEC] * 7,
        0,
    )


def query_grad_kernel(count, starts, h_ref, d_ref, own_ref, other_ref):
    for ref, first in ((other_ref, count // 2), (own_ref, 0)):
        for k in range(count // 2):
            ref[k] = dot_first(columns_of(h_ref, starts, first + k), d_ref[...]).astype(bf16)


def query_grads(starts, h, d, count):
    half = (count // 2, 2 * LANES, d.shape[1])
    return call(
        functools.partial(query_grad_kernel, count),
        "query_grads",
        [(half, bf16), (half, bf16)],
        [starts, h, d],
        [SMEM_SPEC] + [VMEM_SPEC] * 2,
        2 * h.shape[0] * h.shape[1] * d.shape[1],
    )


def key_grad_kernel(count, starts, h_ref, d_ref, ga_ref, gf_ref, own_ref, other_ref):
    row = lax.broadcasted_iota(jnp.int32, (GAIN_ROWS, LANES), 0)
    slab = own_ref.shape[1] // 4 - GAIN_ROWS
    for ref, first in ((other_ref, count // 2), (own_ref, 0)):
        for k in range(count // 2):
            grad = dot_first(columns_of(h_ref, starts, first + k), d_ref[...]).astype(bf16)
            for i in range(4):
                where = run_at(starts, 2 * (first + k) + i // 2)
                gains = jnp.where(row == 0, ga_ref[:, where], gf_ref[:, where])
                at = i * (slab + GAIN_ROWS)
                ref[k, at : at + slab] = grad[i * slab : (i + 1) * slab]
                ref[k, at + slab : at + slab + GAIN_ROWS] = jnp.where(row < 2, gains, 0.0).astype(
                    bf16
                )


def key_grads(starts, h, d, gain_a, gain_f, count, slab):
    half = (count // 2, 4 * (slab + GAIN_ROWS), 2 * HD)
    return call(
        functools.partial(key_grad_kernel, count),
        "key_grads",
        [(half, bf16), (half, bf16)],
        [starts, h, d, gain_a, gain_f],
        [SMEM_SPEC] + [VMEM_SPEC] * 4,
        4 * h.shape[0] * h.shape[1] * HD,
    )


def weight_rows(piece):
    slab = piece.shape[0] // 4 - GAIN_ROWS
    at = [i * (slab + GAIN_ROWS) for i in range(4)]
    return jnp.concatenate([piece[a : a + slab] for a in at], axis=0)


def project_kernel(count, rows, starts, cos_ref, sin_ref, *rest):
    toks, pieces = rest[:4], rest[4 : 4 + count]
    h_ref, q_ref, kv_ref, gain_ref = rest[4 + count :]
    stride = pieces[0].shape[0] // 4
    for k in range(count):
        for z in (0, 1):
            gains = None
            for x in (0, 1):
                at = (2 * z + x + 1) * stride - GAIN_ROWS
                part = pieces[k][at : at + GAIN_ROWS, :LANES].astype(f32)
                gains = part if gains is None else gains + part
            gain_ref[:, run_at(starts, 2 * k + z)] = gains[:8]

    for r, tok_ref in enumerate(toks):
        wide = tok_ref[...].astype(f32)
        h_ref[r * rows : (r + 1) * rows] = (wide * inverse_rms(wide) * gain_ref[:1]).astype(bf16)
    total = None
    for k in range(count):
        product = dot(columns_of(h_ref, starts, k), weight_rows(pieces[k]))
        total = product if total is None else total + product
    turned = total.astype(bf16).astype(f32).T
    cosine, sine = cos_ref[...], sin_ref[...]
    for head in range(HEADS):
        q = rotate(turned[head * HD : (head + 1) * HD], cosine, sine).astype(bf16)
        at = head % PER_CHUNK * rows
        for r in range(4):
            q_ref[r, head // PER_CHUNK, :HD, at : at + rows] = q[:, r * rows : (r + 1) * rows]
    q_ref[:, :, HD:, :] = jnp.zeros((4, CHUNKS, HD, PER_CHUNK * rows), bf16)
    kv_ref[:HD] = rotate(turned[Q_COLS : Q_COLS + HD], cosine, sine).astype(bf16)
    kv_ref[HD:] = turned[Q_COLS + HD :].astype(bf16)


def project(starts, toks, cosine, sine, pieces):
    rows, width = toks[0].shape
    tok = 4 * rows
    count = len(pieces)
    return call(
        functools.partial(project_kernel, count, rows),
        "project",
        [
            ((tok, width), bf16),
            ((4, CHUNKS, 2 * HD, PER_CHUNK * rows), bf16),
            ((2 * HD, tok), bf16),
            ((8, width), f32),
        ],
        [starts, cosine, sine] + toks + pieces,
        [SMEM_SPEC] + [VMEM_SPEC] * (6 + count),
        2 * tok * width * QKV_COLS,
    )


def out_kernel(rows, places, attn_a_ref, attn_b_ref, *rest):
    pieces, parts, (attn_t_ref, w_ref) = rest[:-6], rest[-6:-2], rest[-2:]
    count = places.shape[0] // 2
    slab = pieces[0].shape[0] // count
    for k in range(2 * count):
        piece = pieces[k // count][k % count * slab : (k % count + 1) * slab, :]
        w_ref[pl.ds(pl.multiple_of(places[k], slab), slab), :] = piece
    for head in range(HEADS):
        at = head % PER_CHUNK * rows
        for r in range(4):
            block = (attn_a_ref, attn_b_ref)[r % 2][r // 2, head // PER_CHUNK, :, at : at + rows]
            attn_t_ref[head * HD : (head + 1) * HD, r * rows : (r + 1) * rows] = block.astype(bf16)
    step = 512
    for c in range(0, w_ref.shape[1], step):
        part = dot_first(attn_t_ref[...], w_ref[:, c : c + step]).astype(bf16)
        for r in range(4):
            parts[r][:, c : c + step] = part[r * rows : (r + 1) * rows]


def out_products(places, attn, pieces, rows):
    width = pieces[0].shape[1]
    tok = 4 * rows
    return call(
        functools.partial(out_kernel, rows),
        "out_products",
        [((rows, width), bf16)] * 4 + [((Q_COLS, tok), bf16), ((Q_COLS, width), bf16)],
        [places] + attn + pieces,
        [SMEM_SPEC] + [VMEM_SPEC] * (2 + len(pieces)),
        2 * tok * width * Q_COLS,
    )


def out_back_kernel(rows, w_ref, attn_a_ref, attn_b_ref, *rest):
    parts, (g_ref, delta_ref, d_ref) = rest[:4], rest[4:]
    for r in range(4):
        d_ref[r * rows : (r + 1) * rows] = parts[r][...]
    turned = dot_last(w_ref[...], d_ref[...]).astype(bf16)
    g_ref[:, :, :HD, :] = jnp.zeros((4, CHUNKS, HD, PER_CHUNK * rows), bf16)
    for head in range(HEADS):
        at = head % PER_CHUNK * rows
        chunk = head // PER_CHUNK
        for r in range(4):
            g = turned[head * HD : (head + 1) * HD, r * rows : (r + 1) * rows]
            g_ref[r, chunk, HD:, at : at + rows] = g
            attn = (attn_a_ref, attn_b_ref)[r % 2][r // 2, chunk, :, at : at + rows]
            delta = jnp.sum(g.astype(f32) * attn, axis=0, keepdims=True)
            delta_ref[r, chunk, :, at : at + rows] = delta


def out_back(w, attn, parts):
    rows, width = parts[0].shape
    return call(
        functools.partial(out_back_kernel, rows),
        "out_back",
        [
            ((4, CHUNKS, 2 * HD, PER_CHUNK * rows), bf16),
            ((4, CHUNKS, 1, PER_CHUNK * rows), f32),
        ],
        [w] + attn + parts,
        [VMEM_SPEC] * 7,
        8 * rows * width * Q_COLS,
        [pltpu.VMEM((4 * rows, width), bf16)],
    )


def out_grad_kernel(places, attn_t_ref, *rest):
    parts, (own_ref, other_ref, whole_ref, d_ref) = rest[:4], rest[4:]
    rows = parts[0].shape[0]
    for r in range(4):
        d_ref[r * rows : (r + 1) * rows] = parts[r][...]
    whole_ref[...] = dot(attn_t_ref[...], d_ref[...])
    half, slab = own_ref.shape[0], own_ref.shape[1]
    for k in range(half):
        for ref, place in ((own_ref, places[k]), (other_ref, places[half + k])):
            ref[k] = whole_ref[pl.ds(pl.multiple_of(place, slab), slab), :].astype(bf16)


def out_grads(places, attn_t, parts, slab):
    rows, width = parts[0].shape
    half = (places.shape[0] // 2, slab, width)
    return call(
        out_grad_kernel,
        "out_grads",
        [(half, bf16), (half, bf16)],
        [places, attn_t] + parts,
        [SMEM_SPEC] + [VMEM_SPEC] * 5,
        8 * rows * width * Q_COLS,
        [pltpu.VMEM((Q_COLS, width), f32), pltpu.VMEM((4 * rows, width), bf16)],
    )


def back_query_kernel(rows, dq0_ref, dq1_ref, cos_ref, sin_ref, d_ref, turned_ref):
    cosine, sine = cos_ref[...], sin_ref[...]
    for head in range(HEADS):
        at = head % PER_CHUNK * rows
        blocks = [
            (dq0_ref, dq1_ref)[r % 2][r // 2, head // PER_CHUNK, :, at : at + rows]
            for r in range(4)
        ]
        dq = jnp.concatenate(blocks, axis=1) * score_scale
        turned_ref[head * HD : (head + 1) * HD] = unrotate(dq, cosine, sine)
    d_ref[...] = turned_ref[...].T.astype(bf16)


def back_query(dq0, dq1, cosine, sine, rows):
    return call(
        functools.partial(back_query_kernel, rows),
        "back_query",
        [((4 * rows, Q_COLS), bf16)],
        [dq0, dq1, cosine, sine],
        [VMEM_SPEC] * 4,
        0,
        [pltpu.VMEM((Q_COLS, 4 * rows), f32)],
    )[0]


def back_project_kernel(count, rows, starts, dq_ref, kv_ref, cos_ref, sin_ref, *rest):
    toks, pieces, parts = rest[:4], rest[4 : 4 + count], rest[4 + count : 8 + count]
    d_ref, gain_ref, both_ref, inv_ref = rest[8 + count :]
    kv = kv_ref[...].T
    dk = unrotate(kv[:HD] * score_scale, cos_ref[...], sin_ref[...])
    d_ref[...] = jnp.concatenate([dk, kv[HD:]], axis=0).T.astype(bf16)
    both_ref[:, :Q_COLS] = dq_ref[...]
    both_ref[:, Q_COLS:] = d_ref[...]
    for r, tok_ref in enumerate(toks):
        inverse = inverse_rms(tok_ref[...].astype(f32))
        inv_ref[r * rows : (r + 1) * rows] = jnp.broadcast_to(inverse, (rows, LANES))
    for k in range(count):
        product = dot_last(both_ref[...], weight_rows(pieces[k]))
        for z in (0, 1):
            where = run_at(starts, 2 * k + z)
            term = None
            for r in range(4):
                at = slice(r * rows, (r + 1) * rows)
                value = product[at, run_of(z)]
                parts[r][:, where] = value.astype(bf16)
                normed = toks[r][:, where].astype(f32) * inv_ref[at]
                here = jnp.sum(value * normed, axis=0, keepdims=True)
                term = here if term is None else term + here
            gain_ref[:, where] = term


def back_project(starts, dq, kv_sum, cosine, sine, toks, pieces):
    rows, width = toks[0].shape
    tok = 4 * rows
    count = len(pieces)
    return call(
        functools.partial(back_project_kernel, count, rows),
        "back_project",
        [((rows, width), bf16)] * 4 + [((tok, 2 * HD), bf16), ((1, width), f32)],
        [starts, dq, kv_sum, cosine, sine] + toks + pieces,
        [SMEM_SPEC] + [VMEM_SPEC] * (8 + count),
        2 * tok * width * QKV_COLS,
        [pltpu.VMEM((tok, QKV_COLS), bf16), pltpu.VMEM((tok, LANES), f32)],
    )


def rows_of(tile):
    return pl.ds(pl.multiple_of(tile * KEY_TILE, KEY_TILE), KEY_TILE)


def causal(position, rows, columns):
    shape = (KEY_TILE, columns)
    key = lax.broadcasted_iota(jnp.int32, shape, 0)
    row = lax.broadcasted_iota(jnp.int32, shape, 1) % rows
    return key <= row + position % (KEY_TILE // rows) * rows


def fill_keys(place, rows, core, chip, own, all_ref, kvt_ref, kv_ref):
    per_tile = KEY_TILE // rows
    for p, (at, core_bit, member) in enumerate(place):
        where = pl.ds(pl.multiple_of((member ^ own) * rows, rows), rows)
        block = all_ref[core_bit ^ core, at ^ chip, :, where]
        kvt_ref[p // per_tile, :, p % per_tile * rows : (p % per_tile + 1) * rows] = block
        kv_ref[p * rows : (p + 1) * rows, :] = block.T


def forward_kernel(
    offsets, picks, place, rows, me_ref, q_ref, all_ref, o_ref, log_ref, kv_ref, kvt_ref, vt_ref
):
    me, core, chip, own = me_ref[0], me_ref[1], me_ref[2], me_ref[3]
    chunks = q_ref.shape[1]
    fill_keys(place, rows, core, chip, own, all_ref, kvt_ref, kv_ref)
    vt_ref[:, :ONES] = jnp.ones((vt_ref.shape[0], ONES, KEY_TILE), bf16)
    vt_ref[:, ONES:] = kvt_ref[:, HD:]
    for i, (pick, offset) in enumerate(zip(picks, offsets)):
        position = me ^ offset
        last = position // (KEY_TILE // rows)

        def scores(tile):
            kv = kv_ref[rows_of(tile), :]
            return [dot(kv, q_ref[pick, c]) for c in range(chunks)], vt_ref[tile]

        keep = causal(position, rows, q_ref.shape[3])
        found, vt = scores(last)
        state = []
        for s in found:
            s = jnp.where(keep, s, masked_value)
            top = jnp.max(s, axis=0, keepdims=True)
            state.append((top, dot(vt, jnp.exp2((s - top) * to_log2).astype(bf16))))

        def turn(kt, state):
            found, vt = scores(kt)
            out = []
            for s, (top, total) in zip(found, state):
                new_top = jnp.maximum(top, jnp.max(s, axis=0, keepdims=True))
                p = jnp.exp2((s - new_top) * to_log2).astype(bf16)
                out.append((new_top, total * jnp.exp2((top - new_top) * to_log2) + dot(vt, p)))
            return tuple(out)

        state = lax.fori_loop(0, last, turn, tuple(state))
        for c, (top, total) in enumerate(state):
            weight = total[:1]
            o_ref[i, c] = total[ONES:] / weight
            log_ref[i, c] = top * to_log2 + jnp.log2(weight)


def backward_kernel(offsets, picks, place, rows, core_mask, first, *refs):
    me_ref, q_ref, g_ref, all_ref, log_ref, delta_ref = refs[:6]
    kv_ref, kvt_ref = refs[-2:]
    if first:
        dq_ref, dkv_ref = refs[6:8]
        dkv_ref[...] = jnp.zeros_like(dkv_ref)
    else:
        begun_ref, dq_ref, own_ref, other_ref, dkv_ref = refs[6:11]
        dkv_ref[...] = begun_ref[...]
    me, core, chip, own = me_ref[0], me_ref[1], me_ref[2], me_ref[3]
    chunks = q_ref.shape[1]
    fill_keys(place, rows, core, chip, own, all_ref, kvt_ref, kv_ref)
    for i, (pick, offset) in enumerate(zip(picks, offsets)):
        position = me ^ offset
        last = position // (KEY_TILE // rows)

        def turn(tile, keep):
            kv = kv_ref[rows_of(tile), :]
            kvt = kvt_ref[tile]
            pairs = [(dot(kv, q_ref[pick, c]), dot(kv, g_ref[pick, c])) for c in range(chunks)]
            summed, out = None, []
            for c, (s, dp) in enumerate(pairs):
                p = jnp.exp2(s * to_log2 - log_ref[i, c])
                if keep is not None:
                    p = jnp.where(keep, p, 0.0)
                ds = (p * (dp - delta_ref[pick, c])).astype(bf16)
                part = dot_last(p.astype(bf16), g_ref[pick, c]) + dot_last(ds, q_ref[pick, c])
                summed = part if summed is None else summed + part
                out.append(dot(kvt, ds)[:HD])
            dkv_ref[rows_of(tile), :] += summed
            return tuple(out)

        dq = turn(last, causal(position, rows, q_ref.shape[3]))
        dq = lax.fori_loop(
            0, last, lambda tile, dq: tuple(a + b for a, b in zip(dq, turn(tile, None))), dq
        )
        for c in range(chunks):
            dq_ref[i, c] = dq[c]
    if not first:
        for p, (at, core_bit, member) in enumerate(place):
            if core_bit == 0:
                near = (p + core * core_mask) * rows
                far = (p + (1 - core) * core_mask) * rows
                where = pl.ds(pl.multiple_of((member ^ own) * rows, rows), rows)
                own_ref[at ^ chip, where] = dkv_ref[pl.ds(pl.multiple_of(near, rows), rows), :]
                other = dkv_ref[pl.ds(pl.multiple_of(far, rows), rows), :]
                other_ref[at ^ chip, where] = other.astype(bf16)


def attention_forward(me, q, kv_all, offsets, picks, place, rows):
    blocks, chunks, columns = len(picks), q.shape[1], q.shape[3]
    keys = len(place) * rows
    scores = blocks * chunks * columns * keys // 2
    return call(
        functools.partial(forward_kernel, offsets, picks, place, rows),
        "attention_forward",
        [((blocks, chunks, HD, columns), f32), ((blocks, chunks, 1, columns), f32)],
        [me, q, kv_all],
        [SMEM_SPEC, VMEM_SPEC, VMEM_SPEC],
        scores * 8 * HD,
        [
            pltpu.VMEM((keys, 2 * HD), bf16),
            pltpu.VMEM((keys // KEY_TILE, 2 * HD, KEY_TILE), bf16),
            pltpu.VMEM((keys // KEY_TILE, ONES + HD, KEY_TILE), bf16),
        ],
        scores,
    )


def attention_backward(
    me, q, g, kv_all, log_total, delta, dkv, offsets, picks, place, rows, core_mask
):
    chunks, columns = q.shape[1], q.shape[3]
    keys = len(place) * rows
    scores = len(picks) * chunks * columns * keys // 2
    shares = (kv_all.shape[1], kv_all.shape[3], 2 * HD)
    out = [((len(picks), chunks, HD, columns), f32)]
    scratch = [
        pltpu.VMEM((keys, 2 * HD), bf16),
        pltpu.VMEM((keys // KEY_TILE, 2 * HD, KEY_TILE), bf16),
    ]
    args = [me, q, g, kv_all, log_total, delta]
    if dkv is None:
        out = out + [((keys, 2 * HD), f32)]
    else:
        out = out + [(shares, f32), (shares, bf16)]
        scratch = [pltpu.VMEM((keys, 2 * HD), f32)] + scratch
        args = args + [dkv]
    return call(
        functools.partial(backward_kernel, offsets, picks, place, rows, core_mask, dkv is None),
        "attention_backward",
        out,
        args,
        [SMEM_SPEC] + [VMEM_SPEC] * (len(args) - 1),
        scores * 20 * HD,
        scratch,
        scores,
    )


def on_device(
    tokens, gain_attn, w_query, w_key, w_value, w_out, gain_ffn, w_gate, w_up, w_down, out_grad
):
    n_seq = lax.axis_size("seq")
    n_fsdp = lax.axis_size("fsdp")
    n = n_seq * n_fsdp
    me = lax.axis_index(AXES)
    rows, width = tokens.shape
    slab, hidden_width = w_gate.shape
    x_mask, z_mask, core = 1, 2 * n_fsdp, n_fsdp
    t_masks = [0, x_mask, z_mask, x_mask | z_mask]
    far = [n_fsdp << k for k in range(2, n_seq.bit_length() - 1)]
    near = [1 << k for k in range(1, n_fsdp.bit_length() - 1)]
    d_bits = far + near + [core]
    d_masks = [0]
    for bit in d_bits:
        d_masks = d_masks + [m | bit for m in d_masks]
    chips = d_masks[: len(d_masks) // 2]
    d_all = sum(d_bits)
    t_groups = [[b | m for m in t_masks] for b in sorted(d_masks)]

    def swap(value, mask):
        return lax.ppermute(value, AXES, [(i, i ^ mask) for i in range(n)])

    def trade(value, groups):
        return lax.all_to_all(
            value, AXES, split_axis=0, concat_axis=0, tiled=True, axis_index_groups=groups
        )

    def sum_blocks(value, count):
        value = value.reshape((count, -1) + value.shape[1:])
        total = value[0].astype(f32)
        for i in range(1, count):
            total = total + value[i].astype(f32)
        return total

    def spread(pieces, bits):
        pieces = dict(pieces)
        for bit in bits:
            pieces.update({m | bit: swap(v, bit) for m, v in list(pieces.items())})
        return pieces

    def beyond(pieces):
        return {m: v for m, v in pieces.items() if m}

    def joined(own, relayed):
        pieces = {**own, **relayed}
        half = [pieces[m] for m in chips]
        return half + [swap(p, core) for p in half]

    def sum_over(total, bits, after=None):
        for bit in reversed(bits):
            half = total.shape[0] // 2
            got = swap(total[half:].astype(bf16), bit)
            if after is not None:
                got = hold(got, after)
            total = total[:half].astype(f32) + got.astype(f32)
        return total

    def core_sum(pair):
        own, other = pair
        return own.astype(f32) + swap(other, core).astype(f32)

    unit = 2 * slab
    aligned = unit == LANES
    zs = jnp.array([0, z_mask], jnp.int32)
    relative = ((me & d_all) ^ jnp.array(d_masks, jnp.int32))[:, None] + zs[None, :]
    relative = (relative.reshape(-1) // 2 * unit).astype(jnp.int32)
    t = me % 2 + 2 * ((me // z_mask) % 2)
    fixed = [(m | z) // 2 * unit for m in sorted(d_masks) for z in (0, z_mask)]
    fixed = jnp.array(fixed, jnp.int32)
    d_groups = [[b | m for m in sorted(d_masks)] for b in t_masks]
    side = (me % 2).reshape(1).astype(jnp.int32)

    def arranged(value, where):
        return value.reshape(value.shape[0], -1, unit)[:, where // unit].reshape(value.shape)

    def restored(value, where):
        runs = value.reshape(value.shape[0], -1, unit)
        return jnp.zeros_like(runs).at[:, where // unit].set(runs).reshape(value.shape)

    if aligned:
        starts, n_pieces = relative, len(d_masks)
    else:
        starts, n_pieces = jnp.arange(0, width, LANES, dtype=jnp.int32), width // (2 * LANES)

    def copies(value, count):
        shape = (count,) + value.shape
        return jnp.broadcast_to(value[None], shape).reshape((-1,) + value.shape[1:])

    def gather_t(value):
        return [value] + [swap(value, m) for m in t_masks[1:]]

    def relay_t(value):
        along = swap(value, z_mask)
        return [value, swap(value, x_mask), along, swap(along, x_mask)]

    def scatter_t(parts):
        return [parts[0]] + [swap(p, m) for p, m in zip(parts[1:], t_masks[1:])]

    def blocks_of(value):
        return [value[r * rows : (r + 1) * rows] for r in range(4)]

    def send(total, bits):
        total = sum_over(total, bits[1:])
        half = total.shape[0] // 2
        return total[:half].astype(f32), swap(total[half:].astype(bf16), bits[0])

    def give_back(total):
        return trade(total.reshape(4 * slab, -1).astype(bf16), t_groups)

    def by_member(value):
        size = value.shape[0] // 4
        parts = [lax.dynamic_slice_in_dim(value, (t ^ r) * size, size, 0) for r in range(4)]
        return jnp.concatenate(parts, axis=0)

    qkv_shard = trade(pack_attention(side, w_query, w_key, w_value, gain_attn, gain_ffn), t_groups)
    cols = hidden_width // 4
    qkv_far = spread({0: qkv_shard}, far)
    qkv_own = spread({0: qkv_shard}, near)
    near_tokens = hold(tokens, qkv_shard)
    toks = [tokens] + [swap(near_tokens, m) for m in t_masks[1:3]]
    toks = toks + [swap(hold(tokens, qkv_far, qkv_own), t_masks[3])]
    qkv_w = joined(qkv_own, spread(beyond(qkv_far), near))
    if aligned:
        qkv_k = qkv_w
    else:
        parts = jnp.stack(qkv_w).reshape(-1, 2, 2, slab + GAIN_ROWS, QKV_COLS)
        runs = parts[:, :, :, :slab].reshape(-1, unit, QKV_COLS)
        whole = jnp.zeros_like(runs).at[relative // unit].set(runs).reshape(-1, 4, 64, QKV_COLS)
        gains = jnp.stack(
            [parts[:, :, x, slab:, x * slab : (x + 1) * slab] for x in (0, 1)], axis=3
        ).reshape(-1, GAIN_ROWS, unit)
        gains = jnp.zeros_like(gains).at[relative // unit].set(gains)
        gains = jnp.moveaxis(gains, 1, 0).reshape(GAIN_ROWS, -1, 2, 64)
        gains = jnp.moveaxis(gains, 0, 2)
        lane = jnp.arange(QKV_COLS) // 64
        extra = jnp.where(
            lane[None, None, None] == jnp.arange(2)[None, :, None, None],
            jnp.tile(gains, (1, 1, 1, QKV_COLS // 64)),
            jnp.zeros((), bf16),
        ).reshape(-1, 4, GAIN_ROWS, QKV_COLS)
        whole = jnp.concatenate([whole, extra], axis=2).reshape(n_pieces, -1, QKV_COLS)
        qkv_k = [whole[i] for i in range(n_pieces)]

    bits = n.bit_length() - 1
    source = {z_mask.bit_length() - 1: bits - 1, 0: bits - 2}
    free = list(range(bits - 2))
    open_places = [b for b in range(bits) if b not in source]
    for b in list(open_places):
        if b in free:
            source[b] = b
            free.remove(b)
            open_places.remove(b)
    source.update(zip(open_places, free))

    def goes_to(i):
        return sum(((i >> s) & 1) << b for b, s in source.items())

    def came_from(i):
        return sum(((i >> b) & 1) << s for b, s in source.items())

    per_group = n // 4
    out_shard = lax.ppermute(hold(w_out, qkv_shard), AXES, [(i, goes_to(i)) for i in range(n)])
    my_row = came_from(me) % per_group
    out_places = jnp.array([came_from(m) % per_group for m in d_masks], jnp.int32)
    out_places = ((my_row ^ out_places) * slab).astype(jnp.int32)

    out_shard = hold(out_shard, qkv_far)
    out_far = spread({0: out_shard}, far)
    out_own = spread({0: out_shard}, near)
    qkv_k, toks, out_far, out_own = lax.optimization_barrier((qkv_k, toks, out_far, out_own))
    out_all = {**out_own, **spread(beyond(out_far), near)}
    blocks = me ^ jnp.array(t_masks, jnp.int32)
    positions = (blocks[:, None] * rows + jnp.arange(rows, dtype=jnp.int32)).reshape(-1)
    cosine, sine = rope_tables(positions)
    h_attn, q, kv, gains = project(starts, toks, cosine, sine, qkv_k)
    gain_a, gain_f = gains[0:1], gains[1:2]
    pair_shard = trade(hold(pack_columns([w_gate, w_up], "pack_gate_up"), kv), t_groups)
    kv_parts = [kv] + [swap(kv, m) for m in chips[1:]]
    kv_parts, pair_shard, out_all = lax.optimization_barrier((kv_parts, pair_shard, out_all))
    kv = jnp.stack(kv_parts)
    kv_all = jnp.stack([kv, swap(kv, core)])
    place = [
        (
            chips.index(p & sum(far + near)),
            1 if p & core else 0,
            t_masks.index(p & (x_mask | z_mask)),
        )
        for p in range(n)
    ]
    my_chip = sum(((me // bit) % 2) << i for i, bit in enumerate(far + near))
    me_ref = jnp.stack([me, (me // core) % 2, my_chip, t]).astype(jnp.int32)

    pair_w = lax.all_gather(pair_shard, AXES, axis=0, tiled=True, axis_index_groups=d_groups)
    out_half = jnp.concatenate([out_all[m] for m in chips], axis=0)
    out_pieces = [out_half, swap(hold(out_half, kv_all), core)]
    down_shard = trade(pack_columns([hold(w_down, kv_all)], "pack_down"), t_groups)
    g4 = arrange(relative, out_grad) if aligned else arranged(out_grad, relative)

    def forward(x, q):
        return attention_forward(
            me_ref, q, kv_all, [x * x_mask, z_mask + x * x_mask], [x, 2 + x], place, rows
        )

    def backward(x, dkv):
        return attention_backward(
            me_ref,
            q,
            d_heads,
            kv_all,
            log_totals[x],
            delta,
            dkv,
            [x * x_mask, z_mask + x * x_mask],
            [x, 2 + x],
            place,
            rows,
            core,
        )

    attn_a, log_a = forward(0, q)
    attn_a, q_b, out_pieces, down_shard = lax.optimization_barrier(
        (attn_a, q, out_pieces, down_shard)
    )
    down_own = spread({0: hold(down_shard, attn_a)}, near)
    g = trade(copies(hold(g4, attn_a), 4), t_groups)
    attn_b, log_b = forward(1, q_b)
    attn, log_totals = [attn_a, attn_b], [log_a, log_b]
    *middle_parts, attn_t, out_w = out_products(out_places, attn, out_pieces, rows)
    middle_parts = scatter_t(middle_parts)

    def halves(pieces):
        half = jnp.concatenate([pieces[m] for m in chips], axis=0)
        return [half, swap(half, core)]

    middle_parts, down_own, g = lax.optimization_barrier((middle_parts, down_own, g))
    down_far = spread({0: hold(down_shard, middle_parts)}, far)
    g = by_member(hold(g, middle_parts))

    if aligned:
        middle, h = middle_norm(fixed, tokens, gain_f, middle_parts)
    else:
        middle = tokens.astype(f32) + sum([p.astype(f32) for p in middle_parts])
        h = arranged((middle * inverse_rms(middle) * gain_f).astype(bf16), fixed)
    h_parts = gather_t(h)
    h_parts, g = lax.optimization_barrier((h_parts, g))
    down_all = {**down_own, **spread(hold(beyond(down_far), h_parts), near)}
    h_ffn = jnp.concatenate(h_parts, axis=0)
    half_width = width // 2

    def by_halves(left, w):
        return dot(left[:, :half_width], w[0]) + dot(left[:, half_width:], w[1])

    down_w = halves(down_all)
    pair = dot(h_ffn, pair_w)
    gate, up = pair[:, :cols], pair[:, cols:]
    sig = jax.nn.sigmoid(gate)
    act = gate * sig
    hidden = (act * up).astype(bf16)
    d_hidden = by_halves(g, down_w)
    d_gate = (d_hidden * up * sig * (1.0 + gate * (1.0 - sig))).astype(bf16)
    d_up = (d_hidden * act).astype(bf16)
    d_pair = jnp.concatenate([d_gate, d_up], axis=1)
    d_hffn_part = dot_last(d_pair, pair_w).astype(bf16)
    d_hffn_blocks = blocks_of(d_hffn_part)
    d_hffn_parts = scatter_t(d_hffn_blocks)

    def weight_grad(left, right):
        other = dot_first(left[:, half_width:], right).astype(bf16)
        return dot_first(left[:, :half_width], right) + swap(other, core).astype(f32)

    pair_grad = dot_first(hold(h_ffn, d_hffn_blocks), d_pair).astype(bf16)
    pair_total = lax.psum_scatter(
        pair_grad, AXES, scatter_dimension=0, tiled=True, axis_index_groups=d_groups
    )
    block_part = jnp.concatenate(
        [dot_last(hold(hidden, pair_grad), w).astype(bf16) for w in down_w], axis=1
    )
    d_hffn_parts, pair_grad, block_part = lax.optimization_barrier(
        (d_hffn_parts, pair_grad, block_part)
    )
    down_sum = weight_grad(hold(g, d_hffn_parts), hidden)
    block_blocks = by_member(hold(block_part, d_hffn_parts))

    if aligned:
        d_middle, d_low, gain_ffn_term = norm_back(fixed, middle, out_grad, gain_f, d_hffn_parts)
    else:
        d_hffn = restored(sum([p.astype(f32) for p in d_hffn_parts]), fixed)
        inverse = inverse_rms(middle)
        normed = middle * inverse
        scaled = d_hffn * gain_f
        gain_ffn_term = jnp.sum(d_hffn * normed, axis=0, keepdims=True)
        d_middle = out_grad.astype(f32) + inverse * (
            scaled - normed * jnp.mean(scaled * normed, axis=-1, keepdims=True)
        )
        d_low = d_middle.astype(bf16)
    d_branch = relay_t(d_low)
    d_branch, down_sum, block_blocks = lax.optimization_barrier((d_branch, down_sum, block_blocks))
    d_heads, delta = out_back(out_w, attn, d_branch)

    block_parts = trade(hold(block_blocks, d_heads), t_groups)
    down_near = hold(down_sum, d_heads)
    for bit in reversed(near):
        half = down_near.shape[0] // 2
        down_got = swap(down_near[half:].astype(bf16), bit)
        down_near = down_near[:half].astype(f32)
        if bit != near[0]:
            down_near = down_near + down_got.astype(f32)
    out_pair = out_grads(out_places, attn_t, hold(d_branch, d_heads), slab)
    out_sum = core_sum(out_pair)
    dq0, dkv = backward(0, None)
    dkv, out_sum = lax.optimization_barrier((dkv, out_sum))
    out_keep, out_got = send(out_sum, near)
    dq1, own, other = backward(1, dkv)
    other, down_got, block_parts, out_got = lax.optimization_barrier(
        (other, down_got, block_parts, out_got)
    )
    kv_sums = own + swap(other, core).astype(f32)
    kv_sends = [kv_sums[i].astype(bf16) for i in range(len(chips))]
    kv_parts = [swap(kv_sends[i], m) for i, m in enumerate(chips) if m]
    dq0, dq1, block_parts, down_got, out_got, pair_total = hold(
        (dq0, dq1, block_parts, down_got, out_got, pair_total), kv_sends
    )
    d_query = back_query(dq0, dq1, cosine, sine, rows)
    if aligned:
        query_pair = query_grads(starts, h_attn, d_query, n_pieces)
    else:
        grads = dot_first(h_attn, d_query).astype(bf16).reshape(-1, unit, Q_COLS)
        grads = grads[relative // unit].reshape(len(d_masks), -1, Q_COLS)
        query_pair = grads[: len(chips)], grads[len(chips) :]
    query_sum = core_sum(query_pair)
    down_keep, down_got = send(down_near + down_got.astype(f32), far)
    pair_parts = trade(pair_total, t_groups)
    if aligned:
        block_out = block_output(relative, middle, block_parts)
    else:
        block_out = (middle + restored(sum_blocks(block_parts, 4), relative)).astype(bf16)
    kv_parts, query_sum, block_out = lax.optimization_barrier((kv_parts, query_sum, block_out))
    kv_sum = kv_sums[0]
    for part in kv_parts:
        kv_sum = kv_sum + part.astype(f32)
    query_keep, query_got = send(query_sum, near)
    out_keep, out_got = send(out_keep + out_got.astype(f32), far)
    *d_hattn_blocks, d_kv, gain_attn_part = back_project(
        starts, d_query, kv_sum, cosine, sine, toks, qkv_k
    )
    d_hattn_blocks, query_got = lax.optimization_barrier((d_hattn_blocks, query_got))
    query_keep, query_got = send(query_keep + query_got.astype(f32), far)
    d_hattn_parts = scatter_t(d_hattn_blocks)
    d_kv, gain_attn_part = hold((d_kv, gain_attn_part), d_hattn_blocks)
    if aligned:
        own, other = key_grads(starts, h_attn, d_kv, gain_attn_part, gain_ffn_term, n_pieces, slab)
    else:
        grads = dot_first(h_attn, d_kv).astype(bf16).reshape(-1, unit, 2 * HD)
        grads = grads[relative // unit].reshape(-1, 4, slab, 2 * HD)
        terms = jnp.concatenate([gain_attn_part, gain_ffn_term]).astype(bf16)
        terms = terms.reshape(2, -1, unit)[:, relative // unit].reshape(2, -1, 2, 1, unit)
        terms = jnp.moveaxis(jnp.broadcast_to(terms, terms.shape[:3] + (2, unit)), 0, 3)
        terms = terms.reshape(-1, 4, 2, unit)
        terms = jnp.pad(terms, ((0, 0), (0, 0), (0, GAIN_ROWS - 2), (0, 2 * HD - unit)))
        grads = jnp.concatenate([grads, terms], axis=2).reshape(len(d_masks), -1, 2 * HD)
        own, other = grads[: len(chips)], grads[len(chips) :]
    key_sum = core_sum((own, other))
    after = d_hattn_parts[1:]
    grad_gate, grad_up = unpack_columns(pair_parts, 2, "unpack_gate_up")
    key_sum, query_got, out_got, down_got = hold((key_sum, query_got, out_got, down_got), after)
    d_hattn_parts, grad_gate, grad_up = lax.optimization_barrier((d_hattn_parts, grad_gate, grad_up))
    query_total = query_keep + query_got.astype(f32)
    out_total = (out_keep + out_got.astype(f32)).astype(bf16).reshape(slab, width)
    down_total = down_keep + down_got.astype(f32)
    key_total = sum_over(sum_over(key_sum, near), far)
    grad_out_proj = lax.ppermute(out_total, AXES, [(goes_to(i), i) for i in range(n)]).astype(f32)
    merged = [v.reshape(4 * slab, -1).astype(bf16) for v in (query_total, down_total)]
    merged = trade(jnp.concatenate(merged, axis=1), t_groups)
    grad_query, grad_down = unpack_two(merged, Q_COLS, "unpack_query_down")
    key_parts = trade(key_total.reshape(-1, 2 * HD).astype(bf16), t_groups)
    grad_key, grad_value, gain_terms = unpack_keys(side, key_parts)

    own = tokens.astype(f32)
    inverse_attn = inverse_rms(own)
    normed_attn = own * inverse_attn
    d_hattn = d_hattn_parts[0].astype(f32)
    for part in d_hattn_parts[1:]:
        d_hattn = d_hattn + part.astype(f32)
    scaled = d_hattn * gain_a
    grad_tokens = d_middle + inverse_attn * (
        scaled - normed_attn * jnp.mean(scaled * normed_attn, axis=-1, keepdims=True)
    )
    return (
        block_out,
        grad_tokens,
        gain_terms[0],
        grad_query,
        grad_key,
        grad_value,
        grad_out_proj,
        gain_terms[1],
        grad_gate,
        grad_up,
        grad_down,
    )


def solution(mesh):
    spec2 = P(AXES, None)
    spec1 = P(AXES)
    return jax.shard_map(
        on_device,
        mesh=mesh,
        in_specs=(
            spec2,
            spec1,
            spec2,
            spec2,
            spec2,
            spec2,
            spec1,
            spec2,
            spec2,
            spec2,
            spec2,
        ),
        out_specs=(
            spec2,
            spec2,
            spec1,
            spec2,
            spec2,
            spec2,
            spec2,
            spec1,
            spec2,
            spec2,
            spec2,
        ),
        check_vma=False,
    )
```

```python
import functools
import math

import jax
import jax.numpy as jnp
from jax import lax
from jax.experimental import pallas as pl
from jax.experimental.pallas import tpu as pltpu
from jax.sharding import PartitionSpec as P

H = 32
KV = 4
HD = 64
AXES = ("seq", "fsdp")
norm_eps = 1e-05
rope_base = 10000.0
masked_value = -1e30
score_scale = HD ** (-0.5)
to_log2 = score_scale * math.log2(math.e)
bf16 = jnp.bfloat16
f32 = jnp.float32
KEY_TILE = 512
ONES = 16
LANES = 128
GAIN_ROWS = 16
CHUNKS = 2
HEADS = H // KV
PER_CHUNK = HEADS // CHUNKS
Q_COLS = HEADS * HD
QKV_COLS = Q_COLS + 2 * HD

SMEM_SPEC = pl.BlockSpec(memory_space=pltpu.SMEM)
VMEM_SPEC = pl.BlockSpec(memory_space=pltpu.VMEM)
ANY_SPEC = pl.BlockSpec(memory_space=pl.ANY)


def dot(a, b):
    return lax.dot_general(a, b, (((1,), (0,)), ((), ())), preferred_element_type=f32)


def dot_last(a, b):
    return lax.dot_general(a, b, (((1,), (1,)), ((), ())), preferred_element_type=f32)


def dot_first(a, b):
    return lax.dot_general(a, b, (((0,), (0,)), ((), ())), preferred_element_type=f32)


def inverse_rms(values):
    return lax.rsqrt(jnp.mean(values * values, axis=-1, keepdims=True) + norm_eps)


def rope_tables(positions):
    half = HD // 2
    frequency = rope_base ** (-(jnp.arange(half, dtype=f32) * 2.0) / HD)
    angles = positions.astype(f32)[None, :] * frequency[:, None]
    return (jnp.cos(angles), jnp.sin(angles))


def rotate(values, cosine, sine):
    a, b = values[: HD // 2], values[HD // 2 :]
    return jnp.concatenate([a * cosine - b * sine, b * cosine + a * sine], axis=0)


def unrotate(values, cosine, sine):
    a, b = values[: HD // 2], values[HD // 2 :]
    return jnp.concatenate([a * cosine + b * sine, b * cosine - a * sine], axis=0)


def hold(value, *others):
    return lax.optimization_barrier((value, others))[0]


def call(kernel, name, out, args, specs, flops, scratch=(), exps=0):
    out_shape = tuple(jax.ShapeDtypeStruct(s, d) for s, d in out)
    size = sum(a.size * a.dtype.itemsize for a in args)
    size += sum(math.prod(s.shape) * s.dtype.itemsize for s in out_shape)
    return pl.pallas_call(
        kernel,
        out_shape=out_shape,
        in_specs=specs,
        out_specs=(VMEM_SPEC,) * len(out_shape),
        scratch_shapes=list(scratch),
        compiler_params=pltpu.CompilerParams(vmem_limit_bytes=58 << 20),
        cost_estimate=pl.CostEstimate(flops=flops, bytes_accessed=size, transcendentals=exps),
        name=name,
    )(*args)


def columns_of(ref, starts, k):
    runs = [
        ref[:, pl.ds(pl.multiple_of(starts[2 * k + z], LANES), LANES)] for z in (0, 1)
    ]
    return jnp.concatenate(runs, axis=1)


def pack_kernel(member, q_ref, k_ref, v_ref, ga_ref, gf_ref, out_ref):
    slab = q_ref.shape[0]
    side = member[0]
    row = lax.broadcasted_iota(jnp.int32, (GAIN_ROWS, LANES), 0)
    lane = lax.broadcasted_iota(jnp.int32, (GAIN_ROWS, LANES), 1)
    gains = []
    for ref in (ga_ref, gf_ref):
        gains.append(jnp.concatenate([ref[...].astype(f32)] * (LANES // slab), axis=1))
    block = jnp.where(row == 0, gains[0], jnp.where(row == 1, gains[1], 0.0))
    block = jnp.where(lane // slab == side, block, 0.0).astype(bf16)
    block = jnp.concatenate([block, jnp.zeros((GAIN_ROWS, QKV_COLS - LANES), bf16)], axis=1)
    for i in range(4):
        at = i * (slab + GAIN_ROWS)
        out_ref[at : at + slab, :Q_COLS] = q_ref[:, i * Q_COLS : (i + 1) * Q_COLS]
        kv = [ref[:, i * HD : (i + 1) * HD] for ref in (k_ref, v_ref)]
        out_ref[at : at + slab, Q_COLS:] = jnp.concatenate(kv, axis=1)
        out_ref[at + slab : at + slab + GAIN_ROWS] = block


def pack_attention(side, w_query, w_key, w_value, gain_attn, gain_ffn):
    slab = w_query.shape[0]
    return call(
        pack_kernel,
        "pack_attention",
        [((4 * (slab + GAIN_ROWS), QKV_COLS), bf16)],
        [side, w_query, w_key, w_value, gain_attn.reshape(1, slab), gain_ffn.reshape(1, slab)],
        [SMEM_SPEC] + [VMEM_SPEC] * 5,
        0,
    )[0]


def pack_columns_kernel(cols, *refs):
    ins, out_ref = refs[:-1], refs[-1]
    slab = ins[0].shape[0]
    for i in range(4):
        for w, ref in enumerate(ins):
            out_ref[i * slab : (i + 1) * slab, w * cols : (w + 1) * cols] = ref[
                :, i * cols : (i + 1) * cols
            ]


def pack_columns(weights, name):
    slab, cols = weights[0].shape[0], weights[0].shape[1] // 4
    return call(
        functools.partial(pack_columns_kernel, cols),
        name,
        [((4 * slab, cols * len(weights)), bf16)],
        list(weights),
        [VMEM_SPEC] * len(weights),
        0,
    )[0]


def unpack_columns_kernel(cols, in_ref, *outs):
    slab = outs[0].shape[0]
    for i in range(4):
        for w, ref in enumerate(outs):
            ref[:, i * cols : (i + 1) * cols] = in_ref[
                i * slab : (i + 1) * slab, w * cols : (w + 1) * cols
            ].astype(f32)


def unpack_columns(value, count, name):
    slab, cols = value.shape[0] // 4, value.shape[1] // count
    return call(
        functools.partial(unpack_columns_kernel, cols),
        name,
        [((slab, 4 * cols), f32)] * count,
        [value],
        [VMEM_SPEC],
        0,
    )


def unpack_two_kernel(in_ref, first_ref, second_ref):
    slab = first_ref.shape[0]
    wide, cols = first_ref.shape[1] // 4, second_ref.shape[1] // 4
    for i in range(4):
        rows = slice(i * slab, (i + 1) * slab)
        first_ref[:, i * wide : (i + 1) * wide] = in_ref[rows, :wide].astype(f32)
        second_ref[:, i * cols : (i + 1) * cols] = in_ref[rows, wide:].astype(f32)


def unpack_two(value, wide, name):
    slab, cols = value.shape[0] // 4, value.shape[1] - wide
    return call(
        unpack_two_kernel,
        name,
        [((slab, 4 * wide), f32), ((slab, 4 * cols), f32)],
        [value],
        [VMEM_SPEC],
        0,
    )


def unpack_keys_kernel(member, in_ref, k_ref, v_ref, gain_ref):
    slab = k_ref.shape[0]
    gains = jnp.zeros((2, LANES), f32)
    keys, values = [], []
    for i in range(4):
        at = i * (slab + GAIN_ROWS)
        kv = in_ref[at : at + slab].astype(f32)
        keys.append(kv[:, :HD])
        values.append(kv[:, HD:])
        gains = gains + in_ref[at + slab : at + slab + GAIN_ROWS].astype(f32)[:2]
    k_ref[...] = jnp.concatenate(keys, axis=1)
    v_ref[...] = jnp.concatenate(values, axis=1)
    halves = [gains[:, j * slab : (j + 1) * slab] for j in range(2)]
    gain_ref[...] = jnp.where(member[0] == 0, halves[0], halves[1])


def unpack_keys(side, value):
    slab = value.shape[0] // 4 - GAIN_ROWS
    return call(
        unpack_keys_kernel,
        "unpack_keys",
        [((slab, 4 * HD), f32), ((slab, 4 * HD), f32), ((2, slab), f32)],
        [side, value],
        [SMEM_SPEC, VMEM_SPEC],
        0,
    )


def run_at(starts, j):
    start = starts[j]
    return pl.ds(start if isinstance(start, int) else pl.multiple_of(start, LANES), LANES)


def run_of(j):
    return slice(j * LANES, (j + 1) * LANES)


def sum_of(refs, columns=slice(None)):
    total = refs[0][:, columns].astype(f32)
    for ref in refs[1:]:
        total = total + ref[:, columns].astype(f32)
    return total


def middle_kernel(starts, tok_ref, gain_ref, *rest):
    parts, (mid_ref, h_ref) = rest[:4], rest[4:]
    middle = tok_ref[...].astype(f32) + sum_of(parts)
    mid_ref[...] = middle
    inverse = inverse_rms(middle)
    for j in range(tok_ref.shape[1] // LANES):
        run = run_at(starts, j)
        h_ref[:, run_of(j)] = (mid_ref[:, run] * inverse * gain_ref[:, run]).astype(bf16)


def middle_norm(starts, tokens, gain, parts):
    return call(
        middle_kernel,
        "middle_norm",
        [(tokens.shape, f32), (tokens.shape, bf16)],
        [starts, tokens, gain] + parts,
        [SMEM_SPEC] + [VMEM_SPEC] * 6,
        0,
    )


def arrange_kernel(starts, in_ref, out_ref):
    for j in range(in_ref.shape[1] // LANES):
        out_ref[:, run_of(j)] = in_ref[:, run_at(starts, j)]


def arrange(starts, value):
    return call(
        arrange_kernel,
        "arrange",
        [(value.shape, bf16)],
        [starts, value],
        [SMEM_SPEC, VMEM_SPEC],
        0,
    )[0]


def block_kernel(starts, mid_ref, part_ref, out_ref):
    rows = mid_ref.shape[0]
    parts = [part_ref.at[pl.ds(r * rows, rows)] for r in range(4)]
    for j in range(mid_ref.shape[1] // LANES):
        where = run_at(starts, j)
        out_ref[:, where] = (mid_ref[:, where] + sum_of(parts, run_of(j))).astype(bf16)


def block_output(starts, middle, parts):
    return call(
        block_kernel,
        "block_output",
        [(middle.shape, bf16)],
        [starts, middle, parts],
        [SMEM_SPEC, VMEM_SPEC, VMEM_SPEC],
        0,
    )[0]


def norm_back_kernel(starts, mid_ref, grad_ref, gain_ref, *rest):
    parts, (d_ref, low_ref, term_ref) = rest[:4], rest[4:]
    middle = mid_ref[...]
    inverse = inverse_rms(middle)
    for j in range(mid_ref.shape[1] // LANES):
        d_ref[:, run_at(starts, j)] = sum_of(parts, run_of(j))
    grad = d_ref[...]
    normed = middle * inverse
    term_ref[...] = jnp.sum(grad * normed, axis=0, keepdims=True)
    scaled = grad * gain_ref[...]
    mean = jnp.mean(scaled * normed, axis=-1, keepdims=True)
    d_middle = grad_ref[...].astype(f32) + inverse * (scaled - normed * mean)
    d_ref[...] = d_middle
    low_ref[...] = d_middle.astype(bf16)


def norm_back(starts, middle, out_grad, gain, parts):
    return call(
        norm_back_kernel,
        "norm_back",
        [(middle.shape, f32), (middle.shape, bf16), ((1, middle.shape[1]), f32)],
        [starts, middle, out_grad, gain] + parts,
        [SMEM_SPEC] + [VMEM_SPEC] * 7,
        0,
    )


def query_grad_kernel(count, starts, h_ref, d_ref, own_ref, other_ref):
    for ref, first in ((other_ref, count // 2), (own_ref, 0)):
        for k in range(count // 2):
            ref[k] = dot_first(columns_of(h_ref, starts, first + k), d_ref[...]).astype(bf16)


def query_grads(starts, h, d, count):
    half = (count // 2, 2 * LANES, d.shape[1])
    return call(
        functools.partial(query_grad_kernel, count),
        "query_grads",
        [(half, bf16), (half, bf16)],
        [starts, h, d],
        [SMEM_SPEC] + [VMEM_SPEC] * 2,
        2 * h.shape[0] * h.shape[1] * d.shape[1],
    )


def key_grad_kernel(count, starts, h_ref, d_ref, ga_ref, gf_ref, own_ref, other_ref):
    row = lax.broadcasted_iota(jnp.int32, (GAIN_ROWS, LANES), 0)
    slab = own_ref.shape[1] // 4 - GAIN_ROWS
    for ref, first in ((other_ref, count // 2), (own_ref, 0)):
        for k in range(count // 2):
            grad = dot_first(columns_of(h_ref, starts, first + k), d_ref[...]).astype(bf16)
            for i in range(4):
                where = run_at(starts, 2 * (first + k) + i // 2)
                gains = jnp.where(row == 0, ga_ref[:, where], gf_ref[:, where])
                at = i * (slab + GAIN_ROWS)
                ref[k, at : at + slab] = grad[i * slab : (i + 1) * slab]
                ref[k, at + slab : at + slab + GAIN_ROWS] = jnp.where(row < 2, gains, 0.0).astype(
                    bf16
                )


def key_grads(starts, h, d, gain_a, gain_f, count, slab):
    half = (count // 2, 4 * (slab + GAIN_ROWS), 2 * HD)
    return call(
        functools.partial(key_grad_kernel, count),
        "key_grads",
        [(half, bf16), (half, bf16)],
        [starts, h, d, gain_a, gain_f],
        [SMEM_SPEC] + [VMEM_SPEC] * 4,
        4 * h.shape[0] * h.shape[1] * HD,
    )


def weight_rows(piece):
    slab = piece.shape[0] // 4 - GAIN_ROWS
    at = [i * (slab + GAIN_ROWS) for i in range(4)]
    return jnp.concatenate([piece[a : a + slab] for a in at], axis=0)


def project_kernel(count, rows, starts, cos_ref, sin_ref, *rest):
    toks, pieces = rest[:4], rest[4 : 4 + count]
    h_ref, q_ref, kv_ref, gain_ref = rest[4 + count :]
    stride = pieces[0].shape[0] // 4
    for k in range(count):
        for z in (0, 1):
            gains = None
            for x in (0, 1):
                at = (2 * z + x + 1) * stride - GAIN_ROWS
                part = pieces[k][at : at + GAIN_ROWS, :LANES].astype(f32)
                gains = part if gains is None else gains + part
            gain_ref[:, run_at(starts, 2 * k + z)] = gains[:8]

    for r, tok_ref in enumerate(toks):
        wide = tok_ref[...].astype(f32)
        h_ref[r * rows : (r + 1) * rows] = (wide * inverse_rms(wide) * gain_ref[:1]).astype(bf16)
    total = None
    for k in range(count):
        product = dot(columns_of(h_ref, starts, k), weight_rows(pieces[k]))
        total = product if total is None else total + product
    turned = total.astype(bf16).astype(f32).T
    cosine, sine = cos_ref[...], sin_ref[...]
    for head in range(HEADS):
        q = rotate(turned[head * HD : (head + 1) * HD], cosine, sine).astype(bf16)
        at = head % PER_CHUNK * rows
        for r in range(4):
            q_ref[r, head // PER_CHUNK, :HD, at : at + rows] = q[:, r * rows : (r + 1) * rows]
    q_ref[:, :, HD:, :] = jnp.zeros((4, CHUNKS, HD, PER_CHUNK * rows), bf16)
    kv_ref[:HD] = rotate(turned[Q_COLS : Q_COLS + HD], cosine, sine).astype(bf16)
    kv_ref[HD:] = turned[Q_COLS + HD :].astype(bf16)


def project(starts, toks, cosine, sine, pieces):
    rows, width = toks[0].shape
    tok = 4 * rows
    count = len(pieces)
    return call(
        functools.partial(project_kernel, count, rows),
        "project",
        [
            ((tok, width), bf16),
            ((4, CHUNKS, 2 * HD, PER_CHUNK * rows), bf16),
            ((2 * HD, tok), bf16),
            ((8, width), f32),
        ],
        [starts, cosine, sine] + toks + pieces,
        [SMEM_SPEC] + [VMEM_SPEC] * (6 + count),
        2 * tok * width * QKV_COLS,
    )


def out_kernel(rows, places, attn_a_ref, attn_b_ref, *rest):
    pieces, parts, (attn_t_ref, w_ref) = rest[:-6], rest[-6:-2], rest[-2:]
    count = places.shape[0] // 2
    slab = pieces[0].shape[0] // count
    for k in range(2 * count):
        piece = pieces[k // count][k % count * slab : (k % count + 1) * slab, :]
        w_ref[pl.ds(pl.multiple_of(places[k], slab), slab), :] = piece
    for head in range(HEADS):
        at = head % PER_CHUNK * rows
        for r in range(4):
            block = (attn_a_ref, attn_b_ref)[r % 2][r // 2, head // PER_CHUNK, :, at : at + rows]
            attn_t_ref[head * HD : (head + 1) * HD, r * rows : (r + 1) * rows] = block.astype(bf16)
    step = 512
    for c in range(0, w_ref.shape[1], step):
        part = dot_first(attn_t_ref[...], w_ref[:, c : c + step]).astype(bf16)
        for r in range(4):
            parts[r][:, c : c + step] = part[r * rows : (r + 1) * rows]


def out_products(places, attn, pieces, rows):
    width = pieces[0].shape[1]
    tok = 4 * rows
    return call(
        functools.partial(out_kernel, rows),
        "out_products",
        [((rows, width), bf16)] * 4 + [((Q_COLS, tok), bf16), ((Q_COLS, width), bf16)],
        [places] + attn + pieces,
        [SMEM_SPEC] + [VMEM_SPEC] * (2 + len(pieces)),
        2 * tok * width * Q_COLS,
    )


def out_back_kernel(rows, w_ref, attn_a_ref, attn_b_ref, *rest):
    parts, (g_ref, delta_ref, d_ref) = rest[:4], rest[4:]
    for r in range(4):
        d_ref[r * rows : (r + 1) * rows] = parts[r][...]
    turned = dot_last(w_ref[...], d_ref[...]).astype(bf16)
    g_ref[:, :, :HD, :] = jnp.zeros((4, CHUNKS, HD, PER_CHUNK * rows), bf16)
    for head in range(HEADS):
        at = head % PER_CHUNK * rows
        chunk = head // PER_CHUNK
        for r in range(4):
            g = turned[head * HD : (head + 1) * HD, r * rows : (r + 1) * rows]
            g_ref[r, chunk, HD:, at : at + rows] = g
            attn = (attn_a_ref, attn_b_ref)[r % 2][r // 2, chunk, :, at : at + rows]
            delta = jnp.sum(g.astype(f32) * attn, axis=0, keepdims=True)
            delta_ref[r, chunk, :, at : at + rows] = delta


def out_back(w, attn, parts):
    rows, width = parts[0].shape
    return call(
        functools.partial(out_back_kernel, rows),
        "out_back",
        [
            ((4, CHUNKS, 2 * HD, PER_CHUNK * rows), bf16),
            ((4, CHUNKS, 1, PER_CHUNK * rows), f32),
        ],
        [w] + attn + parts,
        [VMEM_SPEC] * 7,
        8 * rows * width * Q_COLS,
        [pltpu.VMEM((4 * rows, width), bf16)],
    )


def out_grad_kernel(places, attn_t_ref, *rest):
    parts, (own_ref, other_ref, whole_ref, d_ref) = rest[:4], rest[4:]
    rows = parts[0].shape[0]
    for r in range(4):
        d_ref[r * rows : (r + 1) * rows] = parts[r][...]
    whole_ref[...] = dot(attn_t_ref[...], d_ref[...])
    half, slab = own_ref.shape[0], own_ref.shape[1]
    for k in range(half):
        for ref, place in ((own_ref, places[k]), (other_ref, places[half + k])):
            ref[k] = whole_ref[pl.ds(pl.multiple_of(place, slab), slab), :].astype(bf16)


def out_grads(places, attn_t, parts, slab):
    rows, width = parts[0].shape
    half = (places.shape[0] // 2, slab, width)
    return call(
        out_grad_kernel,
        "out_grads",
        [(half, bf16), (half, bf16)],
        [places, attn_t] + parts,
        [SMEM_SPEC] + [VMEM_SPEC] * 5,
        8 * rows * width * Q_COLS,
        [pltpu.VMEM((Q_COLS, width), f32), pltpu.VMEM((4 * rows, width), bf16)],
    )


def back_query_kernel(rows, dq0_ref, dq1_ref, cos_ref, sin_ref, d_ref, turned_ref):
    cosine, sine = cos_ref[...], sin_ref[...]
    for head in range(HEADS):
        at = head % PER_CHUNK * rows
        blocks = [
            (dq0_ref, dq1_ref)[r % 2][r // 2, head // PER_CHUNK, :, at : at + rows]
            for r in range(4)
        ]
        dq = jnp.concatenate(blocks, axis=1) * score_scale
        turned_ref[head * HD : (head + 1) * HD] = unrotate(dq, cosine, sine)
    d_ref[...] = turned_ref[...].T.astype(bf16)


def back_query(dq0, dq1, cosine, sine, rows):
    return call(
        functools.partial(back_query_kernel, rows),
        "back_query",
        [((4 * rows, Q_COLS), bf16)],
        [dq0, dq1, cosine, sine],
        [VMEM_SPEC] * 4,
        0,
        [pltpu.VMEM((Q_COLS, 4 * rows), f32)],
    )[0]


def back_project_kernel(count, rows, starts, dq_ref, kv_ref, cos_ref, sin_ref, *rest):
    toks, pieces, parts = rest[:4], rest[4 : 4 + count], rest[4 + count : 8 + count]
    d_ref, gain_ref, both_ref, inv_ref = rest[8 + count :]
    kv = kv_ref[...].T
    dk = unrotate(kv[:HD] * score_scale, cos_ref[...], sin_ref[...])
    d_ref[...] = jnp.concatenate([dk, kv[HD:]], axis=0).T.astype(bf16)
    both_ref[:, :Q_COLS] = dq_ref[...]
    both_ref[:, Q_COLS:] = d_ref[...]
    for r, tok_ref in enumerate(toks):
        inverse = inverse_rms(tok_ref[...].astype(f32))
        inv_ref[r * rows : (r + 1) * rows] = jnp.broadcast_to(inverse, (rows, LANES))
    for k in range(count):
        product = dot_last(both_ref[...], weight_rows(pieces[k]))
        for z in (0, 1):
            where = run_at(starts, 2 * k + z)
            term = None
            for r in range(4):
                at = slice(r * rows, (r + 1) * rows)
                value = product[at, run_of(z)]
                parts[r][:, where] = value.astype(bf16)
                normed = toks[r][:, where].astype(f32) * inv_ref[at]
                here = jnp.sum(value * normed, axis=0, keepdims=True)
                term = here if term is None else term + here
            gain_ref[:, where] = term


def back_project(starts, dq, kv_sum, cosine, sine, toks, pieces):
    rows, width = toks[0].shape
    tok = 4 * rows
    count = len(pieces)
    return call(
        functools.partial(back_project_kernel, count, rows),
        "back_project",
        [((rows, width), bf16)] * 4 + [((tok, 2 * HD), bf16), ((1, width), f32)],
        [starts, dq, kv_sum, cosine, sine] + toks + pieces,
        [SMEM_SPEC] + [VMEM_SPEC] * (8 + count),
        2 * tok * width * QKV_COLS,
        [pltpu.VMEM((tok, QKV_COLS), bf16), pltpu.VMEM((tok, LANES), f32)],
    )


def rows_of(tile):
    return pl.ds(pl.multiple_of(tile * KEY_TILE, KEY_TILE), KEY_TILE)


def causal(position, rows, columns):
    shape = (KEY_TILE, columns)
    key = lax.broadcasted_iota(jnp.int32, shape, 0)
    row = lax.broadcasted_iota(jnp.int32, shape, 1) % rows
    return key <= row + position % (KEY_TILE // rows) * rows


def fill_keys(place, rows, core, chip, own, all_ref, kvt_ref, kv_ref):
    per_tile = KEY_TILE // rows
    for p, (at, core_bit, member) in enumerate(place):
        where = pl.ds(pl.multiple_of((member ^ own) * rows, rows), rows)
        block = all_ref[core_bit ^ core, at ^ chip, :, where]
        kvt_ref[p // per_tile, :, p % per_tile * rows : (p % per_tile + 1) * rows] = block
        kv_ref[p * rows : (p + 1) * rows, :] = block.T


def forward_kernel(
    offsets, picks, place, rows, me_ref, q_ref, all_ref, o_ref, log_ref, kv_ref, kvt_ref, vt_ref
):
    me, core, chip, own = me_ref[0], me_ref[1], me_ref[2], me_ref[3]
    chunks = q_ref.shape[1]
    fill_keys(place, rows, core, chip, own, all_ref, kvt_ref, kv_ref)
    vt_ref[:, :ONES] = jnp.ones((vt_ref.shape[0], ONES, KEY_TILE), bf16)
    vt_ref[:, ONES:] = kvt_ref[:, HD:]
    for i, (pick, offset) in enumerate(zip(picks, offsets)):
        position = me ^ offset
        last = position // (KEY_TILE // rows)

        def scores(tile):
            kv = kv_ref[rows_of(tile), :]
            return [dot(kv, q_ref[pick, c]) for c in range(chunks)], vt_ref[tile]

        keep = causal(position, rows, q_ref.shape[3])
        found, vt = scores(last)
        state = []
        for s in found:
            s = jnp.where(keep, s, masked_value)
            top = jnp.max(s, axis=0, keepdims=True)
            state.append((top, dot(vt, jnp.exp2((s - top) * to_log2).astype(bf16))))

        def turn(kt, state):
            found, vt = scores(kt)
            out = []
            for s, (top, total) in zip(found, state):
                new_top = jnp.maximum(top, jnp.max(s, axis=0, keepdims=True))
                p = jnp.exp2((s - new_top) * to_log2).astype(bf16)
                out.append((new_top, total * jnp.exp2((top - new_top) * to_log2) + dot(vt, p)))
            return tuple(out)

        state = lax.fori_loop(0, last, turn, tuple(state))
        for c, (top, total) in enumerate(state):
            weight = total[:1]
            o_ref[i, c] = total[ONES:] / weight
            log_ref[i, c] = top * to_log2 + jnp.log2(weight)


def backward_kernel(offsets, picks, place, rows, core_mask, first, *refs):
    me_ref, q_ref, g_ref, all_ref, log_ref, delta_ref = refs[:6]
    kv_ref, kvt_ref = refs[-2:]
    if first:
        dq_ref, dkv_ref = refs[6:8]
        dkv_ref[...] = jnp.zeros_like(dkv_ref)
    else:
        begun_ref, dq_ref, own_ref, other_ref, dkv_ref = refs[6:11]
        dkv_ref[...] = begun_ref[...]
    me, core, chip, own = me_ref[0], me_ref[1], me_ref[2], me_ref[3]
    chunks = q_ref.shape[1]
    fill_keys(place, rows, core, chip, own, all_ref, kvt_ref, kv_ref)
    for i, (pick, offset) in enumerate(zip(picks, offsets)):
        position = me ^ offset
        last = position // (KEY_TILE // rows)

        def turn(tile, keep):
            kv = kv_ref[rows_of(tile), :]
            kvt = kvt_ref[tile]
            pairs = [(dot(kv, q_ref[pick, c]), dot(kv, g_ref[pick, c])) for c in range(chunks)]
            summed, out = None, []
            for c, (s, dp) in enumerate(pairs):
                p = jnp.exp2(s * to_log2 - log_ref[i, c])
                if keep is not None:
                    p = jnp.where(keep, p, 0.0)
                ds = (p * (dp - delta_ref[pick, c])).astype(bf16)
                part = dot_last(p.astype(bf16), g_ref[pick, c]) + dot_last(ds, q_ref[pick, c])
                summed = part if summed is None else summed + part
                out.append(dot(kvt, ds)[:HD])
            dkv_ref[rows_of(tile), :] += summed
            return tuple(out)

        dq = turn(last, causal(position, rows, q_ref.shape[3]))
        dq = lax.fori_loop(
            0, last, lambda tile, dq: tuple(a + b for a, b in zip(dq, turn(tile, None))), dq
        )
        for c in range(chunks):
            dq_ref[i, c] = dq[c]
    if not first:
        for p, (at, core_bit, member) in enumerate(place):
            if core_bit == 0:
                near = (p + core * core_mask) * rows
                far = (p + (1 - core) * core_mask) * rows
                where = pl.ds(pl.multiple_of((member ^ own) * rows, rows), rows)
                own_ref[at ^ chip, where] = dkv_ref[pl.ds(pl.multiple_of(near, rows), rows), :]
                other = dkv_ref[pl.ds(pl.multiple_of(far, rows), rows), :]
                other_ref[at ^ chip, where] = other.astype(bf16)


def attention_forward(me, q, kv_all, offsets, picks, place, rows):
    blocks, chunks, columns = len(picks), q.shape[1], q.shape[3]
    keys = len(place) * rows
    scores = blocks * chunks * columns * keys // 2
    return call(
        functools.partial(forward_kernel, offsets, picks, place, rows),
        "attention_forward",
        [((blocks, chunks, HD, columns), f32), ((blocks, chunks, 1, columns), f32)],
        [me, q, kv_all],
        [SMEM_SPEC, VMEM_SPEC, VMEM_SPEC],
        scores * 8 * HD,
        [
            pltpu.VMEM((keys, 2 * HD), bf16),
            pltpu.VMEM((keys // KEY_TILE, 2 * HD, KEY_TILE), bf16),
            pltpu.VMEM((keys // KEY_TILE, ONES + HD, KEY_TILE), bf16),
        ],
        scores,
    )


def attention_backward(
    me, q, g, kv_all, log_total, delta, dkv, offsets, picks, place, rows, core_mask
):
    chunks, columns = q.shape[1], q.shape[3]
    keys = len(place) * rows
    scores = len(picks) * chunks * columns * keys // 2
    shares = (kv_all.shape[1], kv_all.shape[3], 2 * HD)
    out = [((len(picks), chunks, HD, columns), f32)]
    scratch = [
        pltpu.VMEM((keys, 2 * HD), bf16),
        pltpu.VMEM((keys // KEY_TILE, 2 * HD, KEY_TILE), bf16),
    ]
    args = [me, q, g, kv_all, log_total, delta]
    if dkv is None:
        out = out + [((keys, 2 * HD), f32)]
    else:
        out = out + [(shares, f32), (shares, bf16)]
        scratch = [pltpu.VMEM((keys, 2 * HD), f32)] + scratch
        args = args + [dkv]
    return call(
        functools.partial(backward_kernel, offsets, picks, place, rows, core_mask, dkv is None),
        "attention_backward",
        out,
        args,
        [SMEM_SPEC] + [VMEM_SPEC] * (len(args) - 1),
        scores * 20 * HD,
        scratch,
        scores,
    )


def on_device(
    tokens, gain_attn, w_query, w_key, w_value, w_out, gain_ffn, w_gate, w_up, w_down, out_grad
):
    n_seq = lax.axis_size("seq")
    n_fsdp = lax.axis_size("fsdp")
    n = n_seq * n_fsdp
    me = lax.axis_index(AXES)
    rows, width = tokens.shape
    slab, hidden_width = w_gate.shape
    x_mask, z_mask, core = 1, 2 * n_fsdp, n_fsdp
    t_masks = [0, x_mask, z_mask, x_mask | z_mask]
    far = [n_fsdp << k for k in range(2, n_seq.bit_length() - 1)]
    near = [1 << k for k in range(1, n_fsdp.bit_length() - 1)]
    d_bits = far + near + [core]
    d_masks = [0]
    for bit in d_bits:
        d_masks = d_masks + [m | bit for m in d_masks]
    chips = d_masks[: len(d_masks) // 2]
    d_all = sum(d_bits)
    t_groups = [[b | m for m in t_masks] for b in sorted(d_masks)]

    def swap(value, mask):
        return lax.ppermute(value, AXES, [(i, i ^ mask) for i in range(n)])

    def trade(value, groups):
        return lax.all_to_all(
            value, AXES, split_axis=0, concat_axis=0, tiled=True, axis_index_groups=groups
        )

    def sum_blocks(value, count):
        value = value.reshape((count, -1) + value.shape[1:])
        total = value[0].astype(f32)
        for i in range(1, count):
            total = total + value[i].astype(f32)
        return total

    def spread(pieces, bits):
        pieces = dict(pieces)
        for bit in bits:
            pieces.update({m | bit: swap(v, bit) for m, v in list(pieces.items())})
        return pieces

    def beyond(pieces):
        return {m: v for m, v in pieces.items() if m}

    def joined(own, relayed):
        pieces = {**own, **relayed}
        half = [pieces[m] for m in chips]
        return half + [swap(p, core) for p in half]

    def sum_over(total, bits, after=None):
        for bit in reversed(bits):
            half = total.shape[0] // 2
            got = swap(total[half:].astype(bf16), bit)
            if after is not None:
                got = hold(got, after)
            total = total[:half].astype(f32) + got.astype(f32)
        return total

    def core_sum(pair):
        own, other = pair
        return own.astype(f32) + swap(other, core).astype(f32)

    unit = 2 * slab
    aligned = unit == LANES
    zs = jnp.array([0, z_mask], jnp.int32)
    relative = ((me & d_all) ^ jnp.array(d_masks, jnp.int32))[:, None] + zs[None, :]
    relative = (relative.reshape(-1) // 2 * unit).astype(jnp.int32)
    t = me % 2 + 2 * ((me // z_mask) % 2)
    fixed = [(m | z) // 2 * unit for m in sorted(d_masks) for z in (0, z_mask)]
    fixed = jnp.array(fixed, jnp.int32)
    d_groups = [[b | m for m in sorted(d_masks)] for b in t_masks]
    side = (me % 2).reshape(1).astype(jnp.int32)

    def arranged(value, where):
        return value.reshape(value.shape[0], -1, unit)[:, where // unit].reshape(value.shape)

    def restored(value, where):
        runs = value.reshape(value.shape[0], -1, unit)
        return jnp.zeros_like(runs).at[:, where // unit].set(runs).reshape(value.shape)

    if aligned:
        starts, n_pieces = relative, len(d_masks)
    else:
        starts, n_pieces = jnp.arange(0, width, LANES, dtype=jnp.int32), width // (2 * LANES)

    def copies(value, count):
        shape = (count,) + value.shape
        return jnp.broadcast_to(value[None], shape).reshape((-1,) + value.shape[1:])

    def gather_t(value):
        return [value] + [swap(value, m) for m in t_masks[1:]]

    def relay_t(value):
        along = swap(value, z_mask)
        return [value, swap(value, x_mask), along, swap(along, x_mask)]

    def scatter_t(parts):
        return [parts[0]] + [swap(p, m) for p, m in zip(parts[1:], t_masks[1:])]

    def blocks_of(value):
        return [value[r * rows : (r + 1) * rows] for r in range(4)]

    def send(total, bits):
        total = sum_over(total, bits[1:])
        half = total.shape[0] // 2
        return total[:half].astype(f32), swap(total[half:].astype(bf16), bits[0])

    def give_back(total):
        return trade(total.reshape(4 * slab, -1).astype(bf16), t_groups)

    def by_member(value):
        size = value.shape[0] // 4
        parts = [lax.dynamic_slice_in_dim(value, (t ^ r) * size, size, 0) for r in range(4)]
        return jnp.concatenate(parts, axis=0)

    qkv_shard = trade(pack_attention(side, w_query, w_key, w_value, gain_attn, gain_ffn), t_groups)
    cols = hidden_width // 4
    qkv_far = spread({0: qkv_shard}, far)
    qkv_own = spread({0: qkv_shard}, near)
    near_tokens = hold(tokens, qkv_shard)
    toks = [tokens] + [swap(near_tokens, m) for m in t_masks[1:3]]
    toks = toks + [swap(hold(tokens, qkv_far, qkv_own), t_masks[3])]
    qkv_w = joined(qkv_own, spread(beyond(qkv_far), near))
    if aligned:
        qkv_k = qkv_w
    else:
        parts = jnp.stack(qkv_w).reshape(-1, 2, 2, slab + GAIN_ROWS, QKV_COLS)
        runs = parts[:, :, :, :slab].reshape(-1, unit, QKV_COLS)
        whole = jnp.zeros_like(runs).at[relative // unit].set(runs).reshape(-1, 4, 64, QKV_COLS)
        gains = jnp.stack(
            [parts[:, :, x, slab:, x * slab : (x + 1) * slab] for x in (0, 1)], axis=3
        ).reshape(-1, GAIN_ROWS, unit)
        gains = jnp.zeros_like(gains).at[relative // unit].set(gains)
        gains = jnp.moveaxis(gains, 1, 0).reshape(GAIN_ROWS, -1, 2, 64)
        gains = jnp.moveaxis(gains, 0, 2)
        lane = jnp.arange(QKV_COLS) // 64
        extra = jnp.where(
            lane[None, None, None] == jnp.arange(2)[None, :, None, None],
            jnp.tile(gains, (1, 1, 1, QKV_COLS // 64)),
            jnp.zeros((), bf16),
        ).reshape(-1, 4, GAIN_ROWS, QKV_COLS)
        whole = jnp.concatenate([whole, extra], axis=2).reshape(n_pieces, -1, QKV_COLS)
        qkv_k = [whole[i] for i in range(n_pieces)]

    bits = n.bit_length() - 1
    source = {z_mask.bit_length() - 1: bits - 1, 0: bits - 2}
    free = list(range(bits - 2))
    open_places = [b for b in range(bits) if b not in source]
    for b in list(open_places):
        if b in free:
            source[b] = b
            free.remove(b)
            open_places.remove(b)
    source.update(zip(open_places, free))

    def goes_to(i):
        return sum(((i >> s) & 1) << b for b, s in source.items())

    def came_from(i):
        return sum(((i >> b) & 1) << s for b, s in source.items())

    per_group = n // 4
    out_shard = lax.ppermute(hold(w_out, qkv_shard), AXES, [(i, goes_to(i)) for i in range(n)])
    my_row = came_from(me) % per_group
    out_places = jnp.array([came_from(m) % per_group for m in d_masks], jnp.int32)
    out_places = ((my_row ^ out_places) * slab).astype(jnp.int32)

    out_shard = hold(out_shard, qkv_far)
    out_far = spread({0: out_shard}, far)
    out_own = spread({0: out_shard}, near)
    qkv_k, toks, out_far, out_own = lax.optimization_barrier((qkv_k, toks, out_far, out_own))
    out_all = {**out_own, **spread(beyond(out_far), near)}
    blocks = me ^ jnp.array(t_masks, jnp.int32)
    positions = (blocks[:, None] * rows + jnp.arange(rows, dtype=jnp.int32)).reshape(-1)
    cosine, sine = rope_tables(positions)
    h_attn, q, kv, gains = project(starts, toks, cosine, sine, qkv_k)
    gain_a, gain_f = gains[0:1], gains[1:2]
    pair_shard = trade(hold(pack_columns([w_gate, w_up], "pack_gate_up"), kv), t_groups)
    kv_parts = [kv] + [swap(kv, m) for m in chips[1:]]
    kv_parts, pair_shard, out_all = lax.optimization_barrier((kv_parts, pair_shard, out_all))
    kv = jnp.stack(kv_parts)
    kv_all = jnp.stack([kv, swap(kv, core)])
    place = [
        (
            chips.index(p & sum(far + near)),
            1 if p & core else 0,
            t_masks.index(p & (x_mask | z_mask)),
        )
        for p in range(n)
    ]
    my_chip = sum(((me // bit) % 2) << i for i, bit in enumerate(far + near))
    me_ref = jnp.stack([me, (me // core) % 2, my_chip, t]).astype(jnp.int32)

    pair_w = lax.all_gather(pair_shard, AXES, axis=0, tiled=True, axis_index_groups=d_groups)
    out_half = jnp.concatenate([out_all[m] for m in chips], axis=0)
    out_pieces = [out_half, swap(hold(out_half, kv_all), core)]
    down_shard = trade(pack_columns([hold(w_down, kv_all)], "pack_down"), t_groups)
    g4 = arrange(relative, out_grad) if aligned else arranged(out_grad, relative)

    def forward(x, q):
        return attention_forward(
            me_ref, q, kv_all, [x * x_mask, z_mask + x * x_mask], [x, 2 + x], place, rows
        )

    def backward(x, dkv):
        return attention_backward(
            me_ref,
            q,
            d_heads,
            kv_all,
            log_totals[x],
            delta,
            dkv,
            [x * x_mask, z_mask + x * x_mask],
            [x, 2 + x],
            place,
            rows,
            core,
        )

    attn_a, log_a = forward(0, q)
    attn_a, q_b, out_pieces, down_shard = lax.optimization_barrier(
        (attn_a, q, out_pieces, down_shard)
    )
    down_own = spread({0: hold(down_shard, attn_a)}, near)
    g = trade(copies(hold(g4, attn_a), 4), t_groups)
    attn_b, log_b = forward(1, q_b)
    attn, log_totals = [attn_a, attn_b], [log_a, log_b]
    *middle_parts, attn_t, out_w = out_products(out_places, attn, out_pieces, rows)
    middle_parts = scatter_t(middle_parts)

    def halves(pieces):
        half = jnp.concatenate([pieces[m] for m in chips], axis=0)
        return [half, swap(half, core)]

    middle_parts, down_own, g = lax.optimization_barrier((middle_parts, down_own, g))
    down_far = spread({0: hold(down_shard, middle_parts)}, far)
    g = by_member(hold(g, middle_parts))

    if aligned:
        middle, h = middle_norm(fixed, tokens, gain_f, middle_parts)
    else:
        middle = tokens.astype(f32) + sum([p.astype(f32) for p in middle_parts])
        h = arranged((middle * inverse_rms(middle) * gain_f).astype(bf16), fixed)
    h_parts = gather_t(h)
    h_parts, g = lax.optimization_barrier((h_parts, g))
    down_all = {**down_own, **spread(hold(beyond(down_far), h_parts), near)}
    h_ffn = jnp.concatenate(h_parts, axis=0)
    half_width = width // 2

    def by_halves(left, w):
        return dot(left[:, :half_width], w[0]) + dot(left[:, half_width:], w[1])

    down_w = halves(down_all)
    pair = dot(h_ffn, pair_w)
    gate, up = pair[:, :cols], pair[:, cols:]
    sig = jax.nn.sigmoid(gate)
    act = gate * sig
    hidden = (act * up).astype(bf16)
    d_hidden = by_halves(g, down_w)
    d_gate = (d_hidden * up * sig * (1.0 + gate * (1.0 - sig))).astype(bf16)
    d_up = (d_hidden * act).astype(bf16)
    d_pair = jnp.concatenate([d_gate, d_up], axis=1)
    d_hffn_part = dot_last(d_pair, pair_w).astype(bf16)
    d_hffn_blocks = blocks_of(d_hffn_part)
    d_hffn_parts = scatter_t(d_hffn_blocks)

    def weight_grad(left, right):
        other = dot_first(left[:, half_width:], right).astype(bf16)
        return dot_first(left[:, :half_width], right) + swap(other, core).astype(f32)

    pair_grad = dot_first(hold(h_ffn, d_hffn_blocks), d_pair).astype(bf16)
    pair_total = lax.psum_scatter(
        pair_grad, AXES, scatter_dimension=0, tiled=True, axis_index_groups=d_groups
    )
    block_part = jnp.concatenate(
        [dot_last(hold(hidden, pair_grad), w).astype(bf16) for w in down_w], axis=1
    )
    d_hffn_parts, pair_grad, block_part = lax.optimization_barrier(
        (d_hffn_parts, pair_grad, block_part)
    )
    down_sum = weight_grad(hold(g, d_hffn_parts), hidden)
    block_blocks = by_member(hold(block_part, d_hffn_parts))

    if aligned:
        d_middle, d_low, gain_ffn_term = norm_back(fixed, middle, out_grad, gain_f, d_hffn_parts)
    else:
        d_hffn = restored(sum([p.astype(f32) for p in d_hffn_parts]), fixed)
        inverse = inverse_rms(middle)
        normed = middle * inverse
        scaled = d_hffn * gain_f
        gain_ffn_term = jnp.sum(d_hffn * normed, axis=0, keepdims=True)
        d_middle = out_grad.astype(f32) + inverse * (
            scaled - normed * jnp.mean(scaled * normed, axis=-1, keepdims=True)
        )
        d_low = d_middle.astype(bf16)
    d_branch = relay_t(d_low)
    d_branch, down_sum, block_blocks = lax.optimization_barrier((d_branch, down_sum, block_blocks))
    d_heads, delta = out_back(out_w, attn, d_branch)

    block_parts = trade(hold(block_blocks, d_heads), t_groups)
    down_near = hold(down_sum, d_heads)
    for bit in reversed(near):
        half = down_near.shape[0] // 2
        down_got = swap(down_near[half:].astype(bf16), bit)
        down_near = down_near[:half].astype(f32)
        if bit != near[0]:
            down_near = down_near + down_got.astype(f32)
    dq0, dkv = backward(0, None)
    dq1, own, other = backward(1, dkv)
    other, down_got, block_parts = lax.optimization_barrier((other, down_got, block_parts))
    kv_sums = own + swap(other, core).astype(f32)
    kv_sends = [kv_sums[i].astype(bf16) for i in range(len(chips))]
    kv_parts = [swap(kv_sends[i], m) for i, m in enumerate(chips) if m]
    dq0, dq1, block_parts, down_got, pair_total = hold(
        (dq0, dq1, block_parts, down_got, pair_total), kv_sends
    )
    d_query = back_query(dq0, dq1, cosine, sine, rows)
    if aligned:
        query_pair = query_grads(starts, h_attn, d_query, n_pieces)
    else:
        grads = dot_first(h_attn, d_query).astype(bf16).reshape(-1, unit, Q_COLS)
        grads = grads[relative // unit].reshape(len(d_masks), -1, Q_COLS)
        query_pair = grads[: len(chips)], grads[len(chips) :]
    query_sum = core_sum(query_pair)
    down_keep, down_got = send(down_near + down_got.astype(f32), far)
    pair_parts = trade(pair_total, t_groups)
    if aligned:
        block_out = block_output(relative, middle, block_parts)
    else:
        block_out = (middle + restored(sum_blocks(block_parts, 4), relative)).astype(bf16)
    kv_parts, query_sum, block_out = lax.optimization_barrier((kv_parts, query_sum, block_out))
    kv_sum = kv_sums[0]
    for part in kv_parts:
        kv_sum = kv_sum + part.astype(f32)
    query_keep, query_got = send(query_sum, near)
    *d_hattn_blocks, d_kv, gain_attn_part = back_project(
        starts, d_query, kv_sum, cosine, sine, toks, qkv_k
    )
    d_hattn_blocks, query_got, pair_parts = lax.optimization_barrier(
        (d_hattn_blocks, query_got, pair_parts)
    )
    query_near = query_keep + query_got.astype(f32)
    d_hattn_parts = scatter_t(d_hattn_blocks)
    d_kv, gain_attn_part = hold((d_kv, gain_attn_part), d_hattn_blocks)
    if aligned:
        own, other = key_grads(starts, h_attn, d_kv, gain_attn_part, gain_ffn_term, n_pieces, slab)
    else:
        grads = dot_first(h_attn, d_kv).astype(bf16).reshape(-1, unit, 2 * HD)
        grads = grads[relative // unit].reshape(-1, 4, slab, 2 * HD)
        terms = jnp.concatenate([gain_attn_part, gain_ffn_term]).astype(bf16)
        terms = terms.reshape(2, -1, unit)[:, relative // unit].reshape(2, -1, 2, 1, unit)
        terms = jnp.moveaxis(jnp.broadcast_to(terms, terms.shape[:3] + (2, unit)), 0, 3)
        terms = terms.reshape(-1, 4, 2, unit)
        terms = jnp.pad(terms, ((0, 0), (0, 0), (0, GAIN_ROWS - 2), (0, 2 * HD - unit)))
        grads = jnp.concatenate([grads, terms], axis=2).reshape(len(d_masks), -1, 2 * HD)
        own, other = grads[: len(chips)], grads[len(chips) :]
    key_sum = core_sum((own, other))
    after = d_hattn_parts[1:]
    grad_gate, grad_up = unpack_columns(pair_parts, 2, "unpack_gate_up")
    out_pair = out_grads(out_places, attn_t, hold(d_branch, d_hattn_blocks), slab)
    out_near = sum_over(core_sum(out_pair), near)
    key_sum, query_near, down_got, out_near = hold((key_sum, query_near, down_got, out_near), after)
    query_keep, query_got = send(query_near, far)
    out_keep, out_got = send(out_near, far)
    d_hattn_parts, grad_gate, grad_up = lax.optimization_barrier((d_hattn_parts, grad_gate, grad_up))
    query_total = query_keep + query_got.astype(f32)
    out_total = (out_keep + out_got.astype(f32)).astype(bf16).reshape(slab, width)
    down_total = down_keep + down_got.astype(f32)
    key_total = sum_over(sum_over(key_sum, near), far)
    grad_out_proj = lax.ppermute(out_total, AXES, [(goes_to(i), i) for i in range(n)]).astype(f32)
    merged = [v.reshape(4 * slab, -1).astype(bf16) for v in (query_total, down_total)]
    merged = trade(jnp.concatenate(merged, axis=1), t_groups)
    grad_query, grad_down = unpack_two(merged, Q_COLS, "unpack_query_down")
    key_parts = trade(key_total.reshape(-1, 2 * HD).astype(bf16), t_groups)
    grad_key, grad_value, gain_terms = unpack_keys(side, key_parts)

    own = tokens.astype(f32)
    inverse_attn = inverse_rms(own)
    normed_attn = own * inverse_attn
    d_hattn = d_hattn_parts[0].astype(f32)
    for part in d_hattn_parts[1:]:
        d_hattn = d_hattn + part.astype(f32)
    scaled = d_hattn * gain_a
    grad_tokens = d_middle + inverse_attn * (
        scaled - normed_attn * jnp.mean(scaled * normed_attn, axis=-1, keepdims=True)
    )
    return (
        block_out,
        grad_tokens,
        gain_terms[0],
        grad_query,
        grad_key,
        grad_value,
        grad_out_proj,
        gain_terms[1],
        grad_gate,
        grad_up,
        grad_down,
    )


def solution(mesh):
    spec2 = P(AXES, None)
    spec1 = P(AXES)
    return jax.shard_map(
        on_device,
        mesh=mesh,
        in_specs=(
            spec2,
            spec1,
            spec2,
            spec2,
            spec2,
            spec2,
            spec1,
            spec2,
            spec2,
            spec2,
            spec2,
        ),
        out_specs=(
            spec2,
            spec2,
            spec1,
            spec2,
            spec2,
            spec2,
            spec2,
            spec1,
            spec2,
            spec2,
            spec2,
        ),
        check_vma=False,
    )
```

```python
import functools
import math

import jax
import jax.numpy as jnp
from jax import lax
from jax.experimental import pallas as pl
from jax.experimental.pallas import tpu as pltpu
from jax.sharding import PartitionSpec as P

H = 32
KV = 4
HD = 64
AXES = ("seq", "fsdp")
norm_eps = 1e-05
rope_base = 10000.0
masked_value = -1e30
score_scale = HD ** (-0.5)
to_log2 = score_scale * math.log2(math.e)
bf16 = jnp.bfloat16
f32 = jnp.float32
KEY_TILE = 512
ONES = 16
LANES = 128
GAIN_ROWS = 16
CHUNKS = 2
HEADS = H // KV
PER_CHUNK = HEADS // CHUNKS
Q_COLS = HEADS * HD
QKV_COLS = Q_COLS + 2 * HD

SMEM_SPEC = pl.BlockSpec(memory_space=pltpu.SMEM)
VMEM_SPEC = pl.BlockSpec(memory_space=pltpu.VMEM)
ANY_SPEC = pl.BlockSpec(memory_space=pl.ANY)


def dot(a, b):
    return lax.dot_general(a, b, (((1,), (0,)), ((), ())), preferred_element_type=f32)


def dot_last(a, b):
    return lax.dot_general(a, b, (((1,), (1,)), ((), ())), preferred_element_type=f32)


def dot_first(a, b):
    return lax.dot_general(a, b, (((0,), (0,)), ((), ())), preferred_element_type=f32)


def inverse_rms(values):
    return lax.rsqrt(jnp.mean(values * values, axis=-1, keepdims=True) + norm_eps)


def rope_tables(positions):
    half = HD // 2
    frequency = rope_base ** (-(jnp.arange(half, dtype=f32) * 2.0) / HD)
    angles = positions.astype(f32)[None, :] * frequency[:, None]
    return (jnp.cos(angles), jnp.sin(angles))


def rotate(values, cosine, sine):
    a, b = values[: HD // 2], values[HD // 2 :]
    return jnp.concatenate([a * cosine - b * sine, b * cosine + a * sine], axis=0)


def unrotate(values, cosine, sine):
    a, b = values[: HD // 2], values[HD // 2 :]
    return jnp.concatenate([a * cosine + b * sine, b * cosine - a * sine], axis=0)


def hold(value, *others):
    return lax.optimization_barrier((value, others))[0]


def call(kernel, name, out, args, specs, flops, scratch=(), exps=0):
    out_shape = tuple(jax.ShapeDtypeStruct(s, d) for s, d in out)
    size = sum(a.size * a.dtype.itemsize for a in args)
    size += sum(math.prod(s.shape) * s.dtype.itemsize for s in out_shape)
    return pl.pallas_call(
        kernel,
        out_shape=out_shape,
        in_specs=specs,
        out_specs=(VMEM_SPEC,) * len(out_shape),
        scratch_shapes=list(scratch),
        compiler_params=pltpu.CompilerParams(vmem_limit_bytes=58 << 20),
        cost_estimate=pl.CostEstimate(flops=flops, bytes_accessed=size, transcendentals=exps),
        name=name,
    )(*args)


def columns_of(ref, starts, k):
    runs = [
        ref[:, pl.ds(pl.multiple_of(starts[2 * k + z], LANES), LANES)] for z in (0, 1)
    ]
    return jnp.concatenate(runs, axis=1)


def pack_kernel(member, q_ref, k_ref, v_ref, ga_ref, gf_ref, out_ref):
    slab = q_ref.shape[0]
    side = member[0]
    row = lax.broadcasted_iota(jnp.int32, (GAIN_ROWS, LANES), 0)
    lane = lax.broadcasted_iota(jnp.int32, (GAIN_ROWS, LANES), 1)
    gains = []
    for ref in (ga_ref, gf_ref):
        gains.append(jnp.concatenate([ref[...].astype(f32)] * (LANES // slab), axis=1))
    block = jnp.where(row == 0, gains[0], jnp.where(row == 1, gains[1], 0.0))
    block = jnp.where(lane // slab == side, block, 0.0).astype(bf16)
    block = jnp.concatenate([block, jnp.zeros((GAIN_ROWS, QKV_COLS - LANES), bf16)], axis=1)
    for i in range(4):
        at = i * (slab + GAIN_ROWS)
        out_ref[at : at + slab, :Q_COLS] = q_ref[:, i * Q_COLS : (i + 1) * Q_COLS]
        kv = [ref[:, i * HD : (i + 1) * HD] for ref in (k_ref, v_ref)]
        out_ref[at : at + slab, Q_COLS:] = jnp.concatenate(kv, axis=1)
        out_ref[at + slab : at + slab + GAIN_ROWS] = block


def pack_attention(side, w_query, w_key, w_value, gain_attn, gain_ffn):
    slab = w_query.shape[0]
    return call(
        pack_kernel,
        "pack_attention",
        [((4 * (slab + GAIN_ROWS), QKV_COLS), bf16)],
        [side, w_query, w_key, w_value, gain_attn.reshape(1, slab), gain_ffn.reshape(1, slab)],
        [SMEM_SPEC] + [VMEM_SPEC] * 5,
        0,
    )[0]


def pack_columns_kernel(cols, *refs):
    ins, out_ref = refs[:-1], refs[-1]
    slab = ins[0].shape[0]
    for i in range(4):
        for w, ref in enumerate(ins):
            out_ref[i * slab : (i + 1) * slab, w * cols : (w + 1) * cols] = ref[
                :, i * cols : (i + 1) * cols
            ]


def pack_columns(weights, name):
    slab, cols = weights[0].shape[0], weights[0].shape[1] // 4
    return call(
        functools.partial(pack_columns_kernel, cols),
        name,
        [((4 * slab, cols * len(weights)), bf16)],
        list(weights),
        [VMEM_SPEC] * len(weights),
        0,
    )[0]


def unpack_columns_kernel(cols, in_ref, *outs):
    slab = outs[0].shape[0]
    for i in range(4):
        for w, ref in enumerate(outs):
            ref[:, i * cols : (i + 1) * cols] = in_ref[
                i * slab : (i + 1) * slab, w * cols : (w + 1) * cols
            ].astype(f32)


def unpack_columns(value, count, name):
    slab, cols = value.shape[0] // 4, value.shape[1] // count
    return call(
        functools.partial(unpack_columns_kernel, cols),
        name,
        [((slab, 4 * cols), f32)] * count,
        [value],
        [VMEM_SPEC],
        0,
    )


def unpack_two_kernel(in_ref, first_ref, second_ref):
    slab = first_ref.shape[0]
    wide, cols = first_ref.shape[1] // 4, second_ref.shape[1] // 4
    for i in range(4):
        rows = slice(i * slab, (i + 1) * slab)
        first_ref[:, i * wide : (i + 1) * wide] = in_ref[rows, :wide].astype(f32)
        second_ref[:, i * cols : (i + 1) * cols] = in_ref[rows, wide:].astype(f32)


def unpack_two(value, wide, name):
    slab, cols = value.shape[0] // 4, value.shape[1] - wide
    return call(
        unpack_two_kernel,
        name,
        [((slab, 4 * wide), f32), ((slab, 4 * cols), f32)],
        [value],
        [VMEM_SPEC],
        0,
    )


def unpack_keys_kernel(member, in_ref, k_ref, v_ref, gain_ref):
    slab = k_ref.shape[0]
    gains = jnp.zeros((2, LANES), f32)
    keys, values = [], []
    for i in range(4):
        at = i * (slab + GAIN_ROWS)
        kv = in_ref[at : at + slab].astype(f32)
        keys.append(kv[:, :HD])
        values.append(kv[:, HD:])
        gains = gains + in_ref[at + slab : at + slab + GAIN_ROWS].astype(f32)[:2]
    k_ref[...] = jnp.concatenate(keys, axis=1)
    v_ref[...] = jnp.concatenate(values, axis=1)
    halves = [gains[:, j * slab : (j + 1) * slab] for j in range(2)]
    gain_ref[...] = jnp.where(member[0] == 0, halves[0], halves[1])


def unpack_keys(side, value):
    slab = value.shape[0] // 4 - GAIN_ROWS
    return call(
        unpack_keys_kernel,
        "unpack_keys",
        [((slab, 4 * HD), f32), ((slab, 4 * HD), f32), ((2, slab), f32)],
        [side, value],
        [SMEM_SPEC, VMEM_SPEC],
        0,
    )


def run_at(starts, j):
    start = starts[j]
    return pl.ds(start if isinstance(start, int) else pl.multiple_of(start, LANES), LANES)


def run_of(j):
    return slice(j * LANES, (j + 1) * LANES)


def sum_of(refs, columns=slice(None)):
    total = refs[0][:, columns].astype(f32)
    for ref in refs[1:]:
        total = total + ref[:, columns].astype(f32)
    return total


def middle_kernel(starts, tok_ref, gain_ref, *rest):
    parts, (mid_ref, h_ref) = rest[:4], rest[4:]
    middle = tok_ref[...].astype(f32) + sum_of(parts)
    mid_ref[...] = middle
    inverse = inverse_rms(middle)
    for j in range(tok_ref.shape[1] // LANES):
        run = run_at(starts, j)
        h_ref[:, run_of(j)] = (mid_ref[:, run] * inverse * gain_ref[:, run]).astype(bf16)


def middle_norm(starts, tokens, gain, parts):
    return call(
        middle_kernel,
        "middle_norm",
        [(tokens.shape, f32), (tokens.shape, bf16)],
        [starts, tokens, gain] + parts,
        [SMEM_SPEC] + [VMEM_SPEC] * 6,
        0,
    )


def arrange_kernel(starts, in_ref, out_ref):
    for j in range(in_ref.shape[1] // LANES):
        out_ref[:, run_of(j)] = in_ref[:, run_at(starts, j)]


def arrange(starts, value):
    return call(
        arrange_kernel,
        "arrange",
        [(value.shape, bf16)],
        [starts, value],
        [SMEM_SPEC, VMEM_SPEC],
        0,
    )[0]


def block_kernel(starts, mid_ref, part_ref, out_ref):
    rows = mid_ref.shape[0]
    parts = [part_ref.at[pl.ds(r * rows, rows)] for r in range(4)]
    for j in range(mid_ref.shape[1] // LANES):
        where = run_at(starts, j)
        out_ref[:, where] = (mid_ref[:, where] + sum_of(parts, run_of(j))).astype(bf16)


def block_output(starts, middle, parts):
    return call(
        block_kernel,
        "block_output",
        [(middle.shape, bf16)],
        [starts, middle, parts],
        [SMEM_SPEC, VMEM_SPEC, VMEM_SPEC],
        0,
    )[0]


def norm_back_kernel(starts, mid_ref, grad_ref, gain_ref, *rest):
    parts, (d_ref, low_ref, term_ref) = rest[:4], rest[4:]
    middle = mid_ref[...]
    inverse = inverse_rms(middle)
    for j in range(mid_ref.shape[1] // LANES):
        d_ref[:, run_at(starts, j)] = sum_of(parts, run_of(j))
    grad = d_ref[...]
    normed = middle * inverse
    term_ref[...] = jnp.sum(grad * normed, axis=0, keepdims=True)
    scaled = grad * gain_ref[...]
    mean = jnp.mean(scaled * normed, axis=-1, keepdims=True)
    d_middle = grad_ref[...].astype(f32) + inverse * (scaled - normed * mean)
    d_ref[...] = d_middle
    low_ref[...] = d_middle.astype(bf16)


def norm_back(starts, middle, out_grad, gain, parts):
    return call(
        norm_back_kernel,
        "norm_back",
        [(middle.shape, f32), (middle.shape, bf16), ((1, middle.shape[1]), f32)],
        [starts, middle, out_grad, gain] + parts,
        [SMEM_SPEC] + [VMEM_SPEC] * 7,
        0,
    )


def query_grad_kernel(count, starts, h_ref, d_ref, own_ref, other_ref):
    for ref, first in ((other_ref, count // 2), (own_ref, 0)):
        for k in range(count // 2):
            ref[k] = dot_first(columns_of(h_ref, starts, first + k), d_ref[...]).astype(bf16)


def query_grads(starts, h, d, count):
    half = (count // 2, 2 * LANES, d.shape[1])
    return call(
        functools.partial(query_grad_kernel, count),
        "query_grads",
        [(half, bf16), (half, bf16)],
        [starts, h, d],
        [SMEM_SPEC] + [VMEM_SPEC] * 2,
        2 * h.shape[0] * h.shape[1] * d.shape[1],
    )


def key_grad_kernel(count, starts, h_ref, d_ref, ga_ref, gf_ref, own_ref, other_ref):
    row = lax.broadcasted_iota(jnp.int32, (GAIN_ROWS, LANES), 0)
    slab = own_ref.shape[1] // 4 - GAIN_ROWS
    for ref, first in ((other_ref, count // 2), (own_ref, 0)):
        for k in range(count // 2):
            grad = dot_first(columns_of(h_ref, starts, first + k), d_ref[...]).astype(bf16)
            for i in range(4):
                where = run_at(starts, 2 * (first + k) + i // 2)
                gains = jnp.where(row == 0, ga_ref[:, where], gf_ref[:, where])
                at = i * (slab + GAIN_ROWS)
                ref[k, at : at + slab] = grad[i * slab : (i + 1) * slab]
                ref[k, at + slab : at + slab + GAIN_ROWS] = jnp.where(row < 2, gains, 0.0).astype(
                    bf16
                )


def key_grads(starts, h, d, gain_a, gain_f, count, slab):
    half = (count // 2, 4 * (slab + GAIN_ROWS), 2 * HD)
    return call(
        functools.partial(key_grad_kernel, count),
        "key_grads",
        [(half, bf16), (half, bf16)],
        [starts, h, d, gain_a, gain_f],
        [SMEM_SPEC] + [VMEM_SPEC] * 4,
        4 * h.shape[0] * h.shape[1] * HD,
    )


def weight_rows(piece):
    slab = piece.shape[0] // 4 - GAIN_ROWS
    at = [i * (slab + GAIN_ROWS) for i in range(4)]
    return jnp.concatenate([piece[a : a + slab] for a in at], axis=0)


def project_kernel(count, rows, starts, cos_ref, sin_ref, *rest):
    toks, pieces = rest[:4], rest[4 : 4 + count]
    h_ref, q_ref, kv_ref, gain_ref = rest[4 + count :]
    stride = pieces[0].shape[0] // 4
    for k in range(count):
        for z in (0, 1):
            gains = None
            for x in (0, 1):
                at = (2 * z + x + 1) * stride - GAIN_ROWS
                part = pieces[k][at : at + GAIN_ROWS, :LANES].astype(f32)
                gains = part if gains is None else gains + part
            gain_ref[:, run_at(starts, 2 * k + z)] = gains[:8]

    for r, tok_ref in enumerate(toks):
        wide = tok_ref[...].astype(f32)
        h_ref[r * rows : (r + 1) * rows] = (wide * inverse_rms(wide) * gain_ref[:1]).astype(bf16)
    total = None
    for k in range(count):
        product = dot(columns_of(h_ref, starts, k), weight_rows(pieces[k]))
        total = product if total is None else total + product
    turned = total.astype(bf16).astype(f32).T
    cosine, sine = cos_ref[...], sin_ref[...]
    for head in range(HEADS):
        q = rotate(turned[head * HD : (head + 1) * HD], cosine, sine).astype(bf16)
        at = head % PER_CHUNK * rows
        for r in range(4):
            q_ref[r, head // PER_CHUNK, :HD, at : at + rows] = q[:, r * rows : (r + 1) * rows]
    q_ref[:, :, HD:, :] = jnp.zeros((4, CHUNKS, HD, PER_CHUNK * rows), bf16)
    kv_ref[:HD] = rotate(turned[Q_COLS : Q_COLS + HD], cosine, sine).astype(bf16)
    kv_ref[HD:] = turned[Q_COLS + HD :].astype(bf16)


def project(starts, toks, cosine, sine, pieces):
    rows, width = toks[0].shape
    tok = 4 * rows
    count = len(pieces)
    return call(
        functools.partial(project_kernel, count, rows),
        "project",
        [
            ((tok, width), bf16),
            ((4, CHUNKS, 2 * HD, PER_CHUNK * rows), bf16),
            ((2 * HD, tok), bf16),
            ((8, width), f32),
        ],
        [starts, cosine, sine] + toks + pieces,
        [SMEM_SPEC] + [VMEM_SPEC] * (6 + count),
        2 * tok * width * QKV_COLS,
    )


def out_kernel(rows, places, attn_a_ref, attn_b_ref, *rest):
    pieces, parts, (attn_t_ref, w_ref) = rest[:-6], rest[-6:-2], rest[-2:]
    count = places.shape[0] // 2
    slab = pieces[0].shape[0] // count
    for k in range(2 * count):
        piece = pieces[k // count][k % count * slab : (k % count + 1) * slab, :]
        w_ref[pl.ds(pl.multiple_of(places[k], slab), slab), :] = piece
    for head in range(HEADS):
        at = head % PER_CHUNK * rows
        for r in range(4):
            block = (attn_a_ref, attn_b_ref)[r % 2][r // 2, head // PER_CHUNK, :, at : at + rows]
            attn_t_ref[head * HD : (head + 1) * HD, r * rows : (r + 1) * rows] = block.astype(bf16)
    step = 512
    for c in range(0, w_ref.shape[1], step):
        part = dot_first(attn_t_ref[...], w_ref[:, c : c + step]).astype(bf16)
        for r in range(4):
            parts[r][:, c : c + step] = part[r * rows : (r + 1) * rows]


def out_products(places, attn, pieces, rows):
    width = pieces[0].shape[1]
    tok = 4 * rows
    return call(
        functools.partial(out_kernel, rows),
        "out_products",
        [((rows, width), bf16)] * 4 + [((Q_COLS, tok), bf16), ((Q_COLS, width), bf16)],
        [places] + attn + pieces,
        [SMEM_SPEC] + [VMEM_SPEC] * (2 + len(pieces)),
        2 * tok * width * Q_COLS,
    )


def out_back_kernel(rows, w_ref, attn_a_ref, attn_b_ref, *rest):
    parts, (g_ref, delta_ref, d_ref) = rest[:4], rest[4:]
    for r in range(4):
        d_ref[r * rows : (r + 1) * rows] = parts[r][...]
    turned = dot_last(w_ref[...], d_ref[...]).astype(bf16)
    g_ref[:, :, :HD, :] = jnp.zeros((4, CHUNKS, HD, PER_CHUNK * rows), bf16)
    for head in range(HEADS):
        at = head % PER_CHUNK * rows
        chunk = head // PER_CHUNK
        for r in range(4):
            g = turned[head * HD : (head + 1) * HD, r * rows : (r + 1) * rows]
            g_ref[r, chunk, HD:, at : at + rows] = g
            attn = (attn_a_ref, attn_b_ref)[r % 2][r // 2, chunk, :, at : at + rows]
            delta = jnp.sum(g.astype(f32) * attn, axis=0, keepdims=True)
            delta_ref[r, chunk, :, at : at + rows] = delta


def out_back(w, attn, parts):
    rows, width = parts[0].shape
    return call(
        functools.partial(out_back_kernel, rows),
        "out_back",
        [
            ((4, CHUNKS, 2 * HD, PER_CHUNK * rows), bf16),
            ((4, CHUNKS, 1, PER_CHUNK * rows), f32),
        ],
        [w] + attn + parts,
        [VMEM_SPEC] * 7,
        8 * rows * width * Q_COLS,
        [pltpu.VMEM((4 * rows, width), bf16)],
    )


def out_grad_kernel(places, attn_t_ref, *rest):
    parts, (own_ref, other_ref, whole_ref, d_ref) = rest[:4], rest[4:]
    rows = parts[0].shape[0]
    for r in range(4):
        d_ref[r * rows : (r + 1) * rows] = parts[r][...]
    whole_ref[...] = dot(attn_t_ref[...], d_ref[...])
    half, slab = own_ref.shape[0], own_ref.shape[1]
    for k in range(half):
        for ref, place in ((own_ref, places[k]), (other_ref, places[half + k])):
            ref[k] = whole_ref[pl.ds(pl.multiple_of(place, slab), slab), :].astype(bf16)


def out_grads(places, attn_t, parts, slab):
    rows, width = parts[0].shape
    half = (places.shape[0] // 2, slab, width)
    return call(
        out_grad_kernel,
        "out_grads",
        [(half, bf16), (half, bf16)],
        [places, attn_t] + parts,
        [SMEM_SPEC] + [VMEM_SPEC] * 5,
        8 * rows * width * Q_COLS,
        [pltpu.VMEM((Q_COLS, width), f32), pltpu.VMEM((4 * rows, width), bf16)],
    )


def back_query_kernel(rows, dq0_ref, dq1_ref, cos_ref, sin_ref, d_ref, turned_ref):
    cosine, sine = cos_ref[...], sin_ref[...]
    for head in range(HEADS):
        at = head % PER_CHUNK * rows
        blocks = [
            (dq0_ref, dq1_ref)[r % 2][r // 2, head // PER_CHUNK, :, at : at + rows]
            for r in range(4)
        ]
        dq = jnp.concatenate(blocks, axis=1) * score_scale
        turned_ref[head * HD : (head + 1) * HD] = unrotate(dq, cosine, sine)
    d_ref[...] = turned_ref[...].T.astype(bf16)


def back_query(dq0, dq1, cosine, sine, rows):
    return call(
        functools.partial(back_query_kernel, rows),
        "back_query",
        [((4 * rows, Q_COLS), bf16)],
        [dq0, dq1, cosine, sine],
        [VMEM_SPEC] * 4,
        0,
        [pltpu.VMEM((Q_COLS, 4 * rows), f32)],
    )[0]


def back_project_kernel(count, rows, starts, dq_ref, kv_ref, cos_ref, sin_ref, *rest):
    toks, pieces, parts = rest[:4], rest[4 : 4 + count], rest[4 + count : 8 + count]
    d_ref, gain_ref, both_ref, inv_ref = rest[8 + count :]
    kv = kv_ref[...].T
    dk = unrotate(kv[:HD] * score_scale, cos_ref[...], sin_ref[...])
    d_ref[...] = jnp.concatenate([dk, kv[HD:]], axis=0).T.astype(bf16)
    both_ref[:, :Q_COLS] = dq_ref[...]
    both_ref[:, Q_COLS:] = d_ref[...]
    for r, tok_ref in enumerate(toks):
        inverse = inverse_rms(tok_ref[...].astype(f32))
        inv_ref[r * rows : (r + 1) * rows] = jnp.broadcast_to(inverse, (rows, LANES))
    for k in range(count):
        product = dot_last(both_ref[...], weight_rows(pieces[k]))
        for z in (0, 1):
            where = run_at(starts, 2 * k + z)
            term = None
            for r in range(4):
                at = slice(r * rows, (r + 1) * rows)
                value = product[at, run_of(z)]
                parts[r][:, where] = value.astype(bf16)
                normed = toks[r][:, where].astype(f32) * inv_ref[at]
                here = jnp.sum(value * normed, axis=0, keepdims=True)
                term = here if term is None else term + here
            gain_ref[:, where] = term


def back_project(starts, dq, kv_sum, cosine, sine, toks, pieces):
    rows, width = toks[0].shape
    tok = 4 * rows
    count = len(pieces)
    return call(
        functools.partial(back_project_kernel, count, rows),
        "back_project",
        [((rows, width), bf16)] * 4 + [((tok, 2 * HD), bf16), ((1, width), f32)],
        [starts, dq, kv_sum, cosine, sine] + toks + pieces,
        [SMEM_SPEC] + [VMEM_SPEC] * (8 + count),
        2 * tok * width * QKV_COLS,
        [pltpu.VMEM((tok, QKV_COLS), bf16), pltpu.VMEM((tok, LANES), f32)],
    )


def rows_of(tile):
    return pl.ds(pl.multiple_of(tile * KEY_TILE, KEY_TILE), KEY_TILE)


def causal(position, rows, columns):
    shape = (KEY_TILE, columns)
    key = lax.broadcasted_iota(jnp.int32, shape, 0)
    row = lax.broadcasted_iota(jnp.int32, shape, 1) % rows
    return key <= row + position % (KEY_TILE // rows) * rows


def fill_keys(place, rows, core, chip, own, all_ref, kvt_ref, kv_ref):
    per_tile = KEY_TILE // rows
    for p, (at, core_bit, member) in enumerate(place):
        where = pl.ds(pl.multiple_of((member ^ own) * rows, rows), rows)
        block = all_ref[core_bit ^ core, at ^ chip, :, where]
        kvt_ref[p // per_tile, :, p % per_tile * rows : (p % per_tile + 1) * rows] = block
        kv_ref[p * rows : (p + 1) * rows, :] = block.T


def forward_kernel(
    offsets, picks, place, rows, me_ref, q_ref, all_ref, o_ref, log_ref, kv_ref, kvt_ref, vt_ref
):
    me, core, chip, own = me_ref[0], me_ref[1], me_ref[2], me_ref[3]
    chunks = q_ref.shape[1]
    fill_keys(place, rows, core, chip, own, all_ref, kvt_ref, kv_ref)
    vt_ref[:, :ONES] = jnp.ones((vt_ref.shape[0], ONES, KEY_TILE), bf16)
    vt_ref[:, ONES:] = kvt_ref[:, HD:]
    for i, (pick, offset) in enumerate(zip(picks, offsets)):
        position = me ^ offset
        last = position // (KEY_TILE // rows)

        def scores(tile):
            kv = kv_ref[rows_of(tile), :]
            return [dot(kv, q_ref[pick, c]) for c in range(chunks)], vt_ref[tile]

        keep = causal(position, rows, q_ref.shape[3])
        found, vt = scores(last)
        state = []
        for s in found:
            s = jnp.where(keep, s, masked_value)
            top = jnp.max(s, axis=0, keepdims=True)
            state.append((top, dot(vt, jnp.exp2((s - top) * to_log2).astype(bf16))))

        def turn(kt, state):
            found, vt = scores(kt)
            out = []
            for s, (top, total) in zip(found, state):
                new_top = jnp.maximum(top, jnp.max(s, axis=0, keepdims=True))
                p = jnp.exp2((s - new_top) * to_log2).astype(bf16)
                out.append((new_top, total * jnp.exp2((top - new_top) * to_log2) + dot(vt, p)))
            return tuple(out)

        state = lax.fori_loop(0, last, turn, tuple(state))
        for c, (top, total) in enumerate(state):
            weight = total[:1]
            o_ref[i, c] = total[ONES:] / weight
            log_ref[i, c] = top * to_log2 + jnp.log2(weight)


def backward_kernel(offsets, picks, place, rows, core_mask, first, *refs):
    me_ref, q_ref, g_ref, all_ref, log_ref, delta_ref = refs[:6]
    kv_ref, kvt_ref = refs[-2:]
    if first:
        dq_ref, dkv_ref = refs[6:8]
        dkv_ref[...] = jnp.zeros_like(dkv_ref)
    else:
        begun_ref, dq_ref, own_ref, other_ref, dkv_ref = refs[6:11]
        dkv_ref[...] = begun_ref[...]
    me, core, chip, own = me_ref[0], me_ref[1], me_ref[2], me_ref[3]
    chunks = q_ref.shape[1]
    fill_keys(place, rows, core, chip, own, all_ref, kvt_ref, kv_ref)
    for i, (pick, offset) in enumerate(zip(picks, offsets)):
        position = me ^ offset
        last = position // (KEY_TILE // rows)

        def turn(tile, keep):
            kv = kv_ref[rows_of(tile), :]
            kvt = kvt_ref[tile]
            pairs = [(dot(kv, q_ref[pick, c]), dot(kv, g_ref[pick, c])) for c in range(chunks)]
            summed, out = None, []
            for c, (s, dp) in enumerate(pairs):
                p = jnp.exp2(s * to_log2 - log_ref[i, c])
                if keep is not None:
                    p = jnp.where(keep, p, 0.0)
                ds = (p * (dp - delta_ref[pick, c])).astype(bf16)
                part = dot_last(p.astype(bf16), g_ref[pick, c]) + dot_last(ds, q_ref[pick, c])
                summed = part if summed is None else summed + part
                out.append(dot(kvt, ds)[:HD])
            dkv_ref[rows_of(tile), :] += summed
            return tuple(out)

        dq = turn(last, causal(position, rows, q_ref.shape[3]))
        dq = lax.fori_loop(
            0, last, lambda tile, dq: tuple(a + b for a, b in zip(dq, turn(tile, None))), dq
        )
        for c in range(chunks):
            dq_ref[i, c] = dq[c]
    if not first:
        for p, (at, core_bit, member) in enumerate(place):
            if core_bit == 0:
                near = (p + core * core_mask) * rows
                far = (p + (1 - core) * core_mask) * rows
                where = pl.ds(pl.multiple_of((member ^ own) * rows, rows), rows)
                own_ref[at ^ chip, where] = dkv_ref[pl.ds(pl.multiple_of(near, rows), rows), :]
                other = dkv_ref[pl.ds(pl.multiple_of(far, rows), rows), :]
                other_ref[at ^ chip, where] = other.astype(bf16)


def attention_forward(me, q, kv_all, offsets, picks, place, rows):
    blocks, chunks, columns = len(picks), q.shape[1], q.shape[3]
    keys = len(place) * rows
    scores = blocks * chunks * columns * keys // 2
    return call(
        functools.partial(forward_kernel, offsets, picks, place, rows),
        "attention_forward",
        [((blocks, chunks, HD, columns), f32), ((blocks, chunks, 1, columns), f32)],
        [me, q, kv_all],
        [SMEM_SPEC, VMEM_SPEC, VMEM_SPEC],
        scores * 8 * HD,
        [
            pltpu.VMEM((keys, 2 * HD), bf16),
            pltpu.VMEM((keys // KEY_TILE, 2 * HD, KEY_TILE), bf16),
            pltpu.VMEM((keys // KEY_TILE, ONES + HD, KEY_TILE), bf16),
        ],
        scores,
    )


def attention_backward(
    me, q, g, kv_all, log_total, delta, dkv, offsets, picks, place, rows, core_mask
):
    chunks, columns = q.shape[1], q.shape[3]
    keys = len(place) * rows
    scores = len(picks) * chunks * columns * keys // 2
    shares = (kv_all.shape[1], kv_all.shape[3], 2 * HD)
    out = [((len(picks), chunks, HD, columns), f32)]
    scratch = [
        pltpu.VMEM((keys, 2 * HD), bf16),
        pltpu.VMEM((keys // KEY_TILE, 2 * HD, KEY_TILE), bf16),
    ]
    args = [me, q, g, kv_all, log_total, delta]
    if dkv is None:
        out = out + [((keys, 2 * HD), f32)]
    else:
        out = out + [(shares, f32), (shares, bf16)]
        scratch = [pltpu.VMEM((keys, 2 * HD), f32)] + scratch
        args = args + [dkv]
    return call(
        functools.partial(backward_kernel, offsets, picks, place, rows, core_mask, dkv is None),
        "attention_backward",
        out,
        args,
        [SMEM_SPEC] + [VMEM_SPEC] * (len(args) - 1),
        scores * 20 * HD,
        scratch,
        scores,
    )


def on_device(
    tokens, gain_attn, w_query, w_key, w_value, w_out, gain_ffn, w_gate, w_up, w_down, out_grad
):
    n_seq = lax.axis_size("seq")
    n_fsdp = lax.axis_size("fsdp")
    n = n_seq * n_fsdp
    me = lax.axis_index(AXES)
    rows, width = tokens.shape
    slab, hidden_width = w_gate.shape
    x_mask, z_mask, core = 1, 2 * n_fsdp, n_fsdp
    t_masks = [0, x_mask, z_mask, x_mask | z_mask]
    far = [n_fsdp << k for k in range(2, n_seq.bit_length() - 1)]
    near = [1 << k for k in range(1, n_fsdp.bit_length() - 1)]
    d_bits = far + near + [core]
    d_masks = [0]
    for bit in d_bits:
        d_masks = d_masks + [m | bit for m in d_masks]
    chips = d_masks[: len(d_masks) // 2]
    d_all = sum(d_bits)
    t_groups = [[b | m for m in t_masks] for b in sorted(d_masks)]

    def swap(value, mask):
        return lax.ppermute(value, AXES, [(i, i ^ mask) for i in range(n)])

    def trade(value, groups):
        return lax.all_to_all(
            value, AXES, split_axis=0, concat_axis=0, tiled=True, axis_index_groups=groups
        )

    def sum_blocks(value, count):
        value = value.reshape((count, -1) + value.shape[1:])
        total = value[0].astype(f32)
        for i in range(1, count):
            total = total + value[i].astype(f32)
        return total

    def spread(pieces, bits):
        pieces = dict(pieces)
        for bit in bits:
            pieces.update({m | bit: swap(v, bit) for m, v in list(pieces.items())})
        return pieces

    def beyond(pieces):
        return {m: v for m, v in pieces.items() if m}

    def joined(own, relayed):
        pieces = {**own, **relayed}
        half = [pieces[m] for m in chips]
        return half + [swap(p, core) for p in half]

    def sum_over(total, bits, after=None):
        for bit in reversed(bits):
            half = total.shape[0] // 2
            got = swap(total[half:].astype(bf16), bit)
            if after is not None:
                got = hold(got, after)
            total = total[:half].astype(f32) + got.astype(f32)
        return total

    def core_sum(pair):
        own, other = pair
        return own.astype(f32) + swap(other, core).astype(f32)

    unit = 2 * slab
    aligned = unit == LANES
    zs = jnp.array([0, z_mask], jnp.int32)
    relative = ((me & d_all) ^ jnp.array(d_masks, jnp.int32))[:, None] + zs[None, :]
    relative = (relative.reshape(-1) // 2 * unit).astype(jnp.int32)
    t = me % 2 + 2 * ((me // z_mask) % 2)
    fixed = [(m | z) // 2 * unit for m in sorted(d_masks) for z in (0, z_mask)]
    fixed = jnp.array(fixed, jnp.int32)
    d_groups = [[b | m for m in sorted(d_masks)] for b in t_masks]
    side = (me % 2).reshape(1).astype(jnp.int32)

    def arranged(value, where):
        return value.reshape(value.shape[0], -1, unit)[:, where // unit].reshape(value.shape)

    def restored(value, where):
        runs = value.reshape(value.shape[0], -1, unit)
        return jnp.zeros_like(runs).at[:, where // unit].set(runs).reshape(value.shape)

    if aligned:
        starts, n_pieces = relative, len(d_masks)
    else:
        starts, n_pieces = jnp.arange(0, width, LANES, dtype=jnp.int32), width // (2 * LANES)

    def copies(value, count):
        shape = (count,) + value.shape
        return jnp.broadcast_to(value[None], shape).reshape((-1,) + value.shape[1:])

    def gather_t(value):
        return [value] + [swap(value, m) for m in t_masks[1:]]

    def relay_t(value):
        along = swap(value, z_mask)
        return [value, swap(value, x_mask), along, swap(along, x_mask)]

    def scatter_t(parts):
        return [parts[0]] + [swap(p, m) for p, m in zip(parts[1:], t_masks[1:])]

    def blocks_of(value):
        return [value[r * rows : (r + 1) * rows] for r in range(4)]

    def send(total, bits):
        total = sum_over(total, bits[1:])
        half = total.shape[0] // 2
        return total[:half].astype(f32), swap(total[half:].astype(bf16), bits[0])

    def give_back(total):
        return trade(total.reshape(4 * slab, -1).astype(bf16), t_groups)

    def by_member(value):
        size = value.shape[0] // 4
        parts = [lax.dynamic_slice_in_dim(value, (t ^ r) * size, size, 0) for r in range(4)]
        return jnp.concatenate(parts, axis=0)

    qkv_shard = trade(pack_attention(side, w_query, w_key, w_value, gain_attn, gain_ffn), t_groups)
    cols = hidden_width // 4
    qkv_far = spread({0: qkv_shard}, far)
    qkv_own = spread({0: qkv_shard}, near)
    near_tokens = hold(tokens, qkv_shard)
    toks = [tokens] + [swap(near_tokens, m) for m in t_masks[1:3]]
    toks = toks + [swap(hold(tokens, qkv_far, qkv_own), t_masks[3])]
    qkv_w = joined(qkv_own, spread(beyond(qkv_far), near))
    if aligned:
        qkv_k = qkv_w
    else:
        parts = jnp.stack(qkv_w).reshape(-1, 2, 2, slab + GAIN_ROWS, QKV_COLS)
        runs = parts[:, :, :, :slab].reshape(-1, unit, QKV_COLS)
        whole = jnp.zeros_like(runs).at[relative // unit].set(runs).reshape(-1, 4, 64, QKV_COLS)
        gains = jnp.stack(
            [parts[:, :, x, slab:, x * slab : (x + 1) * slab] for x in (0, 1)], axis=3
        ).reshape(-1, GAIN_ROWS, unit)
        gains = jnp.zeros_like(gains).at[relative // unit].set(gains)
        gains = jnp.moveaxis(gains, 1, 0).reshape(GAIN_ROWS, -1, 2, 64)
        gains = jnp.moveaxis(gains, 0, 2)
        lane = jnp.arange(QKV_COLS) // 64
        extra = jnp.where(
            lane[None, None, None] == jnp.arange(2)[None, :, None, None],
            jnp.tile(gains, (1, 1, 1, QKV_COLS // 64)),
            jnp.zeros((), bf16),
        ).reshape(-1, 4, GAIN_ROWS, QKV_COLS)
        whole = jnp.concatenate([whole, extra], axis=2).reshape(n_pieces, -1, QKV_COLS)
        qkv_k = [whole[i] for i in range(n_pieces)]

    bits = n.bit_length() - 1
    source = {z_mask.bit_length() - 1: bits - 1, 0: bits - 2}
    free = list(range(bits - 2))
    open_places = [b for b in range(bits) if b not in source]
    for b in list(open_places):
        if b in free:
            source[b] = b
            free.remove(b)
            open_places.remove(b)
    source.update(zip(open_places, free))

    def goes_to(i):
        return sum(((i >> s) & 1) << b for b, s in source.items())

    def came_from(i):
        return sum(((i >> b) & 1) << s for b, s in source.items())

    per_group = n // 4
    out_shard = lax.ppermute(hold(w_out, qkv_shard), AXES, [(i, goes_to(i)) for i in range(n)])
    my_row = came_from(me) % per_group
    out_places = jnp.array([came_from(m) % per_group for m in d_masks], jnp.int32)
    out_places = ((my_row ^ out_places) * slab).astype(jnp.int32)

    out_shard = hold(out_shard, qkv_far)
    out_far = spread({0: out_shard}, far)
    out_own = spread({0: out_shard}, near)
    qkv_k, toks, out_far, out_own = lax.optimization_barrier((qkv_k, toks, out_far, out_own))
    out_all = {**out_own, **spread(beyond(out_far), near)}
    blocks = me ^ jnp.array(t_masks, jnp.int32)
    positions = (blocks[:, None] * rows + jnp.arange(rows, dtype=jnp.int32)).reshape(-1)
    cosine, sine = rope_tables(positions)
    h_attn, q, kv, gains = project(starts, toks, cosine, sine, qkv_k)
    gain_a, gain_f = gains[0:1], gains[1:2]
    pair_shard = trade(hold(pack_columns([w_gate, w_up], "pack_gate_up"), kv), t_groups)
    kv_parts = [kv] + [swap(kv, m) for m in chips[1:]]
    kv_parts, pair_shard, out_all = lax.optimization_barrier((kv_parts, pair_shard, out_all))
    kv = jnp.stack(kv_parts)
    kv_all = jnp.stack([kv, swap(kv, core)])
    place = [
        (
            chips.index(p & sum(far + near)),
            1 if p & core else 0,
            t_masks.index(p & (x_mask | z_mask)),
        )
        for p in range(n)
    ]
    my_chip = sum(((me // bit) % 2) << i for i, bit in enumerate(far + near))
    me_ref = jnp.stack([me, (me // core) % 2, my_chip, t]).astype(jnp.int32)

    pair_w = lax.all_gather(pair_shard, AXES, axis=0, tiled=True, axis_index_groups=d_groups)
    out_half = jnp.concatenate([out_all[m] for m in chips], axis=0)
    out_pieces = [out_half, swap(hold(out_half, kv_all), core)]
    down_shard = trade(pack_columns([hold(w_down, kv_all)], "pack_down"), t_groups)
    g4 = arrange(relative, out_grad) if aligned else arranged(out_grad, relative)

    def forward(x, q):
        return attention_forward(
            me_ref, q, kv_all, [x * x_mask, z_mask + x * x_mask], [x, 2 + x], place, rows
        )

    def backward(x, dkv):
        return attention_backward(
            me_ref,
            q,
            d_heads,
            kv_all,
            log_totals[x],
            delta,
            dkv,
            [x * x_mask, z_mask + x * x_mask],
            [x, 2 + x],
            place,
            rows,
            core,
        )

    attn_a, log_a = forward(0, q)
    attn_a, q_b, out_pieces, down_shard = lax.optimization_barrier(
        (attn_a, q, out_pieces, down_shard)
    )
    down_own = spread({0: hold(down_shard, attn_a)}, near)
    g = trade(copies(hold(g4, attn_a), 4), t_groups)
    attn_b, log_b = forward(1, q_b)
    attn, log_totals = [attn_a, attn_b], [log_a, log_b]
    *middle_parts, attn_t, out_w = out_products(out_places, attn, out_pieces, rows)
    middle_parts = scatter_t(middle_parts)

    def halves(pieces):
        half = jnp.concatenate([pieces[m] for m in chips], axis=0)
        return [half, swap(half, core)]

    middle_parts, down_own, g = lax.optimization_barrier((middle_parts, down_own, g))
    down_far = spread({0: hold(down_shard, middle_parts)}, far)
    g = by_member(hold(g, middle_parts))

    if aligned:
        middle, h = middle_norm(fixed, tokens, gain_f, middle_parts)
    else:
        middle = tokens.astype(f32) + sum([p.astype(f32) for p in middle_parts])
        h = arranged((middle * inverse_rms(middle) * gain_f).astype(bf16), fixed)
    h_parts = gather_t(h)
    h_parts, g = lax.optimization_barrier((h_parts, g))
    down_all = {**down_own, **spread(hold(beyond(down_far), h_parts), near)}
    h_ffn = jnp.concatenate(h_parts, axis=0)
    half_width = width // 2

    def by_halves(left, w):
        return dot(left[:, :half_width], w[0]) + dot(left[:, half_width:], w[1])

    down_w = halves(down_all)
    pair = dot(h_ffn, pair_w)
    gate, up = pair[:, :cols], pair[:, cols:]
    sig = jax.nn.sigmoid(gate)
    act = gate * sig
    hidden = (act * up).astype(bf16)
    d_hidden = by_halves(g, down_w)
    d_gate = (d_hidden * up * sig * (1.0 + gate * (1.0 - sig))).astype(bf16)
    d_up = (d_hidden * act).astype(bf16)
    d_pair = jnp.concatenate([d_gate, d_up], axis=1)
    d_hffn_part = dot_last(d_pair, pair_w).astype(bf16)
    d_hffn_blocks = blocks_of(d_hffn_part)
    d_hffn_parts = scatter_t(d_hffn_blocks)

    def weight_grad(left, right):
        other = dot_first(left[:, half_width:], right).astype(bf16)
        return dot_first(left[:, :half_width], right) + swap(other, core).astype(f32)

    pair_grad = dot_first(hold(h_ffn, d_hffn_blocks), d_pair).astype(bf16)
    pair_total = lax.psum_scatter(
        pair_grad, AXES, scatter_dimension=0, tiled=True, axis_index_groups=d_groups
    )
    block_part = jnp.concatenate(
        [dot_last(hold(hidden, pair_grad), w).astype(bf16) for w in down_w], axis=1
    )
    d_hffn_parts, pair_grad, block_part = lax.optimization_barrier(
        (d_hffn_parts, pair_grad, block_part)
    )
    down_sum = weight_grad(hold(g, d_hffn_parts), hidden)
    block_blocks = by_member(hold(block_part, d_hffn_parts))

    if aligned:
        d_middle, d_low, gain_ffn_term = norm_back(fixed, middle, out_grad, gain_f, d_hffn_parts)
    else:
        d_hffn = restored(sum([p.astype(f32) for p in d_hffn_parts]), fixed)
        inverse = inverse_rms(middle)
        normed = middle * inverse
        scaled = d_hffn * gain_f
        gain_ffn_term = jnp.sum(d_hffn * normed, axis=0, keepdims=True)
        d_middle = out_grad.astype(f32) + inverse * (
            scaled - normed * jnp.mean(scaled * normed, axis=-1, keepdims=True)
        )
        d_low = d_middle.astype(bf16)
    d_branch = relay_t(d_low)
    d_branch, down_sum, block_blocks = lax.optimization_barrier((d_branch, down_sum, block_blocks))
    d_heads, delta = out_back(out_w, attn, d_branch)

    block_parts = trade(hold(block_blocks, d_heads), t_groups)
    down_near = hold(down_sum, d_heads)
    for bit in reversed(near):
        half = down_near.shape[0] // 2
        down_got = swap(down_near[half:].astype(bf16), bit)
        down_near = down_near[:half].astype(f32)
        if bit != near[0]:
            down_near = down_near + down_got.astype(f32)
    out_pair = out_grads(out_places, attn_t, hold(d_branch, d_heads), slab)
    out_sum = core_sum(out_pair)
    dq0, dkv = backward(0, None)
    dkv, out_sum = lax.optimization_barrier((dkv, out_sum))
    out_keep, out_got = send(out_sum, near)
    dq1, own, other = backward(1, dkv)
    other, down_got, block_parts, out_got = lax.optimization_barrier(
        (other, down_got, block_parts, out_got)
    )
    kv_sums = own + swap(other, core).astype(f32)
    kv_sends = [kv_sums[i].astype(bf16) for i in range(len(chips))]
    kv_parts = [swap(kv_sends[i], m) for i, m in enumerate(chips) if m]
    dq0, dq1, block_parts, down_got, out_got, pair_total = hold(
        (dq0, dq1, block_parts, down_got, out_got, pair_total), kv_sends
    )
    d_query = back_query(dq0, dq1, cosine, sine, rows)
    if aligned:
        query_pair = query_grads(starts, h_attn, d_query, n_pieces)
    else:
        grads = dot_first(h_attn, d_query).astype(bf16).reshape(-1, unit, Q_COLS)
        grads = grads[relative // unit].reshape(len(d_masks), -1, Q_COLS)
        query_pair = grads[: len(chips)], grads[len(chips) :]
    query_sum = core_sum(query_pair)
    down_keep, down_got = send(down_near + down_got.astype(f32), far)
    pair_parts = trade(pair_total, t_groups)
    if aligned:
        block_out = block_output(relative, middle, block_parts)
    else:
        block_out = (middle + restored(sum_blocks(block_parts, 4), relative)).astype(bf16)
    kv_parts, query_sum, block_out = lax.optimization_barrier((kv_parts, query_sum, block_out))
    kv_sum = kv_sums[0]
    for part in kv_parts:
        kv_sum = kv_sum + part.astype(f32)
    query_keep, query_got = send(query_sum, near)
    out_keep, out_got = send(out_keep + out_got.astype(f32), far)
    *d_hattn_blocks, d_kv, gain_attn_part = back_project(
        starts, d_query, kv_sum, cosine, sine, toks, qkv_k
    )
    d_hattn_blocks, query_got = lax.optimization_barrier((d_hattn_blocks, query_got))
    query_near = query_keep + query_got.astype(f32)
    d_hattn_parts = scatter_t(d_hattn_blocks)
    d_kv, gain_attn_part = hold((d_kv, gain_attn_part), d_hattn_blocks)
    if aligned:
        own, other = key_grads(starts, h_attn, d_kv, gain_attn_part, gain_ffn_term, n_pieces, slab)
    else:
        grads = dot_first(h_attn, d_kv).astype(bf16).reshape(-1, unit, 2 * HD)
        grads = grads[relative // unit].reshape(-1, 4, slab, 2 * HD)
        terms = jnp.concatenate([gain_attn_part, gain_ffn_term]).astype(bf16)
        terms = terms.reshape(2, -1, unit)[:, relative // unit].reshape(2, -1, 2, 1, unit)
        terms = jnp.moveaxis(jnp.broadcast_to(terms, terms.shape[:3] + (2, unit)), 0, 3)
        terms = terms.reshape(-1, 4, 2, unit)
        terms = jnp.pad(terms, ((0, 0), (0, 0), (0, GAIN_ROWS - 2), (0, 2 * HD - unit)))
        grads = jnp.concatenate([grads, terms], axis=2).reshape(len(d_masks), -1, 2 * HD)
        own, other = grads[: len(chips)], grads[len(chips) :]
    key_sum = core_sum((own, other))
    after = d_hattn_parts[1:]
    grad_gate, grad_up = unpack_columns(pair_parts, 2, "unpack_gate_up")
    key_sum, query_near, out_got, down_got = hold((key_sum, query_near, out_got, down_got), after)
    query_keep, query_got = send(query_near, far)
    d_hattn_parts, grad_gate, grad_up = lax.optimization_barrier((d_hattn_parts, grad_gate, grad_up))
    query_total = query_keep + query_got.astype(f32)
    out_total = (out_keep + out_got.astype(f32)).astype(bf16).reshape(slab, width)
    down_total = down_keep + down_got.astype(f32)
    key_total = sum_over(sum_over(key_sum, near), far)
    grad_out_proj = lax.ppermute(out_total, AXES, [(goes_to(i), i) for i in range(n)]).astype(f32)
    merged = [v.reshape(4 * slab, -1).astype(bf16) for v in (query_total, down_total)]
    merged = trade(jnp.concatenate(merged, axis=1), t_groups)
    grad_query, grad_down = unpack_two(merged, Q_COLS, "unpack_query_down")
    key_parts = trade(key_total.reshape(-1, 2 * HD).astype(bf16), t_groups)
    grad_key, grad_value, gain_terms = unpack_keys(side, key_parts)

    own = tokens.astype(f32)
    inverse_attn = inverse_rms(own)
    normed_attn = own * inverse_attn
    d_hattn = d_hattn_parts[0].astype(f32)
    for part in d_hattn_parts[1:]:
        d_hattn = d_hattn + part.astype(f32)
    scaled = d_hattn * gain_a
    grad_tokens = d_middle + inverse_attn * (
        scaled - normed_attn * jnp.mean(scaled * normed_attn, axis=-1, keepdims=True)
    )
    return (
        block_out,
        grad_tokens,
        gain_terms[0],
        grad_query,
        grad_key,
        grad_value,
        grad_out_proj,
        gain_terms[1],
        grad_gate,
        grad_up,
        grad_down,
    )


def solution(mesh):
    spec2 = P(AXES, None)
    spec1 = P(AXES)
    return jax.shard_map(
        on_device,
        mesh=mesh,
        in_specs=(
            spec2,
            spec1,
            spec2,
            spec2,
            spec2,
            spec2,
            spec1,
            spec2,
            spec2,
            spec2,
            spec2,
        ),
        out_specs=(
            spec2,
            spec2,
            spec1,
            spec2,
            spec2,
            spec2,
            spec2,
            spec1,
            spec2,
            spec2,
            spec2,
        ),
        check_vma=False,
    )
```
